32 devices in a mesh: dp: 4 (over z), ctx: 2 (over core), tp: 4 (over y, x).
Axes of the slice: x: 2, y: 2, z: 4, core: 2. Of those that a mesh axis runs over, the one named last changes fastest.
Arguments:
- block_in: bfloat16 [8192, 2048], P(('dp', 'ctx')), may hold values from -6 to 6
- query_proj: bfloat16 [2048, 2048], P('dp', 'tp'), may hold values from -0.125 to 0.125
- forget_proj: bfloat16 [2048, 2048], P('dp', 'tp'), may hold values from -0.0625 to 0.0625
- value_proj: bfloat16 [2048, 2048], P('dp', 'tp'), may hold values from -0.125 to 0.125
- outgate_proj: bfloat16 [2048, 2048], P('dp', 'tp'), may hold values from -0.125 to 0.125
- out_proj: bfloat16 [2048, 2048], P('tp', 'dp'), may hold values from -0.125 to 0.125
- ffn_gate: bfloat16 [2048, 5632], P('dp', 'tp'), may hold values from -0.125 to 0.125
- ffn_up: bfloat16 [2048, 5632], P('dp', 'tp'), may hold values from -0.125 to 0.125
- ffn_down: bfloat16 [5632, 2048], P('tp', 'dp'), may hold values from -0.078125 to 0.078125
- first_gain: float32 [2048], replicated, may hold values from 0.5 to 1.5
- second_gain: float32 [2048], replicated, may hold values from 0.5 to 1.5
- group_gain: float32 [2048], P('tp'), may hold values from 0.5 to 1.5
- forget_bias: float32 [2048], P('tp'), may hold values from 3 to 12
- bound_table: float32 [24, 2048], P(None, 'tp'), may hold values from -4 to 4
- layer_index: int32 [1], replicated, may hold values from 1 to 23
- second_start: int32 [4], P('dp'), may hold values from 1 to 2048, as said below
- cotangent: bfloat16 [8192, 2048], P(('dp', 'ctx')), may hold values from -6 to 6
Outputs:
- block_out: bfloat16 [8192, 2048], P(('dp', 'ctx'))
- input_grad: float32 [8192, 2048], P(('dp', 'ctx'))
- query_grad: float32 [2048, 2048], P('dp', 'tp')
- forget_grad: float32 [2048, 2048], P('dp', 'tp')
- value_grad: float32 [2048, 2048], P('dp', 'tp')
- outgate_grad: float32 [2048, 2048], P('dp', 'tp')
- out_proj_grad: float32 [2048, 2048], P('tp', 'dp')
- ffn_gate_grad: float32 [2048, 5632], P('dp', 'tp')
- ffn_up_grad: float32 [2048, 5632], P('dp', 'tp')
- ffn_down_grad: float32 [5632, 2048], P('tp', 'dp')
- first_gain_grad: float32 [2048], replicated
- second_gain_grad: float32 [2048], replicated
- group_gain_grad: float32 [2048], P('tp')
- forget_bias_grad: float32 [2048], P('tp')
- bound_table_grad: float32 [24, 2048], P(None, 'tp')
The draws below stay inside these ranges and needn't reach their ends.
Inputs may be any that keep to these rules, and one draw needn't show every extreme that they name: second_start[p] is 2048 where pack p is one whole sequence, and otherwise the position inside the pack where its second sequence begins; pack 0 is always one whole sequence and pack 1 always holds two. layer_index names a row of bound_table other than the first.
All inputs are finite; a program needn't handle non-finite values.
Results may differ from the reference program's by a relative error of at most 0.018.
Values may be sent and summed in bfloat16 or wider, within the bound.
No kernel may reach another device: no remote copies, remote signals or barrier semaphores. Data moves between devices by JAX's collectives and lax.ppermute only.
A program may use at most 384 MiB of HBM per device.

```python
import math
import jax
import jax.numpy as jnp
from jax import lax

D = 2048
HEADS = 16
HEAD = 128
FF = 5632
LAYERS = 24
BLOCK = 32
TOK_DEV = 1024
PACKS = 4
PACK_LEN = 2048
TOKENS = 8192


def draw_second_start(key, part):
    own_key = jax.random.fold_in(key, 11)
    first_key, second_key = jax.random.split(own_key)
    has_split = jax.random.randint(first_key, (PACKS,), 0, 3) == 0
    positions = jax.random.randint(second_key, (PACKS,), TOK_DEV // 16, PACK_LEN - TOK_DEV // 16)
    pack_ids = lax.iota(jnp.int32, PACKS)
    split_here = has_split & (pack_ids > 0) | (pack_ids == 1)
    return jnp.where(split_here, positions, PACK_LEN).astype(jnp.int32)


def block_levels(key, dims, shards, low, top_value):
    loudness = 1.0
    for axis_at, shards_of in shards:
        draws = jax.random.uniform(jax.random.fold_in(jax.random.fold_in(key, 6), axis_at), (shards_of,), jnp.float32, low / len(shards), top_value / len(shards))
        loudness = loudness * jnp.repeat(jnp.exp(draws), dims[axis_at] // shards_of).reshape((-1,) + (1,) * (len(dims) - 1 - axis_at))
    return loudness


def scatter_about(stream_key, dims, width, most, cuts=(), kind=jnp.bfloat16):
    values = width * jax.random.normal(stream_key, dims, jnp.float32)
    if cuts:
        values = values * block_levels(stream_key, dims, cuts, -0.22, 0.18)
    return jnp.clip(values, -most, most).astype(kind)


def setup_inputs(seed: int = 0) -> dict:
    splits = jax.random.split(jax.random.key(seed), 18)
    return {
        "block_in": scatter_about(splits[0], (TOKENS, D), 1.0, 6.0, ((0, 8),)),
        "query_proj": scatter_about(splits[1], (D, D), D ** -0.5, 0.125, ((0, 4), (1, 4))),
        "forget_proj": scatter_about(splits[2], (D, D), (4 * D) ** -0.5, 0.0625, ((0, 4), (1, 4))),
        "value_proj": scatter_about(splits[3], (D, D), D ** -0.5, 0.125, ((0, 4), (1, 4))),
        "outgate_proj": scatter_about(splits[4], (D, D), D ** -0.5, 0.125, ((0, 4), (1, 4))),
        "out_proj": scatter_about(splits[5], (D, D), D ** -0.5, 0.125, ((0, 4), (1, 4))),
        "ffn_gate": scatter_about(splits[6], (D, FF), D ** -0.5, 0.125, ((0, 4), (1, 4))),
        "ffn_up": scatter_about(splits[7], (D, FF), D ** -0.5, 0.125, ((0, 4), (1, 4))),
        "ffn_down": scatter_about(splits[8], (FF, D), FF ** -0.5, 0.078125, ((0, 4), (1, 4))),
        "first_gain": jnp.clip(1.0 + 0.1 * jax.random.normal(splits[9], (D,), jnp.float32), 0.5, 1.5),
        "second_gain": jnp.clip(1.0 + 0.1 * jax.random.normal(splits[10], (D,), jnp.float32), 0.5, 1.5),
        "group_gain": jnp.clip(1.0 + 0.1 * jax.random.normal(splits[11], (D,), jnp.float32), 0.5, 1.5),
        "forget_bias": jnp.clip(jnp.exp(math.log(12.0) - 1.3862944 * jax.random.uniform(splits[12], (D,), jnp.float32) ** block_levels(splits[12], (D,), ((0, 4),), -0.2, 0.2)), 3.0, 12.0),
        "bound_table": scatter_about(splits[13], (LAYERS, D), 1.0, 4.0, ((1, 4),), jnp.float32),
        "layer_index": jax.random.randint(splits[14], (1,), 1, LAYERS).astype(jnp.int32),
        "second_start": draw_second_start(jax.random.fold_in(splits[17], 71), 0),
        "cotangent": scatter_about(splits[16], (TOKENS, D), 1.0, 6.0, ((0, 8),)),
    }


HIGH = lax.Precision.HIGHEST
EPS_NORM = 1e-06
EPS_GROUP = 1e-05

@jax.custom_vjp
def low(v):
    return lax.optimization_barrier(v.astype(jnp.bfloat16)).astype(jnp.float32)

@jax.custom_vjp
def low_back(v):
    return v

def low_keep(v):
    return (low(v), None)

def low_pass(kept, grad):
    return (grad,)

def back_keep(v):
    return (v, None)

def back_low(kept, grad):
    return (low(grad),)
low.defvjp(low_keep, low_pass)
low_back.defvjp(back_keep, back_low)

def matmul(left_side, right_side):
    return jnp.dot(left_side, right_side, precision=HIGH)

def rms_norm(rows_in, gain_vec):
    return rows_in * lax.rsqrt(lax.optimization_barrier(jnp.mean(rows_in * rows_in, axis=-1, keepdims=True)) + EPS_NORM) * gain_vec

def head_norm(mixed, pre_gate, gain_vec, head_count):
    row_count = mixed.shape[0]
    grouped = mixed.reshape(row_count, head_count, -1)
    scaled = grouped * lax.rsqrt(lax.optimization_barrier(jnp.mean(grouped * grouped, axis=-1, keepdims=True)) + EPS_GROUP)
    return scaled.reshape(row_count, -1) * gain_vec * jax.nn.silu(pre_gate)

def lower_bound(bound_rows, which_layer):
    weights = jax.nn.softmax(bound_rows, axis=0)
    rising = jnp.cumsum(weights, axis=0) - weights[0:1]
    picked = (lax.broadcasted_iota(jnp.int32, (bound_rows.shape[0], 1), 0) == which_layer[0]).astype(bound_rows.dtype)
    return lax.optimization_barrier(jnp.sum(rising * picked, axis=0))

def gate_values(pre_query, pre_forget, bias_vec, bound_vec):
    shifted = pre_forget + bias_vec
    forget = bound_vec + (1.0 - bound_vec) * jax.nn.sigmoid(shifted)
    return (jax.nn.silu(pre_query), (1.0 - bound_vec) * jax.nn.sigmoid(-shifted), jnp.log(forget))

def chain_link(earlier, later):
    return (earlier[0] * later[0], later[0][..., None] * earlier[1] + later[1])

def block_parts(queries, key_rows, values, log_forget, doc_ids, prev_doc, block_len):
    length, head_count, feature = queries.shape
    block_count = length // block_len
    blocked = (block_count, block_len, head_count, feature)
    queries = queries.reshape(blocked)
    key_rows = key_rows.reshape(blocked)
    values = values.reshape(blocked)
    decays = jnp.cumsum(log_forget.reshape(blocked), axis=1)
    doc_ids = doc_ids.reshape(block_count, block_len)
    before = jnp.concatenate([jnp.reshape(prev_doc, (1,)).astype(jnp.int32), doc_ids[:-1, block_len - 1].astype(jnp.int32)])
    middle = decays[:, block_len // 2:block_len // 2 + 1]
    final_decay = decays[:, block_len - 1:]
    scores = jnp.einsum('nthc,nshc->nhts', queries * jnp.exp(decays - middle), key_rows * jnp.exp(middle - decays), precision=HIGH)
    causal = lax.broadcasted_iota(jnp.int32, (block_len, block_len), 0) >= lax.broadcasted_iota(jnp.int32, (block_len, block_len), 1)
    allowed = causal[None] & (doc_ids[:, :, None] == doc_ids[:, None, :])
    scores = jnp.where(allowed[:, None], scores, 0.0)
    inside = jnp.einsum('nhts,nshe->nthe', scores, values, precision=HIGH)
    in_tail = (doc_ids == doc_ids[:, block_len - 1:]).astype(decays.dtype)
    ending = key_rows * jnp.exp(final_decay - decays) * in_tail[:, :, None, None]
    states = jnp.einsum('nshc,nshe->nhce', ending, values, precision=HIGH)
    kept_flag = (doc_ids[:, block_len - 1] == before).astype(decays.dtype)
    carried = jnp.exp(final_decay[:, 0]) * kept_flag[:, None, None]
    entering = (doc_ids == before[:, None]).astype(decays.dtype)
    reached = queries * jnp.exp(decays) * entering[:, :, None, None]
    prefix_decay, prefix_state = lax.associative_scan(chain_link, (carried, states), axis=0)
    return (inside, reached, prefix_decay, prefix_state)

def finish(pieces, state_in):
    inside, reached, prefix_decay, prefix_state = pieces
    state_ends = prefix_decay[..., None] * state_in[None] + prefix_state
    state_starts = jnp.concatenate([state_in[None], state_ends[:-1]], axis=0)
    outside = jnp.einsum('nthc,nhce->nthe', reached, state_starts, precision=HIGH)
    summed = inside + outside
    block_count, block_len, head_count, feature = summed.shape
    return (summed.reshape(block_count * block_len, head_count, feature), state_ends[-1])

def pack_forward(rows_in, split_at, weights, bound_vec):
    query_mat, forget_mat, value_mat, outgate_mat, out_mat, gate_mat, up_mat, down_mat, first_vec, second_vec, group_vec, bias_vec = weights
    first_low = low(rms_norm(rows_in, first_vec))
    pre_query = low_back(matmul(first_low, query_mat))
    pre_forget = low_back(matmul(first_low, forget_mat))
    pre_value = low_back(matmul(first_low, value_mat))
    pre_outgate = low_back(matmul(first_low, outgate_mat))
    queries, key_rows, log_forget = gate_values(pre_query, pre_forget, bias_vec, bound_vec)
    doc_ids = (lax.iota(jnp.int32, PACK_LEN) >= split_at).astype(jnp.int32)

    def to_heads(flat):
        return flat.reshape(PACK_LEN, HEADS, HEAD)
    pieces = block_parts(to_heads(queries), to_heads(key_rows), to_heads(pre_value), to_heads(log_forget), doc_ids, jnp.zeros((), jnp.int32), BLOCK)
    mixed, _ = finish(pieces, jnp.zeros((HEADS, HEAD, HEAD), jnp.float32))
    gated = low(head_norm(mixed.reshape(PACK_LEN, D), pre_outgate, group_vec, HEADS))
    resid = rows_in + low_back(matmul(gated, out_mat))
    second_low = low(rms_norm(resid, second_vec))
    pre_gate = low_back(matmul(second_low, gate_mat))
    pre_up = low_back(matmul(second_low, up_mat))
    hidden_low = low(jax.nn.silu(pre_gate) * pre_up)
    return resid + low_back(matmul(hidden_low, down_mat))

def reference(block_in, query_proj, forget_proj, value_proj, outgate_proj, out_proj, ffn_gate, ffn_up, ffn_down, first_gain, second_gain, group_gain, forget_bias, bound_table, layer_index, second_start, cotangent):
    floats = [array_in.astype(jnp.float32) for array_in in (block_in, query_proj, forget_proj, value_proj, outgate_proj, out_proj, ffn_gate, ffn_up, ffn_down, first_gain, second_gain, group_gain, forget_bias, bound_table)]

    def forward(inputs, query_mat, forget_mat, value_mat, outgate_mat, out_mat, gate_mat, up_mat, down_mat, first_vec, second_vec, group_vec, bias_vec, table_rows):
        bound_vec = lower_bound(table_rows, layer_index)
        weights = (query_mat, forget_mat, value_mat, outgate_mat, out_mat, gate_mat, up_mat, down_mat, first_vec, second_vec, group_vec, bias_vec)
        stepper = jax.checkpoint(lambda rows_in, split_at: pack_forward(rows_in, split_at, weights, bound_vec))

        def scanner(carry, item_pair):
            return (carry, stepper(item_pair[0], item_pair[1]))
        _, outputs = lax.scan(scanner, jnp.zeros((), jnp.float32), (inputs.reshape(PACKS, PACK_LEN, D), second_start.astype(jnp.int32)))
        return outputs.reshape(TOKENS, D)
    result, pull = jax.vjp(forward, *floats)
    grads = pull(cotangent.astype(jnp.float32))
    return (result.astype(jnp.bfloat16), grads[0], grads[1], grads[2], grads[3], grads[4], grads[5], grads[6], grads[7], grads[8], grads[9], grads[10], grads[11], grads[12], grads[13])
```

```python
import functools

import jax
import jax.numpy as jnp
from jax import lax
from jax.experimental import pallas as pl
from jax.experimental.pallas import tpu as pltpu
from jax.sharding import PartitionSpec as P

HEAD = 128
SUB = 32
CHUNK = 128
EPS_NORM = 1e-06
EPS_GROUP = 1e-05
F32 = jnp.float32
BF16 = jnp.bfloat16


def dot_nn(a, b):
    return lax.dot_general(a, b, (((1,), (0,)), ((), ())), preferred_element_type=F32)


def dot_nt(a, b):
    return lax.dot_general(a, b, (((1,), (1,)), ((), ())), preferred_element_type=F32)


def dot_tn(a, b):
    return lax.dot_general(a, b, (((0,), (0,)), ((), ())), preferred_element_type=F32)


def sigmoid_pair(x):
    small = jnp.exp(-jnp.abs(x))
    inv = 1.0 / (1.0 + small)
    rest = small * inv
    up = x >= 0.0
    return jnp.where(up, inv, rest), jnp.where(up, rest, inv)


def tri_dot(tri, x):
    high = x.astype(BF16)
    low = (x - high.astype(F32)).astype(BF16)
    return dot_nn(tri, high) + dot_nn(tri, low)


def triangle(upper):
    rows = lax.broadcasted_iota(jnp.int32, (CHUNK, CHUNK), 0)
    cols = lax.broadcasted_iota(jnp.int32, (CHUNK, CHUNK), 1)
    keep = rows <= cols if upper else rows >= cols
    return jnp.where(keep, 1.0, 0.0).astype(BF16)


def chunk_masks(start, split):
    rows = lax.broadcasted_iota(jnp.int32, (CHUNK, CHUNK), 0)
    cols = lax.broadcasted_iota(jnp.int32, (CHUNK, CHUNK), 1)
    local = split - start
    causal = rows >= cols
    same = (rows >= local) == (cols >= local)
    token = lax.broadcasted_iota(jnp.int32, (CHUNK, HEAD), 0)
    before = start > split
    enter = jnp.where(jnp.logical_or(token < local, before), 1.0, 0.0)
    last = CHUNK - 1 >= local
    tail = jnp.where((token >= local) == last, 1.0, 0.0)
    kept = jnp.where(jnp.logical_or(jnp.logical_not(last), before), 1.0, 0.0)
    return causal & same, enter, tail, kept


def decays(log_forget, tri):
    b = tri_dot(tri, log_forget)
    return b


def key_rows(k, b, kd, k_end_sub, mids, ends):
    out = []
    count = CHUNK // SUB
    for i in range(count):
        parts = []
        for j in range(i):
            part = k_end_sub[j * SUB : (j + 1) * SUB]
            parts.append(part * jnp.exp(mids[i] - ends[j]))
        parts.append(kd[i * SUB : (i + 1) * SUB])
        if i < count - 1:
            parts.append(jnp.zeros(((count - 1 - i) * SUB, HEAD), F32))
        out.append(jnp.concatenate(parts, axis=0).astype(BF16))
    return out


def spread(rows_list):
    return jnp.concatenate([jnp.broadcast_to(r, (SUB, HEAD)) for r in rows_list], axis=0)


def chunk_common(q, k, log_forget, tri):
    count = CHUNK // SUB
    b = tri_dot(tri, log_forget)
    mids = [b[i * SUB + SUB // 2 : i * SUB + SUB // 2 + 1] for i in range(count)]
    ends = [b[(i + 1) * SUB - 1 : (i + 1) * SUB] for i in range(count)]
    mid = spread(mids)
    end = spread(ends)
    to_mid = jnp.exp(b - mid)
    from_mid = jnp.exp(mid - b)
    to_end = jnp.exp(end - b)
    whole = jnp.exp(b)
    final = ends[-1]
    to_final = jnp.exp(final - b)
    qd = (q * to_mid).astype(BF16)
    keys = key_rows(k, b, k * from_mid, k * to_end, mids, ends)
    return b, mids, ends, to_mid, from_mid, to_end, whole, final, to_final, qd, keys


def scores_of(qd, keys):
    count = CHUNK // SUB
    return jnp.concatenate(
        [dot_nt(qd[i * SUB : (i + 1) * SUB], keys[i]) for i in range(count)], axis=0
    )


def forward_kernel(
    heads, chunks, split_ref, pre_ref, bias_ref, bound_ref, gain_ref, gated_ref, mixed_ref, states_ref, state
):
    step = pl.program_id(0)
    width = heads * HEAD

    @pl.when(step == 0)
    def _():
        state[...] = jnp.zeros_like(state)

    split = split_ref[0]
    tri = triangle(False)
    for n in range(chunks):
        start = (step * chunks + n) * CHUNK
        allowed, enter, tail, kept = chunk_masks(start, split)
        rows = slice(n * CHUNK, (n + 1) * CHUNK)
        for h in range(heads):
            cols = slice(h * HEAD, (h + 1) * HEAD)

            def part(which):
                return pre_ref[rows, which * width + h * HEAD : which * width + (h + 1) * HEAD]

            pre_q = part(0)
            q = pre_q * sigmoid_pair(pre_q)[0]
            bound = bound_ref[:, cols]
            plus, minus = sigmoid_pair(part(1) + bias_ref[:, cols])
            k = (1.0 - bound) * minus
            log_forget = jnp.log(bound + (1.0 - bound) * plus)
            _, _, _, _, _, _, whole, final, to_final, qd, keys = chunk_common(q, k, log_forget, tri)
            v = part(2).astype(BF16)
            scores = jnp.where(allowed, scores_of(qd, keys), 0.0).astype(BF16)
            old = state[h]
            states_ref[n, h] = old
            mixed = dot_nn(scores, v) + dot_nt((q * whole * enter).astype(BF16), old.astype(BF16))
            ending = (k * to_final * tail).astype(BF16)
            state[h] = old * (jnp.exp(final) * kept) + dot_tn(v, ending)
            mixed_ref[rows, cols] = mixed
            scale = lax.rsqrt(jnp.mean(mixed * mixed, axis=-1, keepdims=True) + EPS_GROUP)
            pre_g = part(3)
            gate = pre_g * sigmoid_pair(pre_g)[0]
            gated_ref[rows, cols] = (mixed * scale * gain_ref[:, cols] * gate).astype(BF16)


def mixer_forward(pre, bias, bound, gain, split, chunks=2):
    tokens, wide = pre.shape
    width = wide // 4
    heads = width // HEAD
    block = chunks * CHUNK
    steps = tokens // block
    row = pl.BlockSpec((1, width), lambda i: (0, 0))
    return pl.pallas_call(
        functools.partial(forward_kernel, heads, chunks),
        grid=(steps,),
        in_specs=[
            pl.BlockSpec(memory_space=pltpu.SMEM),
            pl.BlockSpec((block, wide), lambda i: (i, 0)),
            row,
            row,
            row,
        ],
        out_specs=[
            pl.BlockSpec((block, width), lambda i: (i, 0)),
            pl.BlockSpec((block, width), lambda i: (i, 0)),
            pl.BlockSpec((chunks, heads, HEAD, HEAD), lambda i: (i, 0, 0, 0)),
        ],
        out_shape=[
            jax.ShapeDtypeStruct((tokens, width), BF16),
            jax.ShapeDtypeStruct((tokens, width), F32),
            jax.ShapeDtypeStruct((tokens // CHUNK, heads, HEAD, HEAD), F32),
        ],
        scratch_shapes=[pltpu.VMEM((heads, HEAD, HEAD), F32)],
        compiler_params=pltpu.CompilerParams(
            dimension_semantics=("arbitrary",), vmem_limit_bytes=32 << 20
        ),
        cost_estimate=pl.CostEstimate(
            flops=tokens * width * 2048, bytes_accessed=tokens * width * 30, transcendentals=tokens * width * 12
        ),
        name="mixer_forward",
    )(split, pre, bias[None], bound[None], gain[None])


def backward_kernel(
    heads,
    chunks,
    split_ref,
    pre_ref,
    mixed_ref,
    grad_ref,
    states_ref,
    bias_ref,
    bound_ref,
    gain_ref,
    out_ref,
    sums_ref,
    adjoint,
    later,
):
    step = pl.program_id(0)
    steps = pl.num_programs(0)
    width = heads * HEAD
    count = CHUNK // SUB

    @pl.when(step == 0)
    def _():
        adjoint[...] = jnp.zeros_like(adjoint)
        later[...] = jnp.zeros_like(later)
        sums_ref[...] = jnp.zeros_like(sums_ref)

    split = split_ref[0]
    tri = triangle(False)
    tri_up = triangle(True)
    for n in reversed(range(chunks)):
        start = ((steps - 1 - step) * chunks + n) * CHUNK
        allowed, enter, tail, kept = chunk_masks(start, split)
        rows = slice(n * CHUNK, (n + 1) * CHUNK)
        for h in range(heads):
            cols = slice(h * HEAD, (h + 1) * HEAD)

            def part(which):
                return pre_ref[rows, which * width + h * HEAD : which * width + (h + 1) * HEAD]

            def store(which, value):
                out_ref[rows, which * width + h * HEAD : which * width + (h + 1) * HEAD] = value.astype(BF16)

            pre_q = part(0)
            sig_q, sig_nq = sigmoid_pair(pre_q)
            q = pre_q * sig_q
            bound = bound_ref[:, cols]
            plus, minus = sigmoid_pair(part(1) + bias_ref[:, cols])
            k = (1.0 - bound) * minus
            forget = bound + (1.0 - bound) * plus
            _, mids, ends, to_mid, from_mid, to_end, whole, final, to_final, qd, keys = chunk_common(
                q, k, jnp.log(forget), tri
            )
            v = part(2).astype(BF16)

            mixed = mixed_ref[rows, cols]
            grad = grad_ref[rows, cols].astype(F32)
            gain = gain_ref[:, cols]
            scale = lax.rsqrt(jnp.mean(mixed * mixed, axis=-1, keepdims=True) + EPS_GROUP)
            pre_g = part(3)
            sig_g, sig_ng = sigmoid_pair(pre_g)
            gate = pre_g * sig_g
            unit = mixed * scale
            u = grad * gain * gate
            moment = jnp.mean(u * unit, axis=-1, keepdims=True)
            mixed_grad = scale * (u - unit * moment)
            gu = grad * unit
            gain_sum = jnp.sum(gu * gate, axis=0, keepdims=True)
            store(3, gu * gain * (sig_g * (1.0 + pre_g * sig_ng)))

            do = mixed_grad.astype(BF16)
            old = states_ref[n, h]
            lam = adjoint[h]
            old_low = old.astype(BF16)
            lam_low = lam.astype(BF16)
            scores = jnp.where(allowed, scores_of(qd, keys), 0.0).astype(BF16)
            pair = jnp.where(allowed, dot_nt(do, v), 0.0).astype(BF16)
            reach = whole * enter
            remain = to_final * tail
            ending = (k * remain).astype(BF16)
            store(2, dot_tn(scores, do) + dot_nt(ending, lam_low))

            q_rows = []
            k_rows = [None] * count
            for i in range(count):
                pair_i = pair[i * SUB : (i + 1) * SUB]
                q_rows.append(dot_nn(pair_i, keys[i]))
                back = dot_tn(pair_i, qd[i * SUB : (i + 1) * SUB])
                for j in range(i + 1):
                    piece = back[j * SUB : (j + 1) * SUB]
                    if j == i:
                        piece = piece * from_mid[j * SUB : (j + 1) * SUB]
                        k_rows[j] = (k_rows[j], piece)
                    else:
                        piece = piece * jnp.exp(mids[i] - ends[j])
                        first = k_rows[j]
                        k_rows[j] = piece if first is None else first + piece
                diagonal = k_rows[i][1]
                k_rows[i] = None
                if i == 0:
                    diagonals = []
                diagonals.append(diagonal)
            k_intra = []
            for j in range(count):
                piece = diagonals[j]
                if k_rows[j] is not None:
                    piece = piece + k_rows[j] * to_end[j * SUB : (j + 1) * SUB]
                k_intra.append(piece)
            dq = jnp.concatenate(q_rows, axis=0) * to_mid + dot_nn(do, old_low) * reach
            dk = jnp.concatenate(k_intra, axis=0) + dot_nn(v, lam_low) * remain
            anchor = jnp.sum(lam * later[h], axis=0, keepdims=True)
            dlog = tri_dot(tri_up, q * dq - k * dk) + anchor
            adjoint[h] = lam * (jnp.exp(final) * kept) + dot_tn(do, (q * reach).astype(BF16))
            later[h] = old

            store(0, dq * (sig_q * (1.0 + pre_q * sig_nq)))
            drive = minus * (dlog / forget - dk)
            forget_grad = (1.0 - bound) * plus * drive
            store(1, forget_grad)
            sums_ref[0:1, cols] += gain_sum
            sums_ref[1:2, cols] += jnp.sum(forget_grad, axis=0, keepdims=True)
            sums_ref[2:3, cols] += jnp.sum(drive, axis=0, keepdims=True)


def mixer_backward(pre, mixed, grad, states, bias, bound, gain, split, chunks=1):
    tokens, wide = pre.shape
    width = wide // 4
    heads = width // HEAD
    block = chunks * CHUNK
    steps = tokens // block
    row = pl.BlockSpec((1, width), lambda i: (0, 0))
    narrow = pl.BlockSpec((block, width), lambda i: (steps - 1 - i, 0))
    return pl.pallas_call(
        functools.partial(backward_kernel, heads, chunks),
        grid=(steps,),
        in_specs=[
            pl.BlockSpec(memory_space=pltpu.SMEM),
            pl.BlockSpec((block, wide), lambda i: (steps - 1 - i, 0)),
            narrow,
            narrow,
            pl.BlockSpec((chunks, heads, HEAD, HEAD), lambda i: (steps - 1 - i, 0, 0, 0)),
            row,
            row,
            row,
        ],
        out_specs=[
            pl.BlockSpec((block, wide), lambda i: (steps - 1 - i, 0)),
            pl.BlockSpec((8, width), lambda i: (0, 0)),
        ],
        out_shape=[
            jax.ShapeDtypeStruct((tokens, wide), BF16),
            jax.ShapeDtypeStruct((8, width), F32),
        ],
        scratch_shapes=[pltpu.VMEM((heads, HEAD, HEAD), F32), pltpu.VMEM((heads, HEAD, HEAD), F32)],
        compiler_params=pltpu.CompilerParams(
            dimension_semantics=("arbitrary",), vmem_limit_bytes=32 << 20
        ),
        cost_estimate=pl.CostEstimate(
            flops=tokens * width * 5120, bytes_accessed=tokens * width * 34, transcendentals=tokens * width * 14
        ),
        name="mixer_backward",
    )(split, pre, mixed, grad, states, bias[None], bound[None], gain[None])


def rms_rows(rows_in):
    return lax.rsqrt(jnp.mean(rows_in * rows_in, axis=-1, keepdims=True) + EPS_NORM)


def norm_back(grad, rows_in, gain_vec):
    inv = rms_rows(rows_in)
    u = grad * gain_vec
    moment = jnp.mean(u * rows_in, axis=-1, keepdims=True)
    return inv * u - rows_in * (inv * inv * inv * moment), jnp.sum(grad * rows_in * inv, axis=0)


def gather(part, axes, dim):
    return lax.all_gather(part, axes, axis=dim, tiled=True)


def scatter(whole, axes, dim):
    return lax.psum_scatter(whole, axes, scatter_dimension=dim, tiled=True)


def matmul(left_side, right_side):
    return jnp.dot(left_side, right_side, preferred_element_type=F32)


def body(
    block_in,
    query_proj,
    forget_proj,
    value_proj,
    outgate_proj,
    out_proj,
    ffn_gate,
    ffn_up,
    ffn_down,
    first_gain,
    second_gain,
    group_gain,
    forget_bias,
    bound_table,
    layer_index,
    second_start,
    cotangent,
):
    ctx_count, ctx_at = lax.axis_size("ctx"), lax.axis_index("ctx")
    tp_count, tp_at = lax.axis_size("tp"), lax.axis_index("tp")
    row_count = block_in.shape[0]
    local_width = query_proj.shape[1]
    width = local_width // ctx_count
    hidden_width = ffn_gate.shape[1]
    shard_rows = row_count // tp_count

    def own_half(array, dim):
        size = array.shape[dim] // ctx_count
        return lax.dynamic_slice_in_dim(array, ctx_at * size, size, dim)

    def own_rows(array):
        return lax.dynamic_slice_in_dim(array, tp_at * shard_rows, shard_rows, 0)

    mix_full = gather(
        jnp.concatenate(
            [own_half(w, 1) for w in (query_proj, forget_proj, value_proj, outgate_proj)], axis=1
        ),
        "dp",
        0,
    )
    out_full = gather(own_half(out_proj, 0), "dp", 1)
    down_full = gather(own_half(ffn_down, 1), ("dp", "ctx"), 1)
    ffn_full = gather(own_half(jnp.concatenate([ffn_gate, ffn_up], axis=1), 0), ("dp", "ctx"), 0)

    inputs = block_in.astype(F32)
    first_low = (inputs * rms_rows(inputs) * first_gain).astype(BF16)
    first_all = gather(first_low, "ctx", 0)
    table = own_half(bound_table, 1)
    weights = jax.nn.softmax(table, axis=0)
    rows = lax.broadcasted_iota(jnp.int32, (table.shape[0], 1), 0)
    counted = jnp.where((rows >= 1) & (rows <= layer_index[0]), 1.0, 0.0)
    bound = jnp.sum(weights * counted, axis=0)
    bias = own_half(forget_bias, 0)
    gain = own_half(group_gain, 0)
    pre = matmul(first_all, mix_full)
    gated, mixed, states = mixer_forward(pre, bias, bound, gain, second_start)
    out_part = matmul(gated, out_full).astype(BF16)
    resid = own_rows(block_in).astype(F32) + scatter(out_part, ("ctx", "tp"), 0).astype(F32)

    second_low = gather((resid * rms_rows(resid) * second_gain).astype(BF16), "tp", 0)
    gate_up = matmul(second_low, ffn_full)
    pre_gate = gate_up[:, :hidden_width]
    pre_up = gate_up[:, hidden_width:]
    sig = jax.nn.sigmoid(pre_gate)
    hidden = (pre_gate * sig * pre_up).astype(BF16)
    ffn_part = matmul(hidden, down_full).astype(BF16)
    block_out = gather((resid + scatter(ffn_part, "tp", 0).astype(F32)).astype(BF16), "tp", 0)

    hidden_grad = dot_nt(cotangent, down_full)
    gate_grad = hidden_grad * pre_up * sig * (1.0 + pre_gate * (1.0 - sig))
    up_grad = hidden_grad * (pre_gate * sig)
    gate_up_grad = jnp.concatenate([gate_grad.astype(BF16), up_grad.astype(BF16)], axis=1)
    second_part = dot_nt(gate_up_grad, ffn_full).astype(BF16)
    down_sum = scatter(dot_tn(hidden, cotangent).astype(BF16), ("dp", "ctx"), 1)
    ffn_sum = scatter(dot_tn(second_low, gate_up_grad).astype(BF16), ("dp", "ctx"), 0)
    second_total = scatter(second_part, "tp", 0).astype(F32)
    resid_part, second_gain_grad = norm_back(second_total, resid, second_gain)
    resid_grad = own_rows(cotangent).astype(F32) + resid_part
    resid_low = gather(resid_grad.astype(BF16), ("ctx", "tp"), 0)

    gated_grad = dot_nt(resid_low, out_full)
    out_sum = scatter(dot_tn(gated, resid_low).astype(BF16), "dp", 1)
    proj_grad, sums = mixer_backward(pre, mixed, gated_grad, states, bias, bound, gain, second_start)
    first_part = dot_nt(proj_grad, mix_full).astype(BF16)
    mix_sum = scatter(dot_tn(first_all, proj_grad).astype(BF16), "dp", 0)
    first_total = scatter(first_part, ("ctx", "tp"), 0).astype(F32)
    input_part, first_gain_grad = norm_back(first_total, own_rows(block_in).astype(F32), first_gain)
    input_grad = gather((resid_grad + input_part).astype(BF16), "tp", 0).astype(F32)

    head_sums = gather(jnp.sum(gather(sums[:3], "dp", 0).reshape(-1, 3, width), axis=0), "ctx", 1)
    gains = jnp.stack([first_gain_grad, second_gain_grad])
    gain_sums = jnp.sum(gather(gains[None], ("dp", "ctx", "tp"), 0), axis=0)
    all_weights = jax.nn.softmax(bound_table, axis=0)
    all_bound = jnp.sum(all_weights * counted, axis=0)
    table_grad = all_weights * (counted - all_bound) * head_sums[2]

    mix_both = gather(mix_sum[None], "ctx", 0)

    def columns(which):
        parts = [mix_both[c, :, which * width : (which + 1) * width] for c in range(ctx_count)]
        return jnp.concatenate(parts, axis=1).astype(F32)

    ffn_shard = gather(ffn_sum, "ctx", 0).astype(F32)
    return (
        block_out,
        input_grad,
        columns(0),
        columns(1),
        columns(2),
        columns(3),
        gather(out_sum, "ctx", 0).astype(F32),
        ffn_shard[:, :hidden_width],
        ffn_shard[:, hidden_width:],
        gather(down_sum, "ctx", 1).astype(F32),
        gain_sums[0],
        gain_sums[1],
        head_sums[0],
        head_sums[1],
        table_grad,
    )


def solution(mesh):
    return jax.shard_map(
        body,
        mesh=mesh,
        in_specs=(
            P(("dp", "ctx"), None),
            P("dp", "tp"),
            P("dp", "tp"),
            P("dp", "tp"),
            P("dp", "tp"),
            P("tp", "dp"),
            P("dp", "tp"),
            P("dp", "tp"),
            P("tp", "dp"),
            P(),
            P(),
            P("tp"),
            P("tp"),
            P(None, "tp"),
            P(),
            P("dp"),
            P(("dp", "ctx"), None),
        ),
        out_specs=(
            P(("dp", "ctx"), None),
            P(("dp", "ctx"), None),
            P("dp", "tp"),
            P("dp", "tp"),
            P("dp", "tp"),
            P("dp", "tp"),
            P("tp", "dp"),
            P("dp", "tp"),
            P("dp", "tp"),
            P("tp", "dp"),
            P(),
            P(),
            P("tp"),
            P("tp"),
            P(None, "tp"),
        ),
        check_vma=False,
    )
```

```python
import functools

import jax
import jax.numpy as jnp
from jax import lax
from jax.experimental import pallas as pl
from jax.experimental.pallas import tpu as pltpu
from jax.sharding import PartitionSpec as P

HEAD = 128
SUB = 32
CHUNK = 128
EPS_NORM = 1e-06
EPS_GROUP = 1e-05
F32 = jnp.float32
VMEM = 58 << 20
UNREAD = pl.BlockSpec(memory_space=pl.ANY)
BF16 = jnp.bfloat16


def cost(flops):
    return pl.CostEstimate(flops=2 * flops, bytes_accessed=1 << 20, transcendentals=0)


def dot_nn(a, b):
    return lax.dot_general(a, b, (((1,), (0,)), ((), ())), preferred_element_type=F32)


def dot_nt(a, b):
    return lax.dot_general(a, b, (((1,), (1,)), ((), ())), preferred_element_type=F32)


def dot_tn(a, b):
    return lax.dot_general(a, b, (((0,), (0,)), ((), ())), preferred_element_type=F32)


def sigmoid_pair(x):
    small = jnp.exp(-jnp.abs(x))
    inv = 1.0 / (1.0 + small)
    rest = small * inv
    up = x >= 0.0
    return jnp.where(up, inv, rest), jnp.where(up, rest, inv)


def tri_dot(tri, x):
    high = x.astype(BF16)
    low = (x - high.astype(F32)).astype(BF16)
    return dot_nn(tri, high) + dot_nn(tri, low)


def triangle(upper):
    rows = lax.broadcasted_iota(jnp.int32, (CHUNK, CHUNK), 0)
    cols = lax.broadcasted_iota(jnp.int32, (CHUNK, CHUNK), 1)
    keep = rows <= cols if upper else rows >= cols
    return jnp.where(keep, 1.0, 0.0).astype(BF16)


def chunk_masks(start, split):
    rows = lax.broadcasted_iota(jnp.int32, (CHUNK, CHUNK), 0)
    cols = lax.broadcasted_iota(jnp.int32, (CHUNK, CHUNK), 1)
    local = split - start
    causal = rows >= cols
    same = (rows >= local) == (cols >= local)
    token = lax.broadcasted_iota(jnp.int32, (CHUNK, HEAD), 0)
    before = start > split
    enter = jnp.where(jnp.logical_or(token < local, before), 1.0, 0.0)
    last = CHUNK - 1 >= local
    tail = jnp.where((token >= local) == last, 1.0, 0.0)
    kept = jnp.where(jnp.logical_or(jnp.logical_not(last), before), 1.0, 0.0)
    return causal & same, enter, tail, kept


def key_rows(k, b, kd, k_end_sub, mids, ends):
    out = []
    count = CHUNK // SUB
    for i in range(count):
        parts = []
        for j in range(i):
            part = k_end_sub[j * SUB : (j + 1) * SUB]
            parts.append(part * jnp.exp(mids[i] - ends[j]))
        parts.append(kd[i * SUB : (i + 1) * SUB])
        if i < count - 1:
            parts.append(jnp.zeros(((count - 1 - i) * SUB, HEAD), F32))
        out.append(jnp.concatenate(parts, axis=0).astype(BF16))
    return out


def spread(rows_list):
    return jnp.concatenate([jnp.broadcast_to(r, (SUB, HEAD)) for r in rows_list], axis=0)


def chunk_common(q, k, log_forget, tri):
    count = CHUNK // SUB
    b = tri_dot(tri, log_forget)
    mids = [b[i * SUB + SUB // 2 : i * SUB + SUB // 2 + 1] for i in range(count)]
    ends = [b[(i + 1) * SUB - 1 : (i + 1) * SUB] for i in range(count)]
    mid = spread(mids)
    end = spread(ends)
    to_mid = jnp.exp(b - mid)
    from_mid = jnp.exp(mid - b)
    to_end = jnp.exp(end - b)
    whole = jnp.exp(b)
    final = ends[-1]
    to_final = jnp.exp(final - b)
    qd = (q * to_mid).astype(BF16)
    keys = key_rows(k, b, k * from_mid, k * to_end, mids, ends)
    return b, mids, ends, to_mid, from_mid, to_end, whole, final, to_final, qd, keys


def scores_of(qd, keys):
    count = CHUNK // SUB
    return jnp.concatenate(
        [dot_nt(qd[i * SUB : (i + 1) * SUB], keys[i]) for i in range(count)], axis=0
    )


def forward_kernel(
    heads,
    chunks,
    order_ref,
    split_ref,
    pre_ref,
    bias_ref,
    bound_ref,
    gain_ref,
    gated_ref,
    mixed_ref,
    states_ref,
    state,
):
    step = pl.program_id(0)
    width = heads * HEAD

    @pl.when(step == 0)
    def _():
        state[...] = jnp.zeros_like(state)

    split = split_ref[0]
    tri = triangle(False)
    for n in range(chunks):
        start = (step * chunks + n) * CHUNK
        allowed, enter, tail, kept = chunk_masks(start, split)
        rows = slice(n * CHUNK, (n + 1) * CHUNK)
        for h in range(heads):
            cols = slice(h * HEAD, (h + 1) * HEAD)

            def part(which):
                return pre_ref[rows, which * width + h * HEAD : which * width + (h + 1) * HEAD]

            pre_q = part(0)
            q = pre_q * sigmoid_pair(pre_q)[0]
            bound = bound_ref[:, cols]
            plus, minus = sigmoid_pair(part(1) + bias_ref[:, cols])
            k = (1.0 - bound) * minus
            log_forget = jnp.log(bound + (1.0 - bound) * plus)
            _, _, _, _, _, _, whole, final, to_final, qd, keys = chunk_common(q, k, log_forget, tri)
            v = part(2).astype(BF16)
            scores = jnp.where(allowed, scores_of(qd, keys), 0.0).astype(BF16)
            old = state[h]
            states_ref[n, h] = old
            mixed = dot_nn(scores, v) + dot_nt((q * whole * enter).astype(BF16), old.astype(BF16))
            ending = (k * to_final * tail).astype(BF16)
            state[h] = old * (jnp.exp(final) * kept) + dot_tn(v, ending)
            mixed_ref[rows, cols] = mixed
            scale = lax.rsqrt(jnp.mean(mixed * mixed, axis=-1, keepdims=True) + EPS_GROUP)
            pre_g = part(3)
            gate = pre_g * sigmoid_pair(pre_g)[0]
            gated_ref[rows, cols] = (mixed * scale * gain_ref[:, cols] * gate).astype(BF16)


def mixer_forward(pre, bias, bound, gain, split, order):
    tokens, wide = pre.shape
    width = wide // 4
    heads = width // HEAD
    steps = order.shape[0]
    block = tokens // steps
    chunks = block // CHUNK
    row = pl.BlockSpec((1, width), lambda i, order: (0, 0))
    grid_spec = pltpu.PrefetchScalarGridSpec(
        num_scalar_prefetch=1,
        grid=(steps,),
        in_specs=[
            pl.BlockSpec(memory_space=pltpu.SMEM),
            pl.BlockSpec((block, wide), lambda i, order: (order[i], 0)),
            row,
            row,
            row,
        ],
        out_specs=[
            pl.BlockSpec((block, width), lambda i, order: (order[i], 0)),
            pl.BlockSpec((block, width), lambda i, order: (i, 0)),
            pl.BlockSpec((chunks, heads, HEAD, HEAD), lambda i, order: (i, 0, 0, 0)),
        ],
        scratch_shapes=[pltpu.VMEM((heads, HEAD, HEAD), F32)],
    )
    return pl.pallas_call(
        functools.partial(forward_kernel, heads, chunks),
        grid_spec=grid_spec,
        out_shape=[
            jax.ShapeDtypeStruct((tokens, width), BF16),
            jax.ShapeDtypeStruct((tokens, width), F32),
            jax.ShapeDtypeStruct((tokens // CHUNK, heads, HEAD, HEAD), F32),
        ],
        compiler_params=pltpu.CompilerParams(
            dimension_semantics=("arbitrary",), vmem_limit_bytes=VMEM
        ),
        cost_estimate=cost(tokens * width * 14000),
        name="mixer_forward",
    )(order, split, pre, bias[None], bound[None], gain[None])


def backward_kernel(
    heads,
    chunks,
    order_ref,
    split_ref,
    pre_ref,
    mixed_ref,
    grad_ref,
    states_ref,
    bias_ref,
    bound_ref,
    gain_ref,
    out_ref,
    sums_ref,
    adjoint,
    later,
):
    step = pl.program_id(0)
    steps = pl.num_programs(0)
    width = heads * HEAD
    count = CHUNK // SUB

    @pl.when(step == 0)
    def _():
        adjoint[...] = jnp.zeros_like(adjoint)
        later[...] = jnp.zeros_like(later)
        sums_ref[...] = jnp.zeros_like(sums_ref)

    split = split_ref[0]
    tri = triangle(False)
    tri_up = triangle(True)
    for n in reversed(range(chunks)):
        start = ((steps - 1 - step) * chunks + n) * CHUNK
        allowed, enter, tail, kept = chunk_masks(start, split)
        rows = slice(n * CHUNK, (n + 1) * CHUNK)
        for h in range(heads):
            cols = slice(h * HEAD, (h + 1) * HEAD)

            def part(which):
                return pre_ref[rows, which * width + h * HEAD : which * width + (h + 1) * HEAD]

            def store(which, value):
                out_ref[rows, which * width + h * HEAD : which * width + (h + 1) * HEAD] = value.astype(BF16)

            pre_q = part(0)
            sig_q, sig_nq = sigmoid_pair(pre_q)
            q = pre_q * sig_q
            bound = bound_ref[:, cols]
            plus, minus = sigmoid_pair(part(1) + bias_ref[:, cols])
            k = (1.0 - bound) * minus
            forget = bound + (1.0 - bound) * plus
            _, mids, ends, to_mid, from_mid, to_end, whole, final, to_final, qd, keys = chunk_common(
                q, k, jnp.log(forget), tri
            )
            v = part(2).astype(BF16)

            mixed = mixed_ref[rows, cols]
            grad = grad_ref[rows, cols].astype(F32)
            gain = gain_ref[:, cols]
            scale = lax.rsqrt(jnp.mean(mixed * mixed, axis=-1, keepdims=True) + EPS_GROUP)
            pre_g = part(3)
            sig_g, sig_ng = sigmoid_pair(pre_g)
            gate = pre_g * sig_g
            unit = mixed * scale
            u = grad * gain * gate
            moment = jnp.mean(u * unit, axis=-1, keepdims=True)
            mixed_grad = scale * (u - unit * moment)
            gu = grad * unit
            gain_sum = jnp.sum(gu * gate, axis=0, keepdims=True)
            store(3, gu * gain * (sig_g * (1.0 + pre_g * sig_ng)))

            do = mixed_grad.astype(BF16)
            old = states_ref[n, h]
            lam = adjoint[h]
            old_low = old.astype(BF16)
            lam_low = lam.astype(BF16)
            scores = jnp.where(allowed, scores_of(qd, keys), 0.0).astype(BF16)
            pair = jnp.where(allowed, dot_nt(do, v), 0.0).astype(BF16)
            reach = whole * enter
            remain = to_final * tail
            ending = (k * remain).astype(BF16)
            store(2, dot_tn(scores, do) + dot_nt(ending, lam_low))

            q_rows = []
            k_rows = [None] * count
            for i in range(count):
                pair_i = pair[i * SUB : (i + 1) * SUB]
                q_rows.append(dot_nn(pair_i, keys[i]))
                back = dot_tn(pair_i, qd[i * SUB : (i + 1) * SUB])
                for j in range(i + 1):
                    piece = back[j * SUB : (j + 1) * SUB]
                    if j == i:
                        piece = piece * from_mid[j * SUB : (j + 1) * SUB]
                        k_rows[j] = (k_rows[j], piece)
                    else:
                        piece = piece * jnp.exp(mids[i] - ends[j])
                        first = k_rows[j]
                        k_rows[j] = piece if first is None else first + piece
                diagonal = k_rows[i][1]
                k_rows[i] = None
                if i == 0:
                    diagonals = []
                diagonals.append(diagonal)
            k_intra = []
            for j in range(count):
                piece = diagonals[j]
                if k_rows[j] is not None:
                    piece = piece + k_rows[j] * to_end[j * SUB : (j + 1) * SUB]
                k_intra.append(piece)
            dq = jnp.concatenate(q_rows, axis=0) * to_mid + dot_nn(do, old_low) * reach
            dk = jnp.concatenate(k_intra, axis=0) + dot_nn(v, lam_low) * remain
            anchor = jnp.sum(lam * later[h], axis=0, keepdims=True)
            dlog = tri_dot(tri_up, q * dq - k * dk) + anchor
            adjoint[h] = lam * (jnp.exp(final) * kept) + dot_tn(do, (q * reach).astype(BF16))
            later[h] = old

            store(0, dq * (sig_q * (1.0 + pre_q * sig_nq)))
            drive = minus * (dlog / forget - dk)
            forget_grad = (1.0 - bound) * plus * drive
            store(1, forget_grad)
            sums_ref[0:1, cols] += gain_sum
            sums_ref[1:2, cols] += jnp.sum(forget_grad, axis=0, keepdims=True)
            sums_ref[2:3, cols] += jnp.sum(drive, axis=0, keepdims=True)


def mixer_backward(pre, mixed, grad, states, bias, bound, gain, split, order):
    tokens, wide = pre.shape
    width = wide // 4
    heads = width // HEAD
    steps = order.shape[0]
    block = tokens // steps
    chunks = block // CHUNK
    row = pl.BlockSpec((1, width), lambda i, order: (0, 0))
    placed = lambda i, order: (order[steps - 1 - i], 0)
    grid_spec = pltpu.PrefetchScalarGridSpec(
        num_scalar_prefetch=1,
        grid=(steps,),
        in_specs=[
            pl.BlockSpec(memory_space=pltpu.SMEM),
            pl.BlockSpec((block, wide), placed),
            pl.BlockSpec((block, width), lambda i, order: (steps - 1 - i, 0)),
            pl.BlockSpec((block, width), placed),
            pl.BlockSpec((chunks, heads, HEAD, HEAD), lambda i, order: (steps - 1 - i, 0, 0, 0)),
            row,
            row,
            row,
        ],
        out_specs=[
            pl.BlockSpec((block, wide), placed),
            pl.BlockSpec((8, width), lambda i, order: (0, 0)),
        ],
        scratch_shapes=[pltpu.VMEM((heads, HEAD, HEAD), F32), pltpu.VMEM((heads, HEAD, HEAD), F32)],
    )
    return pl.pallas_call(
        functools.partial(backward_kernel, heads, chunks),
        grid_spec=grid_spec,
        out_shape=[
            jax.ShapeDtypeStruct((tokens, wide), BF16),
            jax.ShapeDtypeStruct((8, width), F32),
        ],
        compiler_params=pltpu.CompilerParams(
            dimension_semantics=("arbitrary",), vmem_limit_bytes=VMEM
        ),
        cost_estimate=cost(tokens * width * 22000),
        name="mixer_backward",
    )(order, split, pre, mixed, grad, states, bias[None], bound[None], gain[None])


def product_kernel(dims, a_ref, b_ref, *refs):
    out_ref = refs[-1]
    dot = lax.dot_general(a_ref[...], b_ref[...], (dims, ((), ())), preferred_element_type=F32)
    out_ref[...] = dot.astype(out_ref.dtype)


def product_add_kernel(dims, a_ref, b_ref, add_ref, *refs):
    out_ref = refs[-1]
    dot = lax.dot_general(a_ref[...], b_ref[...], (dims, ((), ())), preferred_element_type=F32)
    out_ref[...] = (dot + add_ref[...].astype(F32)).astype(out_ref.dtype)


NN = ((1,), (0,))
NT = ((1,), (1,))
TN = ((0,), (0,))


def product(a, b, dims, kind, rows=None, cols=None, a_half=None, add=None, wait=()):
    count = a.shape[1 - dims[0][0]] if a_half is None else a.shape[0] // 2
    depth = a.shape[dims[0][0]]
    wide = b.shape[1 - dims[1][0]]
    tile_rows = rows or count
    tile_cols = cols or wide
    by_rows = rows is not None
    shift = (a_half or 0) * (count // tile_rows)

    def at_row(i):
        return (i if by_rows else 0) + shift

    def at_col(i):
        return 0 if by_rows else i

    if dims[0][0] == 1:
        a_spec = pl.BlockSpec((tile_rows, depth), lambda i: (at_row(i), 0))
    else:
        a_spec = pl.BlockSpec((depth, tile_rows), lambda i: (0, at_row(i)))
    if dims[1][0] == 0:
        b_spec = pl.BlockSpec((depth, tile_cols), lambda i: (0, at_col(i)))
    else:
        b_spec = pl.BlockSpec((tile_cols, depth), lambda i: (at_col(i), 0))
    out_spec = pl.BlockSpec((tile_rows, tile_cols), lambda i: (at_row(i) - shift, at_col(i)))
    kernel = product_kernel if add is None else product_add_kernel
    return pl.pallas_call(
        functools.partial(kernel, dims),
        grid=(count // tile_rows * (wide // tile_cols),),
        in_specs=[a_spec, b_spec] + ([] if add is None else [out_spec]) + [UNREAD] * len(wait),
        out_specs=out_spec,
        out_shape=jax.ShapeDtypeStruct((count, wide), kind),
        compiler_params=pltpu.CompilerParams(
            dimension_semantics=("arbitrary",), vmem_limit_bytes=VMEM
        ),
        cost_estimate=cost(2 * count * wide * depth),
        name="product",
    )(a, b, *([] if add is None else [add]), *wait)


def weight_sum_kernel(own_ref, other_ref, b_ref, weight_ref, right_ref, *refs):
    out_ref, sum_ref = refs[-2:]
    half = own_ref.shape[0]
    wide = b_ref.shape[1]
    dot = dot_tn(own_ref[...], b_ref[:half]) + dot_tn(other_ref[...], b_ref[half:])
    out_ref[:, :wide] = dot.astype(out_ref.dtype)
    total = jnp.sum(dot * weight_ref[...].astype(F32), axis=1, keepdims=True)
    sum_ref[...] = jnp.broadcast_to(total, sum_ref.shape)
    start = 0
    more = None
    for ref in refs[:-2]:
        size = ref.shape[0]
        if start < right_ref.shape[0]:
            term = dot_tn(ref[...], right_ref[start : start + size])
            more = term if more is None else more + term
            start += size
    out_ref[:, wide:] = more.astype(out_ref.dtype)


def weight_sum_product(own, other, b, weight, blocks, right, rows=256, wait=()):
    half, count = own.shape
    depth, wide = b.shape
    extra = right.shape[1]
    a_spec = pl.BlockSpec((half, rows), lambda i: (0, i))
    out, total = pl.pallas_call(
        weight_sum_kernel,
        grid=(count // rows,),
        in_specs=[
            a_spec,
            a_spec,
            pl.BlockSpec((depth, wide), lambda i: (0, 0)),
            pl.BlockSpec((rows, wide), lambda i: (i, 0)),
            pl.BlockSpec((depth, extra), lambda i: (0, 0)),
        ]
        + [pl.BlockSpec((block.shape[0], rows), lambda i: (0, i)) for block in blocks]
        + [UNREAD] * len(wait),
        out_specs=[
            pl.BlockSpec((rows, wide + extra), lambda i: (i, 0)),
            pl.BlockSpec((rows, HEAD), lambda i: (i, 0)),
        ],
        out_shape=[
            jax.ShapeDtypeStruct((count, wide + extra), BF16),
            jax.ShapeDtypeStruct((count, HEAD), F32),
        ],
        compiler_params=pltpu.CompilerParams(
            dimension_semantics=("arbitrary",), vmem_limit_bytes=VMEM
        ),
        cost_estimate=cost(2 * count * (wide + extra) * depth),
        name="weight_sum_product",
    )(own, other, b, weight, right, *blocks, *wait)
    return out, total[:, 0]


def blocks_product_kernel(b_ref, *refs):
    out_ref = refs[-1]
    start = 0
    for ref in refs[:-1]:
        size = ref.shape[0]
        out_ref[start : start + size] = dot_nt(ref[...], b_ref[...])
        start += size


def blocks_product(blocks, b):
    count = sum(block.shape[0] for block in blocks)
    return pl.pallas_call(
        blocks_product_kernel,
        out_shape=jax.ShapeDtypeStruct((count, b.shape[0]), F32),
        compiler_params=pltpu.CompilerParams(vmem_limit_bytes=VMEM),
        cost_estimate=cost(2 * count * b.size),
        name="blocks_product",
    )(b, *blocks)


def rms_rows(rows_in):
    return lax.rsqrt(jnp.mean(rows_in * rows_in, axis=-1, keepdims=True) + EPS_NORM)


def norm_back(grad, rows_in, gain_vec):
    inv = rms_rows(rows_in)
    u = grad * gain_vec
    moment = jnp.mean(u * rows_in, axis=-1, keepdims=True)
    return inv * u - rows_in * (inv * inv * inv * moment), jnp.sum(grad * rows_in * inv, axis=0)


def gather(part, axes, dim):
    return lax.all_gather(part, axes, axis=dim, tiled=True)


def scatter(whole, axes, dim):
    return lax.psum_scatter(whole, axes, scatter_dimension=dim, tiled=True)


def matmul(left_side, right_side):
    return jnp.dot(left_side, right_side, preferred_element_type=F32)


def after(value, *others):
    return lax.optimization_barrier((value, *others))[0]


def small_sum(part, axis):
    count = lax.axis_size(axis)
    if count <= 4:
        got = [lax.ppermute(part, axis, [(i, i ^ m) for i in range(count)]) for m in range(1, count)]
        return sum(got, part)
    mask = 1
    while mask < count:
        part = part + lax.ppermute(part, axis, [(i, i ^ mask) for i in range(count)])
        mask *= 2
    return part


def together(*values):
    return lax.optimization_barrier(values)


def swap(part):
    return lax.ppermute(part, "ctx", [(0, 1), (1, 0)])


def in_order(own, dim):
    other = swap(own)
    first = lax.axis_index("ctx") == 0
    return jnp.concatenate([jnp.where(first, own, other), jnp.where(first, other, own)], axis=dim)


def partner(part, mask):
    return lax.ppermute(part, "tp", [(i, i ^ mask) for i in range(lax.axis_size("tp"))])


def blocks_of(array, count):
    size = array.shape[0] // count
    return [array[m * size : (m + 1) * size] for m in range(count)]


def relative(array, count, at):
    size = array.shape[0] // count
    return jnp.concatenate(
        [lax.dynamic_slice_in_dim(array, (at ^ m) * size, size, 0) for m in range(count)], axis=0
    )


def piece(part, block, which):
    half = part.shape[0] // 8
    start = (2 * block + which) * half
    return part[start : start + half]


def sum_first(part):
    near = partner(jnp.concatenate([piece(part, 1, 0), piece(part, 3, 0)], axis=0), 1)
    far = partner(jnp.concatenate([piece(part, 2, 1), piece(part, 3, 1)], axis=0), 2)
    return near, far


def sum_second(part, near, far):
    half = near.shape[0] // 2
    near, far = together(near, far)
    pass_far = (piece(part, 2, 0).astype(F32) + near[half:].astype(F32)).astype(BF16)
    pass_near = (piece(part, 1, 1).astype(F32) + far[half:].astype(F32)).astype(BF16)
    pass_far, pass_near = together(pass_far, pass_near)
    return together(partner(pass_far, 2), partner(pass_near, 1))


def sum_total(part, first, second):
    half = second[0].shape[0]
    halves = [
        piece(part, 0, which).astype(F32) + first[which][:half].astype(F32) + second[which].astype(F32)
        for which in (0, 1)
    ]
    return jnp.concatenate(halves, axis=0)


def gather_first(own):
    return partner(own, 1), partner(own, 2)


def gather_second(near, far):
    half = near.shape[0] // 2
    far_half, near_half = together(far[:half], near[half:])
    return partner(far_half, 1), partner(near_half, 2)


def gather_blocks(own, first, second):
    return [own, *first, jnp.concatenate(second, axis=0)]


def placed_blocks(own, first, second, kind):
    count, at = lax.axis_size("tp"), lax.axis_index("tp")
    size, width = own.shape
    out = jnp.zeros((count * size, width), kind)
    starts = [at * size, (at ^ 1) * size, (at ^ 2) * size, (at ^ 3) * size, (at ^ 3) * size + size // 2]
    for block, start in zip([own, *first, *second], starts):
        out = lax.dynamic_update_slice_in_dim(out, block.astype(kind), start, 0)
    return out


def body(
    block_in,
    query_proj,
    forget_proj,
    value_proj,
    outgate_proj,
    out_proj,
    ffn_gate,
    ffn_up,
    ffn_down,
    first_gain,
    second_gain,
    group_gain,
    forget_bias,
    bound_table,
    layer_index,
    second_start,
    cotangent,
):
    ctx_count, ctx_at = lax.axis_size("ctx"), lax.axis_index("ctx")
    tp_count, tp_at = lax.axis_size("tp"), lax.axis_index("tp")
    row_count, model = block_in.shape
    local_width = query_proj.shape[1]
    width = local_width // ctx_count
    hidden_width = ffn_gate.shape[1]
    shard_rows = row_count // tp_count

    def own_half(array, dim):
        size = array.shape[dim] // ctx_count
        return lax.dynamic_slice_in_dim(array, ctx_at * size, size, dim)

    def sum_over_chip(rows_in, right_side, dot):
        other = swap(dot(rows_in[row_count:], right_side).astype(BF16))
        own = dot(rows_in[:row_count], right_side)
        return (own + other.astype(F32)).astype(BF16)

    blocks = ctx_count * tp_count
    order = lax.iota(jnp.int32, blocks) ^ (ctx_at * tp_count + tp_at)

    mix_full = gather(
        jnp.concatenate(
            [own_half(w, 1) for w in (query_proj, forget_proj, value_proj, outgate_proj)], axis=1
        ),
        "dp",
        0,
    )
    out_full = gather(own_half(out_proj, 0), "dp", 1)
    ffn_full = gather(own_half(jnp.concatenate([ffn_gate, ffn_up], axis=1), 0), ("dp", "ctx"), 0)
    down_full = gather(own_half(ffn_down, 1), ("dp", "ctx"), 1)

    inputs = relative(block_in, tp_count, tp_at).astype(F32)
    first_low = (inputs * rms_rows(inputs) * first_gain).astype(BF16)
    first_swapped = swap(first_low)
    first_all = jnp.concatenate([first_low, first_swapped], axis=0)
    table = own_half(bound_table, 1)
    weights = jax.nn.softmax(table, axis=0)
    rows = lax.broadcasted_iota(jnp.int32, (table.shape[0], 1), 0)
    counted = jnp.where((rows >= 1) & (rows <= layer_index[0]), 1.0, 0.0)
    bound = jnp.sum(weights * counted, axis=0)
    bias = own_half(forget_bias, 0)
    gain = own_half(group_gain, 0)
    pre = matmul(first_all, mix_full)
    gated, mixed, states = mixer_forward(pre, bias, bound, gain, second_start, order)
    inputs_own = inputs[:shard_rows]
    out_part = sum_over_chip(gated, out_full, dot_nn)
    first = sum_first(out_part)
    second = sum_second(out_part, *first)
    resid = inputs_own + sum_total(out_part, first, second)

    second_own = (resid * rms_rows(resid) * second_gain).astype(BF16)
    first = gather_first(second_own)
    second_low = jnp.concatenate(
        gather_blocks(second_own, first, gather_second(*first)), axis=0
    )
    cotangent_rel = relative(cotangent, tp_count, tp_at)
    gate_up = matmul(second_low, ffn_full)
    pre_gate = gate_up[:, :hidden_width]
    pre_up = gate_up[:, hidden_width:]
    sig = jax.nn.sigmoid(pre_gate)
    hidden = (pre_gate * sig * pre_up).astype(BF16)

    down_grad = dot_tn(hidden, cotangent_rel).astype(BF16)
    down_sum = scatter(down_grad, ("dp", "ctx"), 1)
    ffn_part = matmul(after(hidden, down_grad), down_full).astype(BF16)
    ffn_first = sum_first(ffn_part)
    hidden_grad = dot_nt(after(cotangent_rel, ffn_part), down_full)
    gate_grad = (hidden_grad * pre_up * sig * (1.0 + pre_gate * (1.0 - sig))).astype(BF16)
    up_grad = (hidden_grad * (pre_gate * sig)).astype(BF16)
    ffn_second = sum_second(after(ffn_part, gate_grad), *ffn_first)
    gate_up_grad = jnp.concatenate([gate_grad, up_grad], axis=1)
    second_part = dot_nt(after(gate_up_grad, *ffn_first), ffn_full).astype(BF16)
    ffn_total = sum_total(ffn_part, ffn_first, ffn_second)
    second_part = after(second_part, *ffn_second)
    first = sum_first(second_part)
    gate_weight_grad = product(second_low, gate_grad, TN, BF16, rows=256)
    gate_sum = scatter(gate_weight_grad, ("dp", "ctx"), 0)
    second = sum_second(second_part, *first)
    second_total = sum_total(second_part, first, second)
    resid_part, second_gain_grad = norm_back(
        after(second_total, down_sum), resid, second_gain
    )
    resid_grad = cotangent_rel[:shard_rows].astype(F32) + resid_part
    resid_own = resid_grad.astype(BF16)
    first = gather_first(resid_own)
    up_weight_grad = product(second_low, up_grad, TN, BF16, rows=256)
    up_sum = scatter(up_weight_grad, ("dp", "ctx"), 0)
    resid_second = gather_second(*first)
    resid_blocks = [resid_own, *first, *resid_second]
    resid_blocks = resid_blocks + [swap(block) for block in resid_blocks]

    block_own = after((resid + ffn_total).astype(BF16), *resid_second)
    block_first = gather_first(block_own)

    gated_grad = blocks_product(resid_blocks, out_full)
    proj_grad, sums = mixer_backward(pre, mixed, gated_grad, states, bias, bound, gain, second_start, order)
    first_other = product(after(proj_grad, *block_first), mix_full, NT, BF16, cols=256, a_half=1)
    block_second = gather_second(*[after(block, proj_grad) for block in block_first])
    first_part = product(
        after(proj_grad, first_other), mix_full, NT, BF16, cols=256, a_half=0, add=swap(first_other)
    )
    first_part = after(first_part, *block_second)
    first = sum_first(first_part)
    mix_grad, first_sum = weight_sum_product(
        first_low, first_swapped, after(proj_grad, first_part), mix_full, resid_blocks, gated, wait=[gate_sum, up_sum]
    )
    mix_sum = scatter(mix_grad, "dp", 0)
    block_own = after(block_own, first_part)
    block_out = placed_blocks(block_own, block_first, block_second, BF16)
    final_first = first
    second = sum_second(first_part, *first)
    input_part, _ = norm_back(sum_total(first_part, first, second), inputs_own, first_gain)
    input_own = (resid_grad + input_part).astype(BF16)
    first = gather_first(input_own)
    input_grad = placed_blocks(input_own, first, gather_second(*first), F32)

    first_gain_grad = first_sum / first_gain
    first_gain_grad = first_sum / first_gain
    gains = jnp.concatenate([first_gain_grad, second_gain_grad]).reshape(-1, HEAD)
    gains = after(gains, *final_first)
    gains = small_sum(gains + swap(gains), "tp")
    heads = sums[:3].reshape(-1, HEAD)
    small = small_sum(jnp.concatenate([heads, gains]), "dp")
    cut = heads.shape[0]
    head_sums = in_order(small[:cut].reshape(3, width), 1)
    gain_sums = small[cut:].reshape(-1)
    all_weights = jax.nn.softmax(bound_table, axis=0)
    all_bound = jnp.sum(all_weights * counted, axis=0)
    table_grad = all_weights * (counted - all_bound) * head_sums[2]

    mix_other = swap(mix_sum)
    first_core = ctx_at == 0
    mix_pair = [jnp.where(first_core, mix_sum, mix_other), jnp.where(first_core, mix_other, mix_sum)]

    def columns(which):
        cols = slice(which * width, (which + 1) * width)
        return jnp.concatenate([part[:, cols] for part in mix_pair], axis=1).astype(F32)

    return (
        block_out,
        input_grad,
        columns(0),
        columns(1),
        columns(2),
        columns(3),
        jnp.concatenate([mix_pair[0][:, 4 * width :].T, mix_pair[1][:, 4 * width :].T], axis=0).astype(F32),
        in_order(after(gate_sum, *final_first), 0).astype(F32),
        in_order(after(up_sum, *final_first), 0).astype(F32),
        in_order(after(down_sum, *final_first), 1).astype(F32),
        gain_sums[:model],
        gain_sums[model:],
        head_sums[0],
        head_sums[1],
        table_grad,
    )


def solution(mesh):
    return jax.shard_map(
        body,
        mesh=mesh,
        in_specs=(
            P(("dp", "ctx"), None),
            P("dp", "tp"),
            P("dp", "tp"),
            P("dp", "tp"),
            P("dp", "tp"),
            P("tp", "dp"),
            P("dp", "tp"),
            P("dp", "tp"),
            P("tp", "dp"),
            P(),
            P(),
            P("tp"),
            P("tp"),
            P(None, "tp"),
            P(),
            P("dp"),
            P(("dp", "ctx"), None),
        ),
        out_specs=(
            P(("dp", "ctx"), None),
            P(("dp", "ctx"), None),
            P("dp", "tp"),
            P("dp", "tp"),
            P("dp", "tp"),
            P("dp", "tp"),
            P("tp", "dp"),
            P("dp", "tp"),
            P("dp", "tp"),
            P("tp", "dp"),
            P(),
            P(),
            P("tp"),
            P("tp"),
            P(None, "tp"),
        ),
        check_vma=False,
    )
```

```python
import functools

import jax
import jax.numpy as jnp
from jax import lax
from jax.experimental import pallas as pl
from jax.experimental.pallas import tpu as pltpu
from jax.sharding import PartitionSpec as P

HEAD = 128
SUB = 32
CHUNK = 128
EPS_NORM = 1e-06
EPS_GROUP = 1e-05
F32 = jnp.float32
VMEM = 58 << 20
UNREAD = pl.BlockSpec(memory_space=pl.ANY)
BF16 = jnp.bfloat16


def cost(flops):
    return pl.CostEstimate(flops=2 * flops, bytes_accessed=1 << 20, transcendentals=0)


def dot_nn(a, b):
    return lax.dot_general(a, b, (((1,), (0,)), ((), ())), preferred_element_type=F32)


def dot_nt(a, b):
    return lax.dot_general(a, b, (((1,), (1,)), ((), ())), preferred_element_type=F32)


def dot_tn(a, b):
    return lax.dot_general(a, b, (((0,), (0,)), ((), ())), preferred_element_type=F32)


def sigmoid_pair(x):
    small = jnp.exp(-jnp.abs(x))
    inv = 1.0 / (1.0 + small)
    rest = small * inv
    up = x >= 0.0
    return jnp.where(up, inv, rest), jnp.where(up, rest, inv)


def tri_dot(tri, x):
    high = x.astype(BF16)
    low = (x - high.astype(F32)).astype(BF16)
    return dot_nn(tri, high) + dot_nn(tri, low)


def triangle(upper):
    rows = lax.broadcasted_iota(jnp.int32, (CHUNK, CHUNK), 0)
    cols = lax.broadcasted_iota(jnp.int32, (CHUNK, CHUNK), 1)
    keep = rows <= cols if upper else rows >= cols
    return jnp.where(keep, 1.0, 0.0).astype(BF16)


def chunk_masks(start, split):
    rows = lax.broadcasted_iota(jnp.int32, (CHUNK, CHUNK), 0)
    cols = lax.broadcasted_iota(jnp.int32, (CHUNK, CHUNK), 1)
    local = split - start
    causal = rows >= cols
    same = (rows >= local) == (cols >= local)
    token = lax.broadcasted_iota(jnp.int32, (CHUNK, HEAD), 0)
    before = start > split
    enter = jnp.where(jnp.logical_or(token < local, before), 1.0, 0.0)
    last = CHUNK - 1 >= local
    tail = jnp.where((token >= local) == last, 1.0, 0.0)
    kept = jnp.where(jnp.logical_or(jnp.logical_not(last), before), 1.0, 0.0)
    return causal & same, enter, tail, kept


def key_rows(k, b, kd, k_end_sub, mids, ends):
    out = []
    count = CHUNK // SUB
    for i in range(count):
        parts = []
        for j in range(i):
            part = k_end_sub[j * SUB : (j + 1) * SUB]
            parts.append(part * jnp.exp(mids[i] - ends[j]))
        parts.append(kd[i * SUB : (i + 1) * SUB])
        if i < count - 1:
            parts.append(jnp.zeros(((count - 1 - i) * SUB, HEAD), F32))
        out.append(jnp.concatenate(parts, axis=0).astype(BF16))
    return out


def spread(rows_list):
    return jnp.concatenate([jnp.broadcast_to(r, (SUB, HEAD)) for r in rows_list], axis=0)


def chunk_common(q, k, log_forget, tri):
    count = CHUNK // SUB
    b = tri_dot(tri, log_forget)
    mids = [b[i * SUB + SUB // 2 : i * SUB + SUB // 2 + 1] for i in range(count)]
    ends = [b[(i + 1) * SUB - 1 : (i + 1) * SUB] for i in range(count)]
    mid = spread(mids)
    end = spread(ends)
    to_mid = jnp.exp(b - mid)
    from_mid = jnp.exp(mid - b)
    to_end = jnp.exp(end - b)
    whole = jnp.exp(b)
    final = ends[-1]
    to_final = jnp.exp(final - b)
    qd = (q * to_mid).astype(BF16)
    keys = key_rows(k, b, k * from_mid, k * to_end, mids, ends)
    return b, mids, ends, to_mid, from_mid, to_end, whole, final, to_final, qd, keys


def scores_of(qd, keys):
    count = CHUNK // SUB
    return jnp.concatenate(
        [dot_nt(qd[i * SUB : (i + 1) * SUB], keys[i]) for i in range(count)], axis=0
    )


def forward_kernel(
    heads,
    chunks,
    order_ref,
    split_ref,
    pre_ref,
    bias_ref,
    bound_ref,
    gain_ref,
    gated_ref,
    mixed_ref,
    states_ref,
    state,
):
    step = pl.program_id(0)
    width = heads * HEAD

    @pl.when(step == 0)
    def _():
        state[...] = jnp.zeros_like(state)

    split = split_ref[0]
    tri = triangle(False)
    for n in range(chunks):
        start = (step * chunks + n) * CHUNK
        allowed, enter, tail, kept = chunk_masks(start, split)
        rows = slice(n * CHUNK, (n + 1) * CHUNK)
        for h in range(heads):
            cols = slice(h * HEAD, (h + 1) * HEAD)

            def part(which):
                return pre_ref[rows, which * width + h * HEAD : which * width + (h + 1) * HEAD]

            pre_q = part(0)
            q = pre_q * sigmoid_pair(pre_q)[0]
            bound = bound_ref[:, cols]
            plus, minus = sigmoid_pair(part(1) + bias_ref[:, cols])
            k = (1.0 - bound) * minus
            log_forget = jnp.log(bound + (1.0 - bound) * plus)
            _, _, _, _, _, _, whole, final, to_final, qd, keys = chunk_common(q, k, log_forget, tri)
            v = part(2).astype(BF16)
            scores = jnp.where(allowed, scores_of(qd, keys), 0.0).astype(BF16)
            old = state[h]
            states_ref[n, h] = old
            mixed = dot_nn(scores, v) + dot_nt((q * whole * enter).astype(BF16), old.astype(BF16))
            ending = (k * to_final * tail).astype(BF16)
            state[h] = old * (jnp.exp(final) * kept) + dot_tn(v, ending)
            mixed_ref[rows, cols] = mixed
            scale = lax.rsqrt(jnp.mean(mixed * mixed, axis=-1, keepdims=True) + EPS_GROUP)
            pre_g = part(3)
            gate = pre_g * sigmoid_pair(pre_g)[0]
            gated_ref[rows, cols] = (mixed * scale * gain_ref[:, cols] * gate).astype(BF16)


def mixer_forward(pre, bias, bound, gain, split, order):
    tokens, wide = pre.shape
    width = wide // 4
    heads = width // HEAD
    steps = order.shape[0]
    block = tokens // steps
    chunks = block // CHUNK
    row = pl.BlockSpec((1, width), lambda i, order: (0, 0))
    grid_spec = pltpu.PrefetchScalarGridSpec(
        num_scalar_prefetch=1,
        grid=(steps,),
        in_specs=[
            pl.BlockSpec(memory_space=pltpu.SMEM),
            pl.BlockSpec((block, wide), lambda i, order: (order[i], 0)),
            row,
            row,
            row,
        ],
        out_specs=[
            pl.BlockSpec((block, width), lambda i, order: (order[i], 0)),
            pl.BlockSpec((block, width), lambda i, order: (i, 0)),
            pl.BlockSpec((chunks, heads, HEAD, HEAD), lambda i, order: (i, 0, 0, 0)),
        ],
        scratch_shapes=[pltpu.VMEM((heads, HEAD, HEAD), F32)],
    )
    return pl.pallas_call(
        functools.partial(forward_kernel, heads, chunks),
        grid_spec=grid_spec,
        out_shape=[
            jax.ShapeDtypeStruct((tokens, width), BF16),
            jax.ShapeDtypeStruct((tokens, width), F32),
            jax.ShapeDtypeStruct((tokens // CHUNK, heads, HEAD, HEAD), F32),
        ],
        compiler_params=pltpu.CompilerParams(
            dimension_semantics=("arbitrary",), vmem_limit_bytes=VMEM
        ),
        cost_estimate=cost(tokens * width * 14000),
        name="mixer_forward",
    )(order, split, pre, bias[None], bound[None], gain[None])


def backward_kernel(
    heads,
    chunks,
    order_ref,
    split_ref,
    pre_ref,
    mixed_ref,
    grad_ref,
    states_ref,
    bias_ref,
    bound_ref,
    gain_ref,
    out_ref,
    sums_ref,
    adjoint,
    later,
):
    step = pl.program_id(0)
    steps = pl.num_programs(0)
    width = heads * HEAD
    count = CHUNK // SUB

    @pl.when(step == 0)
    def _():
        adjoint[...] = jnp.zeros_like(adjoint)
        later[...] = jnp.zeros_like(later)
        sums_ref[...] = jnp.zeros_like(sums_ref)

    split = split_ref[0]
    tri = triangle(False)
    tri_up = triangle(True)
    for n in reversed(range(chunks)):
        start = ((steps - 1 - step) * chunks + n) * CHUNK
        allowed, enter, tail, kept = chunk_masks(start, split)
        rows = slice(n * CHUNK, (n + 1) * CHUNK)
        for h in range(heads):
            cols = slice(h * HEAD, (h + 1) * HEAD)

            def part(which):
                return pre_ref[rows, which * width + h * HEAD : which * width + (h + 1) * HEAD]

            def store(which, value):
                out_ref[rows, which * width + h * HEAD : which * width + (h + 1) * HEAD] = value.astype(BF16)

            pre_q = part(0)
            sig_q, sig_nq = sigmoid_pair(pre_q)
            q = pre_q * sig_q
            bound = bound_ref[:, cols]
            plus, minus = sigmoid_pair(part(1) + bias_ref[:, cols])
            k = (1.0 - bound) * minus
            forget = bound + (1.0 - bound) * plus
            _, mids, ends, to_mid, from_mid, to_end, whole, final, to_final, qd, keys = chunk_common(
                q, k, jnp.log(forget), tri
            )
            v = part(2).astype(BF16)

            mixed = mixed_ref[rows, cols]
            grad = grad_ref[rows, cols].astype(F32)
            gain = gain_ref[:, cols]
            scale = lax.rsqrt(jnp.mean(mixed * mixed, axis=-1, keepdims=True) + EPS_GROUP)
            pre_g = part(3)
            sig_g, sig_ng = sigmoid_pair(pre_g)
            gate = pre_g * sig_g
            unit = mixed * scale
            u = grad * gain * gate
            moment = jnp.mean(u * unit, axis=-1, keepdims=True)
            mixed_grad = scale * (u - unit * moment)
            gu = grad * unit
            gain_sum = jnp.sum(gu * gate, axis=0, keepdims=True)
            store(3, gu * gain * (sig_g * (1.0 + pre_g * sig_ng)))

            do = mixed_grad.astype(BF16)
            old = states_ref[n, h]
            lam = adjoint[h]
            old_low = old.astype(BF16)
            lam_low = lam.astype(BF16)
            scores = jnp.where(allowed, scores_of(qd, keys), 0.0).astype(BF16)
            pair = jnp.where(allowed, dot_nt(do, v), 0.0).astype(BF16)
            reach = whole * enter
            remain = to_final * tail
            ending = (k * remain).astype(BF16)
            store(2, dot_tn(scores, do) + dot_nt(ending, lam_low))

            q_rows = []
            k_rows = [None] * count
            for i in range(count):
                pair_i = pair[i * SUB : (i + 1) * SUB]
                q_rows.append(dot_nn(pair_i, keys[i]))
                back = dot_tn(pair_i, qd[i * SUB : (i + 1) * SUB])
                for j in range(i + 1):
                    piece = back[j * SUB : (j + 1) * SUB]
                    if j == i:
                        piece = piece * from_mid[j * SUB : (j + 1) * SUB]
                        k_rows[j] = (k_rows[j], piece)
                    else:
                        piece = piece * jnp.exp(mids[i] - ends[j])
                        first = k_rows[j]
                        k_rows[j] = piece if first is None else first + piece
                diagonal = k_rows[i][1]
                k_rows[i] = None
                if i == 0:
                    diagonals = []
                diagonals.append(diagonal)
            k_intra = []
            for j in range(count):
                piece = diagonals[j]
                if k_rows[j] is not None:
                    piece = piece + k_rows[j] * to_end[j * SUB : (j + 1) * SUB]
                k_intra.append(piece)
            dq = jnp.concatenate(q_rows, axis=0) * to_mid + dot_nn(do, old_low) * reach
            dk = jnp.concatenate(k_intra, axis=0) + dot_nn(v, lam_low) * remain
            anchor = jnp.sum(lam * later[h], axis=0, keepdims=True)
            dlog = tri_dot(tri_up, q * dq - k * dk) + anchor
            adjoint[h] = lam * (jnp.exp(final) * kept) + dot_tn(do, (q * reach).astype(BF16))
            later[h] = old

            store(0, dq * (sig_q * (1.0 + pre_q * sig_nq)))
            drive = minus * (dlog / forget - dk)
            forget_grad = (1.0 - bound) * plus * drive
            store(1, forget_grad)
            sums_ref[0:1, cols] += gain_sum
            sums_ref[1:2, cols] += jnp.sum(forget_grad, axis=0, keepdims=True)
            sums_ref[2:3, cols] += jnp.sum(drive, axis=0, keepdims=True)


def mixer_backward(pre, mixed, grad, states, bias, bound, gain, split, order):
    tokens, wide = pre.shape
    width = wide // 4
    heads = width // HEAD
    steps = order.shape[0]
    block = tokens // steps
    chunks = block // CHUNK
    row = pl.BlockSpec((1, width), lambda i, order: (0, 0))
    placed = lambda i, order: (order[steps - 1 - i], 0)
    grid_spec = pltpu.PrefetchScalarGridSpec(
        num_scalar_prefetch=1,
        grid=(steps,),
        in_specs=[
            pl.BlockSpec(memory_space=pltpu.SMEM),
            pl.BlockSpec((block, wide), placed),
            pl.BlockSpec((block, width), lambda i, order: (steps - 1 - i, 0)),
            pl.BlockSpec((block, width), placed),
            pl.BlockSpec((chunks, heads, HEAD, HEAD), lambda i, order: (steps - 1 - i, 0, 0, 0)),
            row,
            row,
            row,
        ],
        out_specs=[
            pl.BlockSpec((block, wide), placed),
            pl.BlockSpec((8, width), lambda i, order: (0, 0)),
        ],
        scratch_shapes=[pltpu.VMEM((heads, HEAD, HEAD), F32), pltpu.VMEM((heads, HEAD, HEAD), F32)],
    )
    return pl.pallas_call(
        functools.partial(backward_kernel, heads, chunks),
        grid_spec=grid_spec,
        out_shape=[
            jax.ShapeDtypeStruct((tokens, wide), BF16),
            jax.ShapeDtypeStruct((8, width), F32),
        ],
        compiler_params=pltpu.CompilerParams(
            dimension_semantics=("arbitrary",), vmem_limit_bytes=VMEM
        ),
        cost_estimate=cost(tokens * width * 22000),
        name="mixer_backward",
    )(order, split, pre, mixed, grad, states, bias[None], bound[None], gain[None])


def blocks_of(array, count):
    size = array.shape[0] // count
    return [array[m * size : (m + 1) * size] for m in range(count)]


def product_kernel(dims, parts, a_ref, b_ref, *refs):
    dot = lax.dot_general(a_ref[...], b_ref[...], (dims, ((), ())), preferred_element_type=F32)
    for block, out_ref in zip(blocks_of(dot, parts), refs[len(refs) - parts :]):
        out_ref[...] = block.astype(out_ref.dtype)


NN = ((1,), (0,))
NT = ((1,), (1,))
TN = ((0,), (0,))


def product(a, b, dims, kind, rows=None, cols=None, a_half=None, parts=1, wait=()):
    count = a.shape[1 - dims[0][0]] if a_half is None else a.shape[0] // 2
    depth = a.shape[dims[0][0]]
    wide = b.shape[1 - dims[1][0]]
    tile_rows = rows or count
    tile_cols = cols or wide
    by_rows = rows is not None
    shift = (a_half or 0) * (count // tile_rows)

    def at_row(i):
        return (i if by_rows else 0) + shift

    def at_col(i):
        return 0 if by_rows else i

    if dims[0][0] == 1:
        a_spec = pl.BlockSpec((tile_rows, depth), lambda i: (at_row(i), 0))
    else:
        a_spec = pl.BlockSpec((depth, tile_rows), lambda i: (0, at_row(i)))
    if dims[1][0] == 0:
        b_spec = pl.BlockSpec((depth, tile_cols), lambda i: (0, at_col(i)))
    else:
        b_spec = pl.BlockSpec((tile_cols, depth), lambda i: (at_col(i), 0))
    out_spec = pl.BlockSpec((tile_rows // parts, tile_cols), lambda i: (at_row(i) - shift, at_col(i)))
    out = pl.pallas_call(
        functools.partial(product_kernel, dims, parts),
        grid=(count // tile_rows * (wide // tile_cols),),
        in_specs=[a_spec, b_spec] + [UNREAD] * len(wait),
        out_specs=[out_spec] * parts,
        out_shape=[jax.ShapeDtypeStruct((count // parts, wide), kind)] * parts,
        compiler_params=pltpu.CompilerParams(
            dimension_semantics=("arbitrary",), vmem_limit_bytes=VMEM
        ),
        cost_estimate=cost(2 * count * wide * depth),
        name="product",
    )(a, b, *wait)
    return out[0] if parts == 1 else out


def weight_sum_kernel(own_ref, other_ref, b_ref, weight_ref, right_ref, *refs):
    out_ref, sum_ref = refs[-2:]
    half = own_ref.shape[0]
    wide = b_ref.shape[1]
    dot = dot_tn(own_ref[...], b_ref[:half]) + dot_tn(other_ref[...], b_ref[half:])
    out_ref[:, :wide] = dot.astype(out_ref.dtype)
    total = jnp.sum(dot * weight_ref[...].astype(F32), axis=1, keepdims=True)
    sum_ref[...] = jnp.broadcast_to(total, sum_ref.shape)
    start = 0
    more = None
    for ref in refs[:-2]:
        size = ref.shape[0]
        if start < right_ref.shape[0]:
            term = dot_tn(ref[...], right_ref[start : start + size])
            more = term if more is None else more + term
            start += size
    out_ref[:, wide:] = more.astype(out_ref.dtype)


def weight_sum_product(own, other, b, weight, blocks, right, rows=256, wait=()):
    half, count = own.shape
    depth, wide = b.shape
    extra = right.shape[1]
    a_spec = pl.BlockSpec((half, rows), lambda i: (0, i))
    out, total = pl.pallas_call(
        weight_sum_kernel,
        grid=(count // rows,),
        in_specs=[
            a_spec,
            a_spec,
            pl.BlockSpec((depth, wide), lambda i: (0, 0)),
            pl.BlockSpec((rows, wide), lambda i: (i, 0)),
            pl.BlockSpec((depth, extra), lambda i: (0, 0)),
        ]
        + [pl.BlockSpec((block.shape[0], rows), lambda i: (0, i)) for block in blocks]
        + [UNREAD] * len(wait),
        out_specs=[
            pl.BlockSpec((rows, wide + extra), lambda i: (i, 0)),
            pl.BlockSpec((rows, HEAD), lambda i: (i, 0)),
        ],
        out_shape=[
            jax.ShapeDtypeStruct((count, wide + extra), BF16),
            jax.ShapeDtypeStruct((count, HEAD), F32),
        ],
        compiler_params=pltpu.CompilerParams(
            dimension_semantics=("arbitrary",), vmem_limit_bytes=VMEM
        ),
        cost_estimate=cost(2 * count * (wide + extra) * depth),
        name="weight_sum_product",
    )(own, other, b, weight, right, *blocks, *wait)
    return out, total[:, 0]


def blocks_product_kernel(b_ref, *refs):
    out_ref = refs[-1]
    start = 0
    for ref in refs[:-1]:
        size = ref.shape[0]
        out_ref[start : start + size] = dot_nt(ref[...], b_ref[...])
        start += size


def blocks_product(blocks, b):
    count = sum(block.shape[0] for block in blocks)
    return pl.pallas_call(
        blocks_product_kernel,
        out_shape=jax.ShapeDtypeStruct((count, b.shape[0]), F32),
        compiler_params=pltpu.CompilerParams(vmem_limit_bytes=VMEM),
        cost_estimate=cost(2 * count * b.size),
        name="blocks_product",
    )(b, *blocks)


def joined_columns_kernel(width, at_ref, own_ref, other_ref, *out_refs):
    def store(ref):
        for which in range(4):
            out_refs[which][...] = ref[:, which * width : (which + 1) * width].astype(F32)
        out_refs[4][...] = ref[:, 4 * width :].astype(F32).T

    mine = pl.program_id(0) == at_ref[0]
    pl.when(mine)(lambda: store(own_ref))
    pl.when(jnp.logical_not(mine))(lambda: store(other_ref))


def joined_columns(own, other, at, width):
    rows = own.shape[0]
    whole = pl.BlockSpec(own.shape, lambda i, at: (0, 0))
    beside = pl.BlockSpec((rows, width), lambda i, at: (0, i))
    return pl.pallas_call(
        functools.partial(joined_columns_kernel, width),
        grid_spec=pltpu.PrefetchScalarGridSpec(
            num_scalar_prefetch=1,
            grid=(2,),
            in_specs=[whole, whole],
            out_specs=[beside] * 4 + [pl.BlockSpec((width, rows), lambda i, at: (i, 0))],
        ),
        out_shape=[jax.ShapeDtypeStruct((rows, 2 * width), F32)] * 4
        + [jax.ShapeDtypeStruct((2 * width, rows), F32)],
        compiler_params=pltpu.CompilerParams(
            dimension_semantics=("arbitrary",), vmem_limit_bytes=VMEM
        ),
        cost_estimate=cost(1 << 20),
        name="joined_columns",
    )(at.astype(jnp.int32).reshape(1), own, other)


def rms_rows(rows_in):
    return lax.rsqrt(jnp.mean(rows_in * rows_in, axis=-1, keepdims=True) + EPS_NORM)


def norm_back(grad, rows_in, gain_vec):
    inv = rms_rows(rows_in)
    u = grad * gain_vec
    moment = jnp.mean(u * rows_in, axis=-1, keepdims=True)
    return inv * u - rows_in * (inv * inv * inv * moment), jnp.sum(grad * rows_in * inv, axis=0)


def gather(part, axes, dim):
    return lax.all_gather(part, axes, axis=dim, tiled=True)


def scatter(whole, axes, dim):
    return lax.psum_scatter(whole, axes, scatter_dimension=dim, tiled=True)


def matmul(left_side, right_side):
    return jnp.dot(left_side, right_side, preferred_element_type=F32)


def after(value, *others):
    return lax.optimization_barrier((value, *others))[0]


def small_sum(part, axis):
    count = lax.axis_size(axis)
    if count <= 4:
        got = [lax.ppermute(part, axis, [(i, i ^ m) for i in range(count)]) for m in range(1, count)]
        return sum(got, part)
    mask = 1
    while mask < count:
        part = part + lax.ppermute(part, axis, [(i, i ^ mask) for i in range(count)])
        mask *= 2
    return part


def together(*values):
    return lax.optimization_barrier(values)


def swap(part):
    return lax.ppermute(part, "ctx", [(0, 1), (1, 0)])


def in_order(own, dim):
    other = swap(own)
    first = lax.axis_index("ctx") == 0
    return jnp.concatenate([jnp.where(first, own, other), jnp.where(first, other, own)], axis=dim)


def partner(part, mask):
    return lax.ppermute(part, "tp", [(i, i ^ mask) for i in range(lax.axis_size("tp"))])


def relative(array, count, at):
    size = array.shape[0] // count
    return jnp.concatenate(
        [lax.dynamic_slice_in_dim(array, (at ^ m) * size, size, 0) for m in range(count)], axis=0
    )


def piece(parts, block, which):
    half = parts[block].shape[0] // 2
    return parts[block][which * half : (which + 1) * half]


def sum_first(parts):
    near = partner(jnp.concatenate([piece(parts, 1, 0), piece(parts, 3, 0)], axis=0), 1)
    far = partner(jnp.concatenate([piece(parts, 2, 1), piece(parts, 3, 1)], axis=0), 2)
    return near, far


def sum_second(parts, near, far):
    half = near.shape[0] // 2
    near, far = together(near, far)
    pass_far = (piece(parts, 2, 0).astype(F32) + near[half:].astype(F32)).astype(BF16)
    pass_near = (piece(parts, 1, 1).astype(F32) + far[half:].astype(F32)).astype(BF16)
    pass_far, pass_near = together(pass_far, pass_near)
    return together(partner(pass_far, 2), partner(pass_near, 1))


def sum_total(parts, first, second):
    half = second[0].shape[0]
    halves = [
        piece(parts, 0, which).astype(F32) + first[which][:half].astype(F32) + second[which].astype(F32)
        for which in (0, 1)
    ]
    return jnp.concatenate(halves, axis=0)


def gather_first(own):
    return partner(own, 1), partner(own, 2)


def gather_second(near, far):
    half = near.shape[0] // 2
    return partner(far[:half], 1), partner(near[half:], 2)


def gather_blocks(own, first, second):
    return [own, *first, jnp.concatenate(second, axis=0)]


def placed_kernel(at_ref, own_ref, near_ref, far_ref, top_ref, bottom_ref, out_ref):
    step = pl.program_id(0)
    half = top_ref.shape[0]
    for which, ref in enumerate((own_ref, near_ref, far_ref)):

        @pl.when(step == which)
        def _(ref=ref):
            out_ref[...] = ref[...].astype(out_ref.dtype)

    @pl.when(step == 3)
    def _():
        out_ref[:half] = top_ref[...].astype(out_ref.dtype)
        out_ref[half:] = bottom_ref[...].astype(out_ref.dtype)


def placed_blocks(own, near, far, top, bottom, at, kind):
    size, width = own.shape
    inputs = [own, near, far, top, bottom]
    return pl.pallas_call(
        placed_kernel,
        grid_spec=pltpu.PrefetchScalarGridSpec(
            num_scalar_prefetch=1,
            grid=(4,),
            in_specs=[pl.BlockSpec(part.shape, lambda i, at: (0, 0)) for part in inputs],
            out_specs=pl.BlockSpec((size, width), lambda i, at: (i ^ at[0], 0)),
        ),
        out_shape=jax.ShapeDtypeStruct((4 * size, width), kind),
        compiler_params=pltpu.CompilerParams(
            dimension_semantics=("arbitrary",), vmem_limit_bytes=VMEM
        ),
        cost_estimate=cost(1 << 20),
        name="placed_blocks",
    )(at.astype(jnp.int32).reshape(1), *inputs)


def body(
    block_in,
    query_proj,
    forget_proj,
    value_proj,
    outgate_proj,
    out_proj,
    ffn_gate,
    ffn_up,
    ffn_down,
    first_gain,
    second_gain,
    group_gain,
    forget_bias,
    bound_table,
    layer_index,
    second_start,
    cotangent,
):
    ctx_count, ctx_at = lax.axis_size("ctx"), lax.axis_index("ctx")
    tp_count, tp_at = lax.axis_size("tp"), lax.axis_index("tp")
    row_count, model = block_in.shape
    local_width = query_proj.shape[1]
    width = local_width // ctx_count
    hidden_width = ffn_gate.shape[1]
    shard_rows = row_count // tp_count

    def own_half(array, dim):
        size = array.shape[dim] // ctx_count
        return lax.dynamic_slice_in_dim(array, ctx_at * size, size, dim)

    def sum_over_chip(rows_in, right_side, dot):
        other = swap(dot(rows_in[row_count:], right_side).astype(BF16))
        own = dot(rows_in[:row_count], right_side)
        return (own + other.astype(F32)).astype(BF16)

    blocks = ctx_count * tp_count
    order = lax.iota(jnp.int32, blocks) ^ (ctx_at * tp_count + tp_at)

    mix_full = gather(
        jnp.concatenate(
            [own_half(w, 1) for w in (query_proj, forget_proj, value_proj, outgate_proj)], axis=1
        ),
        "dp",
        0,
    )
    out_full = gather(own_half(out_proj, 0), "dp", 1)
    ffn_full = gather(own_half(jnp.concatenate([ffn_gate, ffn_up], axis=1), 0), ("dp", "ctx"), 0)
    down_full = gather(own_half(ffn_down, 1), ("dp", "ctx"), 1)

    inputs = relative(block_in, tp_count, tp_at).astype(F32)
    first_low = (inputs * rms_rows(inputs) * first_gain).astype(BF16)
    first_swapped = swap(first_low)
    first_all = jnp.concatenate([first_low, first_swapped], axis=0)
    table = own_half(bound_table, 1)
    weights = jax.nn.softmax(table, axis=0)
    rows = lax.broadcasted_iota(jnp.int32, (table.shape[0], 1), 0)
    counted = jnp.where((rows >= 1) & (rows <= layer_index[0]), 1.0, 0.0)
    bound = jnp.sum(weights * counted, axis=0)
    bias = own_half(forget_bias, 0)
    gain = own_half(group_gain, 0)
    pre = matmul(first_all, mix_full)
    gated, mixed, states = mixer_forward(pre, bias, bound, gain, second_start, order)
    inputs_own = inputs[:shard_rows]
    out_part = blocks_of(sum_over_chip(gated, out_full, dot_nn), tp_count)
    first = sum_first(out_part)
    second = sum_second(out_part, *first)
    resid = inputs_own + sum_total(out_part, first, second)

    second_own = (resid * rms_rows(resid) * second_gain).astype(BF16)
    first = gather_first(second_own)
    second_low = jnp.concatenate(
        gather_blocks(second_own, first, gather_second(*first)), axis=0
    )
    cotangent_rel = relative(cotangent, tp_count, tp_at)
    gate_up = matmul(second_low, ffn_full)
    pre_gate = gate_up[:, :hidden_width]
    pre_up = gate_up[:, hidden_width:]
    sig = jax.nn.sigmoid(pre_gate)
    hidden = (pre_gate * sig * pre_up).astype(BF16)

    down_grad = dot_tn(hidden, cotangent_rel).astype(BF16)
    down_sum = scatter(down_grad, ("dp", "ctx"), 1)
    hidden_grad = dot_nt(after(cotangent_rel, down_grad), down_full)
    gate_grad = (hidden_grad * pre_up * sig * (1.0 + pre_gate * (1.0 - sig))).astype(BF16)
    up_grad = (hidden_grad * (pre_gate * sig)).astype(BF16)
    gate_up_grad = jnp.concatenate([gate_grad, up_grad], axis=1)
    second_part = blocks_of(dot_nt(gate_up_grad, ffn_full).astype(BF16), tp_count)
    first = sum_first(second_part)
    ffn_part = matmul(after(hidden, *second_part), down_full).astype(BF16)
    gate_weight_grad = product(second_low, gate_grad, TN, BF16, rows=256)
    gate_sum = scatter(after(gate_weight_grad, *first), ("dp", "ctx"), 0)
    second = sum_second(second_part, *first)
    second_total = sum_total(second_part, first, second)
    resid_part, second_gain_grad = norm_back(
        after(second_total, down_sum), resid, second_gain
    )
    resid_grad = cotangent_rel[:shard_rows].astype(F32) + resid_part
    resid_own = resid_grad.astype(BF16)
    first = gather_first(resid_own)
    up_weight_grad = product(second_low, up_grad, TN, BF16, rows=256)
    up_sum = scatter(after(up_weight_grad, *first), ("dp", "ctx"), 0)
    resid_second = gather_second(*first)
    resid_blocks = [resid_own, *first, *resid_second]
    resid_blocks = resid_blocks + [swap(block) for block in resid_blocks]

    ffn_part = blocks_of(after(ffn_part, *resid_second), tp_count)
    ffn_first = sum_first(ffn_part)
    gated_grad = blocks_product(resid_blocks, out_full)
    proj_grad, sums = mixer_backward(pre, mixed, gated_grad, states, bias, bound, gain, second_start, order)
    first_other = product(proj_grad, mix_full, NT, BF16, cols=256, a_half=1, parts=tp_count, wait=ffn_first)
    ffn_second = sum_second([after(block, proj_grad) for block in ffn_part], *ffn_first)
    block_own = (resid + sum_total(ffn_part, ffn_first, ffn_second)).astype(BF16)
    first_own = product(
        proj_grad, mix_full, NT, BF16, cols=256, a_half=0, parts=tp_count, wait=[first_other[0], block_own]
    )
    block_first = gather_first(block_own)
    first_part = [
        after((own.astype(F32) + swap(other).astype(F32)).astype(BF16), *block_first)
        for own, other in zip(first_own, first_other)
    ]
    first = sum_first(first_part)
    mix_grad, first_sum = weight_sum_product(
        first_low, first_swapped, proj_grad, mix_full, resid_blocks, gated, wait=[gate_sum, up_sum]
    )
    mix_sum = scatter(after(mix_grad, *first), "dp", 0)
    final_first = first
    second = sum_second(first_part, *first)
    input_part, _ = norm_back(sum_total(first_part, first, second), inputs_own, first_gain)
    input_own = (resid_grad + input_part).astype(BF16)
    block_second = gather_second(*[after(block, input_own) for block in block_first])
    first = together(*gather_first(input_own), *block_second)[:2]
    input_grad = placed_blocks(input_own, *first, *gather_second(*first), tp_at, F32)
    block_out = placed_blocks(block_own, *block_first, *after(block_second, *first), tp_at, BF16)

    gains = jnp.concatenate([first_sum / first_gain, second_gain_grad]).reshape(-1, HEAD)
    gains = after(gains, *first)
    gains = small_sum(gains + swap(gains), "tp")
    heads = sums[:3].reshape(-1, HEAD)
    small = small_sum(jnp.concatenate([heads, gains]), "dp")
    cut = heads.shape[0]
    head_sums = in_order(small[:cut].reshape(3, width), 1)
    gain_sums = small[cut:].reshape(-1)
    all_weights = jax.nn.softmax(bound_table, axis=0)
    all_bound = jnp.sum(all_weights * counted, axis=0)
    table_grad = all_weights * (counted - all_bound) * head_sums[2]

    *mix_shards, out_shard = joined_columns(mix_sum, swap(mix_sum), ctx_at, width)

    return (
        block_out,
        input_grad,
        *mix_shards,
        out_shard,
        in_order(after(gate_sum, *final_first), 0).astype(F32),
        in_order(after(up_sum, *final_first), 0).astype(F32),
        in_order(after(down_sum, *final_first), 1).astype(F32),
        gain_sums[:model],
        gain_sums[model:],
        head_sums[0],
        head_sums[1],
        table_grad,
    )


def solution(mesh):
    return jax.shard_map(
        body,
        mesh=mesh,
        in_specs=(
            P(("dp", "ctx"), None),
            P("dp", "tp"),
            P("dp", "tp"),
            P("dp", "tp"),
            P("dp", "tp"),
            P("tp", "dp"),
            P("dp", "tp"),
            P("dp", "tp"),
            P("tp", "dp"),
            P(),
            P(),
            P("tp"),
            P("tp"),
            P(None, "tp"),
            P(),
            P("dp"),
            P(("dp", "ctx"), None),
        ),
        out_specs=(
            P(("dp", "ctx"), None),
            P(("dp", "ctx"), None),
            P("dp", "tp"),
            P("dp", "tp"),
            P("dp", "tp"),
            P("dp", "tp"),
            P("tp", "dp"),
            P("dp", "tp"),
            P("dp", "tp"),
            P("tp", "dp"),
            P(),
            P(),
            P("tp"),
            P("tp"),
            P(None, "tp"),
        ),
        check_vma=False,
    )
```

```python
import functools

import jax
import jax.numpy as jnp
from jax import lax
from jax.experimental import pallas as pl
from jax.experimental.pallas import tpu as pltpu
from jax.sharding import PartitionSpec as P

HEAD = 128
SUB = 32
CHUNK = 128
EPS_NORM = 1e-06
EPS_GROUP = 1e-05
F32 = jnp.float32
VMEM = 58 << 20
UNREAD = pl.BlockSpec(memory_space=pl.ANY)
BF16 = jnp.bfloat16


def cost(flops):
    return pl.CostEstimate(flops=2 * flops, bytes_accessed=1 << 20, transcendentals=0)


def dot_nn(a, b):
    return lax.dot_general(a, b, (((1,), (0,)), ((), ())), preferred_element_type=F32)


def dot_nt(a, b):
    return lax.dot_general(a, b, (((1,), (1,)), ((), ())), preferred_element_type=F32)


def dot_tn(a, b):
    return lax.dot_general(a, b, (((0,), (0,)), ((), ())), preferred_element_type=F32)


def sigmoid_pair(x):
    small = jnp.exp(-jnp.abs(x))
    inv = 1.0 / (1.0 + small)
    rest = small * inv
    up = x >= 0.0
    return jnp.where(up, inv, rest), jnp.where(up, rest, inv)


def tri_dot(tri, x):
    high = x.astype(BF16)
    low = (x - high.astype(F32)).astype(BF16)
    return dot_nn(tri, high) + dot_nn(tri, low)


def triangle(upper):
    rows = lax.broadcasted_iota(jnp.int32, (CHUNK, CHUNK), 0)
    cols = lax.broadcasted_iota(jnp.int32, (CHUNK, CHUNK), 1)
    keep = rows <= cols if upper else rows >= cols
    return jnp.where(keep, 1.0, 0.0).astype(BF16)


def chunk_masks(start, split):
    rows = lax.broadcasted_iota(jnp.int32, (CHUNK, CHUNK), 0)
    cols = lax.broadcasted_iota(jnp.int32, (CHUNK, CHUNK), 1)
    local = split - start
    causal = rows >= cols
    same = (rows >= local) == (cols >= local)
    token = lax.broadcasted_iota(jnp.int32, (CHUNK, HEAD), 0)
    before = start > split
    enter = jnp.where(jnp.logical_or(token < local, before), 1.0, 0.0)
    last = CHUNK - 1 >= local
    tail = jnp.where((token >= local) == last, 1.0, 0.0)
    kept = jnp.where(jnp.logical_or(jnp.logical_not(last), before), 1.0, 0.0)
    return causal & same, enter, tail, kept


def key_rows(k, b, kd, k_end_sub, mids, ends):
    out = []
    count = CHUNK // SUB
    for i in range(count):
        parts = []
        for j in range(i):
            part = k_end_sub[j * SUB : (j + 1) * SUB]
            parts.append(part * jnp.exp(mids[i] - ends[j]))
        parts.append(kd[i * SUB : (i + 1) * SUB])
        if i < count - 1:
            parts.append(jnp.zeros(((count - 1 - i) * SUB, HEAD), F32))
        out.append(jnp.concatenate(parts, axis=0).astype(BF16))
    return out


def spread(rows_list):
    return jnp.concatenate([jnp.broadcast_to(r, (SUB, HEAD)) for r in rows_list], axis=0)


def chunk_common(q, k, log_forget, tri):
    count = CHUNK // SUB
    b = tri_dot(tri, log_forget)
    mids = [b[i * SUB + SUB // 2 : i * SUB + SUB // 2 + 1] for i in range(count)]
    ends = [b[(i + 1) * SUB - 1 : (i + 1) * SUB] for i in range(count)]
    mid = spread(mids)
    end = spread(ends)
    to_mid = jnp.exp(b - mid)
    from_mid = jnp.exp(mid - b)
    to_end = jnp.exp(end - b)
    whole = jnp.exp(b)
    final = ends[-1]
    to_final = jnp.exp(final - b)
    qd = (q * to_mid).astype(BF16)
    keys = key_rows(k, b, k * from_mid, k * to_end, mids, ends)
    return b, mids, ends, to_mid, from_mid, to_end, whole, final, to_final, qd, keys


def scores_of(qd, keys):
    count = CHUNK // SUB
    return jnp.concatenate(
        [dot_nt(qd[i * SUB : (i + 1) * SUB], keys[i]) for i in range(count)], axis=0
    )


def forward_kernel(
    heads,
    chunks,
    order_ref,
    split_ref,
    pre_ref,
    bias_ref,
    bound_ref,
    gain_ref,
    gated_ref,
    mixed_ref,
    states_ref,
    state,
):
    step = pl.program_id(0)
    width = heads * HEAD

    @pl.when(step == 0)
    def _():
        state[...] = jnp.zeros_like(state)

    split = split_ref[0]
    tri = triangle(False)
    for n in range(chunks):
        start = (step * chunks + n) * CHUNK
        allowed, enter, tail, kept = chunk_masks(start, split)
        rows = slice(n * CHUNK, (n + 1) * CHUNK)
        for h in range(heads):
            cols = slice(h * HEAD, (h + 1) * HEAD)

            def part(which):
                return pre_ref[rows, which * width + h * HEAD : which * width + (h + 1) * HEAD]

            pre_q = part(0)
            q = pre_q * sigmoid_pair(pre_q)[0]
            bound = bound_ref[:, cols]
            plus, minus = sigmoid_pair(part(1) + bias_ref[:, cols])
            k = (1.0 - bound) * minus
            log_forget = jnp.log(bound + (1.0 - bound) * plus)
            _, _, _, _, _, _, whole, final, to_final, qd, keys = chunk_common(q, k, log_forget, tri)
            v = part(2).astype(BF16)
            scores = jnp.where(allowed, scores_of(qd, keys), 0.0).astype(BF16)
            old = state[h]
            states_ref[n, h] = old
            mixed = dot_nn(scores, v) + dot_nt((q * whole * enter).astype(BF16), old.astype(BF16))
            ending = (k * to_final * tail).astype(BF16)
            state[h] = old * (jnp.exp(final) * kept) + dot_tn(v, ending)
            mixed_ref[rows, cols] = mixed
            scale = lax.rsqrt(jnp.mean(mixed * mixed, axis=-1, keepdims=True) + EPS_GROUP)
            pre_g = part(3)
            gate = pre_g * sigmoid_pair(pre_g)[0]
            gated_ref[rows, cols] = (mixed * scale * gain_ref[:, cols] * gate).astype(BF16)


def mixer_forward(pre, bias, bound, gain, split, order):
    tokens, wide = pre.shape
    width = wide // 4
    heads = width // HEAD
    steps = order.shape[0]
    block = tokens // steps
    chunks = block // CHUNK
    row = pl.BlockSpec((1, width), lambda i, order: (0, 0))
    grid_spec = pltpu.PrefetchScalarGridSpec(
        num_scalar_prefetch=1,
        grid=(steps,),
        in_specs=[
            pl.BlockSpec(memory_space=pltpu.SMEM),
            pl.BlockSpec((block, wide), lambda i, order: (order[i], 0)),
            row,
            row,
            row,
        ],
        out_specs=[
            pl.BlockSpec((block, width), lambda i, order: (order[i], 0)),
            pl.BlockSpec((block, width), lambda i, order: (i, 0)),
            pl.BlockSpec((chunks, heads, HEAD, HEAD), lambda i, order: (i, 0, 0, 0)),
        ],
        scratch_shapes=[pltpu.VMEM((heads, HEAD, HEAD), F32)],
    )
    return pl.pallas_call(
        functools.partial(forward_kernel, heads, chunks),
        grid_spec=grid_spec,
        out_shape=[
            jax.ShapeDtypeStruct((tokens, width), BF16),
            jax.ShapeDtypeStruct((tokens, width), F32),
            jax.ShapeDtypeStruct((tokens // CHUNK, heads, HEAD, HEAD), F32),
        ],
        compiler_params=pltpu.CompilerParams(
            dimension_semantics=("arbitrary",), vmem_limit_bytes=VMEM
        ),
        cost_estimate=cost(tokens * width * 14000),
        name="mixer_forward",
    )(order, split, pre, bias[None], bound[None], gain[None])


def backward_kernel(
    heads,
    chunks,
    order_ref,
    split_ref,
    pre_ref,
    mixed_ref,
    grad_ref,
    states_ref,
    bias_ref,
    bound_ref,
    gain_ref,
    out_ref,
    sums_ref,
    adjoint,
    later,
):
    step = pl.program_id(0)
    steps = pl.num_programs(0)
    width = heads * HEAD
    count = CHUNK // SUB

    @pl.when(step == 0)
    def _():
        adjoint[...] = jnp.zeros_like(adjoint)
        later[...] = jnp.zeros_like(later)
        sums_ref[...] = jnp.zeros_like(sums_ref)

    split = split_ref[0]
    tri = triangle(False)
    tri_up = triangle(True)
    for n in reversed(range(chunks)):
        start = ((steps - 1 - step) * chunks + n) * CHUNK
        allowed, enter, tail, kept = chunk_masks(start, split)
        rows = slice(n * CHUNK, (n + 1) * CHUNK)
        for h in range(heads):
            cols = slice(h * HEAD, (h + 1) * HEAD)

            def part(which):
                return pre_ref[rows, which * width + h * HEAD : which * width + (h + 1) * HEAD]

            def store(which, value):
                out_ref[rows, which * width + h * HEAD : which * width + (h + 1) * HEAD] = value.astype(BF16)

            pre_q = part(0)
            sig_q, sig_nq = sigmoid_pair(pre_q)
            q = pre_q * sig_q
            bound = bound_ref[:, cols]
            plus, minus = sigmoid_pair(part(1) + bias_ref[:, cols])
            k = (1.0 - bound) * minus
            forget = bound + (1.0 - bound) * plus
            _, mids, ends, to_mid, from_mid, to_end, whole, final, to_final, qd, keys = chunk_common(
                q, k, jnp.log(forget), tri
            )
            v = part(2).astype(BF16)

            mixed = mixed_ref[rows, cols]
            grad = grad_ref[rows, cols].astype(F32)
            gain = gain_ref[:, cols]
            scale = lax.rsqrt(jnp.mean(mixed * mixed, axis=-1, keepdims=True) + EPS_GROUP)
            pre_g = part(3)
            sig_g, sig_ng = sigmoid_pair(pre_g)
            gate = pre_g * sig_g
            unit = mixed * scale
            u = grad * gain * gate
            moment = jnp.mean(u * unit, axis=-1, keepdims=True)
            mixed_grad = scale * (u - unit * moment)
            gu = grad * unit
            gain_sum = jnp.sum(gu * gate, axis=0, keepdims=True)
            store(3, gu * gain * (sig_g * (1.0 + pre_g * sig_ng)))

            do = mixed_grad.astype(BF16)
            old = states_ref[n, h]
            lam = adjoint[h]
            old_low = old.astype(BF16)
            lam_low = lam.astype(BF16)
            scores = jnp.where(allowed, scores_of(qd, keys), 0.0).astype(BF16)
            pair = jnp.where(allowed, dot_nt(do, v), 0.0).astype(BF16)
            reach = whole * enter
            remain = to_final * tail
            ending = (k * remain).astype(BF16)
            store(2, dot_tn(scores, do) + dot_nt(ending, lam_low))

            q_rows = []
            k_rows = [None] * count
            for i in range(count):
                pair_i = pair[i * SUB : (i + 1) * SUB]
                q_rows.append(dot_nn(pair_i, keys[i]))
                back = dot_tn(pair_i, qd[i * SUB : (i + 1) * SUB])
                for j in range(i + 1):
                    piece = back[j * SUB : (j + 1) * SUB]
                    if j == i:
                        piece = piece * from_mid[j * SUB : (j + 1) * SUB]
                        k_rows[j] = (k_rows[j], piece)
                    else:
                        piece = piece * jnp.exp(mids[i] - ends[j])
                        first = k_rows[j]
                        k_rows[j] = piece if first is None else first + piece
                diagonal = k_rows[i][1]
                k_rows[i] = None
                if i == 0:
                    diagonals = []
                diagonals.append(diagonal)
            k_intra = []
            for j in range(count):
                piece = diagonals[j]
                if k_rows[j] is not None:
                    piece = piece + k_rows[j] * to_end[j * SUB : (j + 1) * SUB]
                k_intra.append(piece)
            dq = jnp.concatenate(q_rows, axis=0) * to_mid + dot_nn(do, old_low) * reach
            dk = jnp.concatenate(k_intra, axis=0) + dot_nn(v, lam_low) * remain
            anchor = jnp.sum(lam * later[h], axis=0, keepdims=True)
            dlog = tri_dot(tri_up, q * dq - k * dk) + anchor
            adjoint[h] = lam * (jnp.exp(final) * kept) + dot_tn(do, (q * reach).astype(BF16))
            later[h] = old

            store(0, dq * (sig_q * (1.0 + pre_q * sig_nq)))
            drive = minus * (dlog / forget - dk)
            forget_grad = (1.0 - bound) * plus * drive
            store(1, forget_grad)
            sums_ref[0:1, cols] += gain_sum
            sums_ref[1:2, cols] += jnp.sum(forget_grad, axis=0, keepdims=True)
            sums_ref[2:3, cols] += jnp.sum(drive, axis=0, keepdims=True)


def mixer_backward(pre, mixed, grad, states, bias, bound, gain, split, order):
    tokens, wide = pre.shape
    width = wide // 4
    heads = width // HEAD
    steps = order.shape[0]
    block = tokens // steps
    chunks = block // CHUNK
    row = pl.BlockSpec((1, width), lambda i, order: (0, 0))
    placed = lambda i, order: (order[steps - 1 - i], 0)
    grid_spec = pltpu.PrefetchScalarGridSpec(
        num_scalar_prefetch=1,
        grid=(steps,),
        in_specs=[
            pl.BlockSpec(memory_space=pltpu.SMEM),
            pl.BlockSpec((block, wide), placed),
            pl.BlockSpec((block, width), lambda i, order: (steps - 1 - i, 0)),
            pl.BlockSpec((block, width), placed),
            pl.BlockSpec((chunks, heads, HEAD, HEAD), lambda i, order: (steps - 1 - i, 0, 0, 0)),
            row,
            row,
            row,
        ],
        out_specs=[
            pl.BlockSpec((block, wide), placed),
            pl.BlockSpec((8, width), lambda i, order: (0, 0)),
        ],
        scratch_shapes=[pltpu.VMEM((heads, HEAD, HEAD), F32), pltpu.VMEM((heads, HEAD, HEAD), F32)],
    )
    return pl.pallas_call(
        functools.partial(backward_kernel, heads, chunks),
        grid_spec=grid_spec,
        out_shape=[
            jax.ShapeDtypeStruct((tokens, wide), BF16),
            jax.ShapeDtypeStruct((8, width), F32),
        ],
        compiler_params=pltpu.CompilerParams(
            dimension_semantics=("arbitrary",), vmem_limit_bytes=VMEM
        ),
        cost_estimate=cost(tokens * width * 22000),
        name="mixer_backward",
    )(order, split, pre, mixed, grad, states, bias[None], bound[None], gain[None])


def blocks_of(array, count):
    size = array.shape[0] // count
    return [array[m * size : (m + 1) * size] for m in range(count)]


def product_kernel(dims, parts, a_ref, b_ref, *refs):
    dot = lax.dot_general(a_ref[...], b_ref[...], (dims, ((), ())), preferred_element_type=F32)
    for block, out_ref in zip(blocks_of(dot, parts), refs[len(refs) - parts :]):
        out_ref[...] = block.astype(out_ref.dtype)


NN = ((1,), (0,))
NT = ((1,), (1,))
TN = ((0,), (0,))


def product(a, b, dims, kind, rows=None, cols=None, a_half=None, b_half=None, parts=1, wait=()):
    count = a.shape[1 - dims[0][0]] if a_half is None else a.shape[0] // 2
    depth = a.shape[dims[0][0]]
    wide = b.shape[1 - dims[1][0]] // (1 if b_half is None else 2)
    tile_rows = rows or count
    tile_cols = cols or wide
    by_rows = rows is not None
    shift = (a_half or 0) * (count // tile_rows)

    def at_row(i):
        return (i if by_rows else 0) + shift

    def at_col(i):
        return 0 if by_rows else i

    b_shift = (b_half or 0) * (wide // tile_cols)

    if dims[0][0] == 1:
        a_spec = pl.BlockSpec((tile_rows, depth), lambda i: (at_row(i), 0))
    else:
        a_spec = pl.BlockSpec((depth, tile_rows), lambda i: (0, at_row(i)))
    if dims[1][0] == 0:
        b_spec = pl.BlockSpec((depth, tile_cols), lambda i: (0, at_col(i) + b_shift))
    else:
        b_spec = pl.BlockSpec((tile_cols, depth), lambda i: (at_col(i) + b_shift, 0))
    out_spec = pl.BlockSpec((tile_rows // parts, tile_cols), lambda i: (at_row(i) - shift, at_col(i)))
    out = pl.pallas_call(
        functools.partial(product_kernel, dims, parts),
        grid=(count // tile_rows * (wide // tile_cols),),
        in_specs=[a_spec, b_spec] + [UNREAD] * len(wait),
        out_specs=[out_spec] * parts,
        out_shape=[jax.ShapeDtypeStruct((count // parts, wide), kind)] * parts,
        compiler_params=pltpu.CompilerParams(
            dimension_semantics=("arbitrary",), vmem_limit_bytes=VMEM
        ),
        cost_estimate=cost(2 * count * wide * depth),
        name="product",
    )(a, b, *wait)
    return out[0] if parts == 1 else out


def gate_kernel(low_ref, weight_ref, pre_ref, hidden_ref):
    half = hidden_ref.shape[1]
    pre = dot_nn(low_ref[...], weight_ref[...])
    pre_ref[...] = pre
    gate = pre[:, :half]
    hidden_ref[...] = (gate * sigmoid_pair(gate)[0] * pre[:, half:]).astype(BF16)


def gate_product(low, weight, rows=256):
    count, depth = low.shape
    wide = weight.shape[1]
    return pl.pallas_call(
        gate_kernel,
        grid=(count // rows,),
        in_specs=[
            pl.BlockSpec((rows, depth), lambda i: (i, 0)),
            pl.BlockSpec((depth, wide), lambda i: (0, 0)),
        ],
        out_specs=[
            pl.BlockSpec((rows, wide), lambda i: (i, 0)),
            pl.BlockSpec((rows, wide // 2), lambda i: (i, 0)),
        ],
        out_shape=[
            jax.ShapeDtypeStruct((count, wide), F32),
            jax.ShapeDtypeStruct((count, wide // 2), BF16),
        ],
        compiler_params=pltpu.CompilerParams(
            dimension_semantics=("arbitrary",), vmem_limit_bytes=VMEM
        ),
        cost_estimate=cost(2 * count * depth * wide),
        name="gate_product",
    )(low, weight)


def hidden_back_kernel(grad_ref, weight_ref, pre_ref, out_ref):
    half = out_ref.shape[1] // 2
    grad = dot_nt(grad_ref[...], weight_ref[...])
    gate, up = pre_ref[:, :half], pre_ref[:, half:]
    sig, rest = sigmoid_pair(gate)
    out_ref[:, :half] = (grad * up * sig * (1.0 + gate * rest)).astype(BF16)
    out_ref[:, half:] = (grad * (gate * sig)).astype(BF16)


def hidden_back(grad, weight, pre, rows=256, wait=()):
    count, depth = grad.shape
    wide = pre.shape[1]
    return pl.pallas_call(
        lambda *refs: hidden_back_kernel(*refs[:3], refs[-1]),
        grid=(count // rows,),
        in_specs=[
            pl.BlockSpec((rows, depth), lambda i: (i, 0)),
            pl.BlockSpec(weight.shape, lambda i: (0, 0)),
            pl.BlockSpec((rows, wide), lambda i: (i, 0)),
        ]
        + [UNREAD] * len(wait),
        out_specs=pl.BlockSpec((rows, wide), lambda i: (i, 0)),
        out_shape=jax.ShapeDtypeStruct((count, wide), BF16),
        compiler_params=pltpu.CompilerParams(
            dimension_semantics=("arbitrary",), vmem_limit_bytes=VMEM
        ),
        cost_estimate=cost(count * depth * wide),
        name="hidden_back",
    )(grad, weight, pre, *wait)


def weight_sum_kernel(own_ref, other_ref, b_ref, weight_ref, right_ref, *refs):
    out_ref, sum_ref = refs[-2:]
    half = own_ref.shape[0]
    wide = b_ref.shape[1]
    dot = dot_tn(own_ref[...], b_ref[:half]) + dot_tn(other_ref[...], b_ref[half:])
    out_ref[:, :wide] = dot.astype(out_ref.dtype)
    total = jnp.sum(dot * weight_ref[...].astype(F32), axis=1, keepdims=True)
    sum_ref[...] = jnp.broadcast_to(total, sum_ref.shape)
    start = 0
    more = None
    for ref in refs[:-2]:
        size = ref.shape[0]
        if start < right_ref.shape[0]:
            term = dot_tn(ref[...], right_ref[start : start + size])
            more = term if more is None else more + term
            start += size
    out_ref[:, wide:] = more.astype(out_ref.dtype)


def weight_sum_product(own, other, b, weight, blocks, right, rows=256, wait=()):
    half, count = own.shape
    depth, wide = b.shape
    extra = right.shape[1]
    a_spec = pl.BlockSpec((half, rows), lambda i: (0, i))
    out, total = pl.pallas_call(
        weight_sum_kernel,
        grid=(count // rows,),
        in_specs=[
            a_spec,
            a_spec,
            pl.BlockSpec((depth, wide), lambda i: (0, 0)),
            pl.BlockSpec((rows, wide), lambda i: (i, 0)),
            pl.BlockSpec((depth, extra), lambda i: (0, 0)),
        ]
        + [pl.BlockSpec((block.shape[0], rows), lambda i: (0, i)) for block in blocks]
        + [UNREAD] * len(wait),
        out_specs=[
            pl.BlockSpec((rows, wide + extra), lambda i: (i, 0)),
            pl.BlockSpec((rows, HEAD), lambda i: (i, 0)),
        ],
        out_shape=[
            jax.ShapeDtypeStruct((count, wide + extra), BF16),
            jax.ShapeDtypeStruct((count, HEAD), F32),
        ],
        compiler_params=pltpu.CompilerParams(
            dimension_semantics=("arbitrary",), vmem_limit_bytes=VMEM
        ),
        cost_estimate=cost(2 * count * (wide + extra) * depth),
        name="weight_sum_product",
    )(own, other, b, weight, right, *blocks, *wait)
    return out, total[:, 0]


def early_product_kernel(b_ref, *refs):
    out_ref = refs[-1]
    size = refs[0].shape[0]
    for ref, block in zip(refs[:-1], (0, 1, 2, 4, 5, 6)):
        out_ref[block * size : (block + 1) * size] = dot_nt(ref[...], b_ref[...])


def late_product_kernel(b_ref, early_ref, *refs):
    out_ref = refs[-1]
    for step in range(2):

        @pl.when(pl.program_id(0) == step)
        def _(step=step):
            half = refs[0].shape[0]
            out_ref[:half] = dot_nt(refs[2 * step][...], b_ref[...])
            out_ref[half:] = dot_nt(refs[2 * step + 1][...], b_ref[...])


def early_product(blocks, b):
    size = blocks[0].shape[0]
    return pl.pallas_call(
        early_product_kernel,
        out_shape=jax.ShapeDtypeStruct((8 * size, b.shape[0]), F32),
        compiler_params=pltpu.CompilerParams(vmem_limit_bytes=VMEM),
        cost_estimate=cost(2 * 6 * size * b.size),
        name="early_product",
    )(b, *blocks)


def late_product(out, late, b):
    size = 2 * late[0].shape[0]
    width = b.shape[0]
    whole = [pl.BlockSpec(part.shape, lambda i: (0, 0)) for part in late]
    return pl.pallas_call(
        late_product_kernel,
        grid=(2,),
        in_specs=[pl.BlockSpec(b.shape, lambda i: (0, 0)), UNREAD] + whole,
        out_specs=pl.BlockSpec((size, width), lambda i: (4 * i + 3, 0)),
        out_shape=jax.ShapeDtypeStruct(out.shape, F32),
        input_output_aliases={1: 0},
        compiler_params=pltpu.CompilerParams(vmem_limit_bytes=VMEM),
        cost_estimate=cost(2 * 2 * size * b.size),
        name="late_product",
    )(b, out, *late)


def joined_columns_kernel(width, at_ref, own_ref, other_ref, *out_refs):
    def store(ref):
        for which in range(4):
            out_refs[which][...] = ref[:, which * width : (which + 1) * width].astype(F32)
        out_refs[4][...] = ref[:, 4 * width :].astype(F32).T

    mine = pl.program_id(0) == at_ref[0]
    pl.when(mine)(lambda: store(own_ref))
    pl.when(jnp.logical_not(mine))(lambda: store(other_ref))


def joined_columns(own, other, at, width):
    rows = own.shape[0]
    whole = pl.BlockSpec(own.shape, lambda i, at: (0, 0))
    beside = pl.BlockSpec((rows, width), lambda i, at: (0, i))
    return pl.pallas_call(
        functools.partial(joined_columns_kernel, width),
        grid_spec=pltpu.PrefetchScalarGridSpec(
            num_scalar_prefetch=1,
            grid=(2,),
            in_specs=[whole, whole],
            out_specs=[beside] * 4 + [pl.BlockSpec((width, rows), lambda i, at: (i, 0))],
        ),
        out_shape=[jax.ShapeDtypeStruct((rows, 2 * width), F32)] * 4
        + [jax.ShapeDtypeStruct((2 * width, rows), F32)],
        compiler_params=pltpu.CompilerParams(
            dimension_semantics=("arbitrary",), vmem_limit_bytes=VMEM
        ),
        cost_estimate=cost(1 << 20),
        name="joined_columns",
    )(at.astype(jnp.int32).reshape(1), own, other)


def rms_rows(rows_in):
    return lax.rsqrt(jnp.mean(rows_in * rows_in, axis=-1, keepdims=True) + EPS_NORM)


def norm_back(grad, rows_in, gain_vec):
    inv = rms_rows(rows_in)
    u = grad * gain_vec
    moment = jnp.mean(u * rows_in, axis=-1, keepdims=True)
    return inv * u - rows_in * (inv * inv * inv * moment), jnp.sum(grad * rows_in * inv, axis=0)


def gather(part, axes, dim):
    return lax.all_gather(part, axes, axis=dim, tiled=True)


def gather_columns(part, axis):
    count, at = lax.axis_size(axis), lax.axis_index(axis)
    if count > 4:
        return gather(part, axis, 1)
    size = part.shape[1]
    out = jnp.zeros((part.shape[0], count * size), part.dtype)
    for m in range(count):
        block = part if m == 0 else lax.ppermute(part, axis, [(i, i ^ m) for i in range(count)])
        out = lax.dynamic_update_slice_in_dim(out, block, (at ^ m) * size, 1)
    return out


def scatter(whole, axes, dim):
    return lax.psum_scatter(whole, axes, scatter_dimension=dim, tiled=True)


def matmul(left_side, right_side):
    return jnp.dot(left_side, right_side, preferred_element_type=F32)


def after(value, *others):
    return lax.optimization_barrier((value, *others))[0]


def small_sum(part, axis):
    count = lax.axis_size(axis)
    if count <= 4:
        got = [lax.ppermute(part, axis, [(i, i ^ m) for i in range(count)]) for m in range(1, count)]
        return sum(got, part)
    mask = 1
    while mask < count:
        part = part + lax.ppermute(part, axis, [(i, i ^ mask) for i in range(count)])
        mask *= 2
    return part


def together(*values):
    return lax.optimization_barrier(values)


def swap(part):
    return lax.ppermute(part, "ctx", [(0, 1), (1, 0)])


def in_order(own, dim):
    other = swap(own)
    first = lax.axis_index("ctx") == 0
    return jnp.concatenate([jnp.where(first, own, other), jnp.where(first, other, own)], axis=dim)


def partner(part, mask):
    return lax.ppermute(part, "tp", [(i, i ^ mask) for i in range(lax.axis_size("tp"))])


def relative(array, count, at):
    size = array.shape[0] // count
    return jnp.concatenate(
        [lax.dynamic_slice_in_dim(array, (at ^ m) * size, size, 0) for m in range(count)], axis=0
    )


def parts_of(blocks):
    half = blocks[0].shape[0] // 2
    low, high = [block[:half] for block in blocks], [block[half:] for block in blocks]
    near = jnp.concatenate([low[1], low[3]], axis=0)
    far = jnp.concatenate([high[2], high[3]], axis=0)
    return [near, far, blocks[0], low[2], high[1]]


def sum_first(parts):
    return partner(parts[0], 1), partner(parts[1], 2)


def sum_second(parts, near, far):
    half = near.shape[0] // 2
    near, far = together(near, far)
    pass_far = (parts[3].astype(F32) + near[half:].astype(F32)).astype(BF16)
    pass_near = (parts[4].astype(F32) + far[half:].astype(F32)).astype(BF16)
    pass_far, pass_near = together(pass_far, pass_near)
    return together(partner(pass_far, 2), partner(pass_near, 1))


def sum_total(parts, first, second):
    half = second[0].shape[0]
    halves = [
        parts[2][which * half : (which + 1) * half].astype(F32)
        + first[which][:half].astype(F32)
        + second[which].astype(F32)
        for which in (0, 1)
    ]
    return jnp.concatenate(halves, axis=0)


def gather_first(own):
    return partner(own, 1), partner(own, 2)


def gather_second(near, far):
    half = near.shape[0] // 2
    return partner(far[:half], 1), partner(near[half:], 2)


def gathered_parts(own, first, second):
    near, far = first
    half = second[0].shape[0]
    return [near[:half], second[0], far[half:], second[1], own, far[:half], near[half:]]


def placed_kernel(at_ref, own_ref, near_ref, far_ref, top_ref, bottom_ref, *refs):
    out_ref = refs[-1]
    step = pl.program_id(0)
    half = top_ref.shape[0]
    for which, ref in enumerate((own_ref, near_ref, far_ref)):

        @pl.when(step == which)
        def _(ref=ref):
            out_ref[...] = ref[...].astype(out_ref.dtype)

    @pl.when(step == 3)
    def _():
        out_ref[:half] = top_ref[...].astype(out_ref.dtype)
        out_ref[half:] = bottom_ref[...].astype(out_ref.dtype)


def placed_blocks(own, near, far, top, bottom, at, kind, wait=()):
    size, width = own.shape
    inputs = [own, near, far, top, bottom]
    return pl.pallas_call(
        placed_kernel,
        grid_spec=pltpu.PrefetchScalarGridSpec(
            num_scalar_prefetch=1,
            grid=(4,),
            in_specs=[pl.BlockSpec(part.shape, lambda i, at: (0, 0)) for part in inputs] + [UNREAD] * len(wait),
            out_specs=pl.BlockSpec((size, width), lambda i, at: (i ^ at[0], 0)),
        ),
        out_shape=jax.ShapeDtypeStruct((4 * size, width), kind),
        compiler_params=pltpu.CompilerParams(
            dimension_semantics=("arbitrary",), vmem_limit_bytes=VMEM
        ),
        cost_estimate=cost(3 << 30),
        name="placed_blocks",
    )(at.astype(jnp.int32).reshape(1), *inputs, *wait)


def body(
    block_in,
    query_proj,
    forget_proj,
    value_proj,
    outgate_proj,
    out_proj,
    ffn_gate,
    ffn_up,
    ffn_down,
    first_gain,
    second_gain,
    group_gain,
    forget_bias,
    bound_table,
    layer_index,
    second_start,
    cotangent,
):
    ctx_count, ctx_at = lax.axis_size("ctx"), lax.axis_index("ctx")
    tp_count, tp_at = lax.axis_size("tp"), lax.axis_index("tp")
    row_count, model = block_in.shape
    local_width = query_proj.shape[1]
    width = local_width // ctx_count
    hidden_width = ffn_gate.shape[1]
    shard_rows = row_count // tp_count

    def own_half(array, dim):
        size = array.shape[dim] // ctx_count
        return lax.dynamic_slice_in_dim(array, ctx_at * size, size, dim)

    blocks = ctx_count * tp_count
    order = lax.iota(jnp.int32, blocks) ^ (ctx_at * tp_count + tp_at)

    mix_full = gather(
        jnp.concatenate(
            [own_half(w, 1) for w in (query_proj, forget_proj, value_proj, outgate_proj)], axis=1
        ),
        "dp",
        0,
    )
    out_full = gather_columns(own_half(out_proj, 0), "dp")
    ffn_full = gather(own_half(jnp.concatenate([ffn_gate, ffn_up], axis=1), 0), ("dp", "ctx"), 0)
    down_full = gather(own_half(ffn_down, 1), ("dp", "ctx"), 1)

    inputs = relative(block_in, tp_count, tp_at).astype(F32)
    first_low = (inputs * rms_rows(inputs) * first_gain).astype(BF16)
    first_swapped = swap(first_low)
    first_all = jnp.concatenate([first_low, first_swapped], axis=0)
    table = own_half(bound_table, 1)
    weights = jax.nn.softmax(table, axis=0)
    rows = lax.broadcasted_iota(jnp.int32, (table.shape[0], 1), 0)
    counted = jnp.where((rows >= 1) & (rows <= layer_index[0]), 1.0, 0.0)
    bound = jnp.sum(weights * counted, axis=0)
    bias = own_half(forget_bias, 0)
    gain = own_half(group_gain, 0)
    pre = product(first_all, mix_full, NN, F32, rows=512)
    gated, mixed, states = mixer_forward(pre, bias, bound, gain, second_start, order)
    inputs_own = inputs[:shard_rows]
    out_other = [
        swap(block) for block in product(gated, out_full, NN, BF16, cols=512, a_half=1, parts=tp_count)
    ]
    out_own = product(gated, out_full, NN, BF16, cols=512, a_half=0, parts=tp_count)
    out_part = parts_of([(a.astype(F32) + b.astype(F32)).astype(BF16) for a, b in zip(out_own, out_other)])
    first = sum_first(out_part)
    second = sum_second(out_part, *first)
    resid = inputs_own + sum_total(out_part, first, second)

    second_own = (resid * rms_rows(resid) * second_gain).astype(BF16)
    first = gather_first(second_own)
    second_low = jnp.concatenate(
        gathered_parts(second_own, first, gather_second(*first)), axis=0
    )
    cotangent_blocks = blocks_of(relative(cotangent, tp_count, tp_at), tp_count)
    cotangent_rel = jnp.concatenate(parts_of(cotangent_blocks), axis=0)
    gate_up, hidden = gate_product(second_low, ffn_full)

    down_grad = product(hidden, cotangent_rel, TN, BF16, cols=512)
    down_sum = scatter(down_grad, ("dp", "ctx"), 1)
    gate_up_grad = hidden_back(cotangent_rel, down_full, gate_up, wait=[down_grad])
    second_sent = product(gate_up_grad, ffn_full, NT, BF16, cols=512, a_half=0, parts=2)
    first = sum_first(second_sent)
    second_kept = product(gate_up_grad, ffn_full, NT, BF16, cols=512, a_half=1, wait=second_sent)
    half_rows = shard_rows // 2
    second_part = [
        *second_sent,
        second_kept[:shard_rows],
        second_kept[shard_rows : shard_rows + half_rows],
        second_kept[shard_rows + half_rows :],
    ]
    ffn_rows = product(hidden, down_full, NN, BF16, cols=256, parts=tp_count, wait=[second_kept])
    gate_weight_grad = product(second_low, gate_up_grad, TN, BF16, rows=256, b_half=0)
    gate_sum = scatter(after(gate_weight_grad, second_kept, *first), ("dp", "ctx"), 0)
    second = sum_second(second_part, *first)
    second_total = sum_total(second_part, first, second)
    resid_part, second_gain_grad = norm_back(
        after(second_total, down_sum, ffn_rows[0]), resid, second_gain
    )
    resid_grad = cotangent_blocks[0].astype(F32) + resid_part
    resid_own = resid_grad.astype(BF16)
    first = gather_first(resid_own)
    up_weight_grad = product(second_low, gate_up_grad, TN, BF16, rows=256, b_half=1)
    up_sum = scatter(after(up_weight_grad, *first), ("dp", "ctx"), 0)
    resid_second = gather_second(*first)
    resid_early = [resid_own, *first]
    resid_early = resid_early + [swap(block) for block in resid_early]
    early_grad = early_product(resid_early, out_full)
    resid_late = [*resid_second, *[swap(after(block, early_grad)) for block in resid_second]]
    resid_blocks = [*resid_early[:3], *resid_late[:2], *resid_early[3:], *resid_late[2:]]

    ffn_rows = [after(part, *resid_second) for part in ffn_rows]
    ffn_part = [*ffn_rows[:3], ffn_rows[3][:half_rows], ffn_rows[3][half_rows:]]
    ffn_first = sum_first(ffn_part)
    gated_grad = late_product(early_grad, resid_late, out_full)
    proj_grad, sums = mixer_backward(pre, mixed, gated_grad, states, bias, bound, gain, second_start, order)
    first_other = product(proj_grad, mix_full, NT, BF16, cols=256, a_half=1, parts=tp_count, wait=ffn_first)
    ffn_second = sum_second([after(block, proj_grad) for block in ffn_part], *ffn_first)
    block_own = (resid + sum_total(ffn_part, ffn_first, ffn_second)).astype(BF16)
    first_own = product(
        proj_grad, mix_full, NT, BF16, cols=256, a_half=0, parts=tp_count, wait=[first_other[0], block_own]
    )
    block_first = gather_first(block_own)
    first_part = [
        (own.astype(F32) + swap(other).astype(F32)).astype(BF16)
        for own, other in zip(first_own, first_other)
    ]
    first_part = parts_of(first_part)
    first = sum_first(first_part)
    mix_grad, first_sum = weight_sum_product(
        first_low, first_swapped, proj_grad, mix_full, resid_blocks, gated, wait=block_first
    )
    mix_sum = scatter(after(mix_grad, gate_sum, up_sum, *first), "dp", 0)
    final_first = first
    second = sum_second(first_part, *first)
    input_part, _ = norm_back(sum_total(first_part, first, second), inputs_own, first_gain)
    input_own = (resid_grad + input_part).astype(BF16)
    block_second = gather_second(*[after(block, *second) for block in block_first])
    input_own = after(input_own, *block_second)
    first = gather_first(input_own)

    gains = jnp.concatenate([first_sum / first_gain, second_gain_grad]).reshape(-1, HEAD)
    gains = gains + swap(gains)
    block_out = placed_blocks(block_own, *block_first, *block_second, tp_at, BF16, wait=[gains])
    gains = small_sum(gains, "tp")
    input_second = gather_second(*[after(block, block_out) for block in first])
    small = small_sum(jnp.concatenate([sums[:3].reshape(-1, HEAD), gains]), "dp")
    input_grad = placed_blocks(input_own, *first, *input_second, tp_at, F32, wait=[gains])
    cut = 3 * width // HEAD
    head_sums = in_order(small[:cut].reshape(3, width), 1)
    gain_sums = small[cut:].reshape(-1)
    all_weights = jax.nn.softmax(bound_table, axis=0)
    all_bound = jnp.sum(all_weights * counted, axis=0)
    table_grad = all_weights * (counted - all_bound) * head_sums[2]

    *mix_shards, out_shard = joined_columns(mix_sum, after(swap(mix_sum), small), ctx_at, width)

    return (
        block_out,
        input_grad,
        *mix_shards,
        out_shard,
        in_order(after(gate_sum, *final_first), 0).astype(F32),
        in_order(after(up_sum, *final_first), 0).astype(F32),
        in_order(after(down_sum, *final_first), 1).astype(F32),
        gain_sums[:model],
        gain_sums[model:],
        head_sums[0],
        head_sums[1],
        table_grad,
    )


def solution(mesh):
    return jax.shard_map(
        body,
        mesh=mesh,
        in_specs=(
            P(("dp", "ctx"), None),
            P("dp", "tp"),
            P("dp", "tp"),
            P("dp", "tp"),
            P("dp", "tp"),
            P("tp", "dp"),
            P("dp", "tp"),
            P("dp", "tp"),
            P("tp", "dp"),
            P(),
            P(),
            P("tp"),
            P("tp"),
            P(None, "tp"),
            P(),
            P("dp"),
            P(("dp", "ctx"), None),
        ),
        out_specs=(
            P(("dp", "ctx"), None),
            P(("dp", "ctx"), None),
            P("dp", "tp"),
            P("dp", "tp"),
            P("dp", "tp"),
            P("dp", "tp"),
            P("tp", "dp"),
            P("dp", "tp"),
            P("dp", "tp"),
            P("tp", "dp"),
            P(),
            P(),
            P("tp"),
            P("tp"),
            P(None, "tp"),
        ),
        check_vma=False,
    )
```

```python
import functools

import jax
import jax.numpy as jnp
from jax import lax
from jax.experimental import pallas as pl
from jax.experimental.pallas import tpu as pltpu
from jax.sharding import PartitionSpec as P

HEAD = 128
SUB = 32
CHUNK = 128
EPS_NORM = 1e-06
EPS_GROUP = 1e-05
F32 = jnp.float32
VMEM = 58 << 20
UNREAD = pl.BlockSpec(memory_space=pl.ANY)
BF16 = jnp.bfloat16


def cost(flops):
    return pl.CostEstimate(flops=2 * flops, bytes_accessed=1 << 20, transcendentals=0)


def dot_nn(a, b):
    return lax.dot_general(a, b, (((1,), (0,)), ((), ())), preferred_element_type=F32)


def dot_nt(a, b):
    return lax.dot_general(a, b, (((1,), (1,)), ((), ())), preferred_element_type=F32)


def dot_tn(a, b):
    return lax.dot_general(a, b, (((0,), (0,)), ((), ())), preferred_element_type=F32)


def sigmoid_pair(x):
    small = jnp.exp(-jnp.abs(x))
    inv = 1.0 / (1.0 + small)
    rest = small * inv
    up = x >= 0.0
    return jnp.where(up, inv, rest), jnp.where(up, rest, inv)


def tri_dot(tri, x):
    high = x.astype(BF16)
    low = (x - high.astype(F32)).astype(BF16)
    return dot_nn(tri, high) + dot_nn(tri, low)


def triangle(upper):
    rows = lax.broadcasted_iota(jnp.int32, (CHUNK, CHUNK), 0)
    cols = lax.broadcasted_iota(jnp.int32, (CHUNK, CHUNK), 1)
    keep = rows <= cols if upper else rows >= cols
    return jnp.where(keep, 1.0, 0.0).astype(BF16)


def chunk_masks(start, split):
    rows = lax.broadcasted_iota(jnp.int32, (CHUNK, CHUNK), 0)
    cols = lax.broadcasted_iota(jnp.int32, (CHUNK, CHUNK), 1)
    local = split - start
    causal = rows >= cols
    same = (rows >= local) == (cols >= local)
    token = lax.broadcasted_iota(jnp.int32, (CHUNK, HEAD), 0)
    before = start > split
    enter = jnp.where(jnp.logical_or(token < local, before), 1.0, 0.0)
    last = CHUNK - 1 >= local
    tail = jnp.where((token >= local) == last, 1.0, 0.0)
    kept = jnp.where(jnp.logical_or(jnp.logical_not(last), before), 1.0, 0.0)
    return causal & same, enter, tail, kept


def key_rows(k, b, kd, k_end_sub, mids, ends):
    out = []
    count = CHUNK // SUB
    for i in range(count):
        parts = []
        for j in range(i):
            part = k_end_sub[j * SUB : (j + 1) * SUB]
            parts.append(part * jnp.exp(mids[i] - ends[j]))
        parts.append(kd[i * SUB : (i + 1) * SUB])
        if i < count - 1:
            parts.append(jnp.zeros(((count - 1 - i) * SUB, HEAD), F32))
        out.append(jnp.concatenate(parts, axis=0).astype(BF16))
    return out


def spread(rows_list):
    return jnp.concatenate([jnp.broadcast_to(r, (SUB, HEAD)) for r in rows_list], axis=0)


def chunk_common(q, k, log_forget, tri):
    count = CHUNK // SUB
    b = tri_dot(tri, log_forget)
    mids = [b[i * SUB + SUB // 2 : i * SUB + SUB // 2 + 1] for i in range(count)]
    ends = [b[(i + 1) * SUB - 1 : (i + 1) * SUB] for i in range(count)]
    mid = spread(mids)
    end = spread(ends)
    to_mid = jnp.exp(b - mid)
    from_mid = jnp.exp(mid - b)
    to_end = jnp.exp(end - b)
    whole = jnp.exp(b)
    final = ends[-1]
    to_final = jnp.exp(final - b)
    qd = (q * to_mid).astype(BF16)
    keys = key_rows(k, b, k * from_mid, k * to_end, mids, ends)
    return b, mids, ends, to_mid, from_mid, to_end, whole, final, to_final, qd, keys


def scores_of(qd, keys):
    count = CHUNK // SUB
    return jnp.concatenate(
        [dot_nt(qd[i * SUB : (i + 1) * SUB], keys[i]) for i in range(count)], axis=0
    )


def forward_kernel(
    heads,
    chunks,
    order_ref,
    split_ref,
    pre_ref,
    bias_ref,
    bound_ref,
    gain_ref,
    gated_ref,
    mixed_ref,
    states_ref,
    state,
):
    step = pl.program_id(0)
    width = heads * HEAD

    @pl.when(step == 0)
    def _():
        state[...] = jnp.zeros_like(state)

    split = split_ref[0]
    tri = triangle(False)
    for n in range(chunks):
        start = (step * chunks + n) * CHUNK
        allowed, enter, tail, kept = chunk_masks(start, split)
        rows = slice(n * CHUNK, (n + 1) * CHUNK)
        for h in range(heads):
            cols = slice(h * HEAD, (h + 1) * HEAD)

            def part(which):
                return pre_ref[rows, which * width + h * HEAD : which * width + (h + 1) * HEAD]

            pre_q = part(0)
            q = pre_q * sigmoid_pair(pre_q)[0]
            bound = bound_ref[:, cols]
            plus, minus = sigmoid_pair(part(1) + bias_ref[:, cols])
            k = (1.0 - bound) * minus
            log_forget = jnp.log(bound + (1.0 - bound) * plus)
            _, _, _, _, _, _, whole, final, to_final, qd, keys = chunk_common(q, k, log_forget, tri)
            v = part(2).astype(BF16)
            scores = jnp.where(allowed, scores_of(qd, keys), 0.0).astype(BF16)
            old = state[h]
            states_ref[n, h] = old
            mixed = dot_nn(scores, v) + dot_nt((q * whole * enter).astype(BF16), old.astype(BF16))
            ending = (k * to_final * tail).astype(BF16)
            state[h] = old * (jnp.exp(final) * kept) + dot_tn(v, ending)
            mixed_ref[rows, cols] = mixed
            scale = lax.rsqrt(jnp.mean(mixed * mixed, axis=-1, keepdims=True) + EPS_GROUP)
            pre_g = part(3)
            gate = pre_g * sigmoid_pair(pre_g)[0]
            gated_ref[rows, cols] = (mixed * scale * gain_ref[:, cols] * gate).astype(BF16)


def mixer_forward(pre, bias, bound, gain, split, order):
    tokens, wide = pre.shape
    width = wide // 4
    heads = width // HEAD
    steps = order.shape[0]
    block = tokens // steps
    chunks = block // CHUNK
    row = pl.BlockSpec((1, width), lambda i, order: (0, 0))
    grid_spec = pltpu.PrefetchScalarGridSpec(
        num_scalar_prefetch=1,
        grid=(steps,),
        in_specs=[
            pl.BlockSpec(memory_space=pltpu.SMEM),
            pl.BlockSpec((block, wide), lambda i, order: (order[i], 0)),
            row,
            row,
            row,
        ],
        out_specs=[
            pl.BlockSpec((block, width), lambda i, order: (order[i], 0)),
            pl.BlockSpec((block, width), lambda i, order: (i, 0)),
            pl.BlockSpec((chunks, heads, HEAD, HEAD), lambda i, order: (i, 0, 0, 0)),
        ],
        scratch_shapes=[pltpu.VMEM((heads, HEAD, HEAD), F32)],
    )
    return pl.pallas_call(
        functools.partial(forward_kernel, heads, chunks),
        grid_spec=grid_spec,
        out_shape=[
            jax.ShapeDtypeStruct((tokens, width), BF16),
            jax.ShapeDtypeStruct((tokens, width), F32),
            jax.ShapeDtypeStruct((tokens // CHUNK, heads, HEAD, HEAD), F32),
        ],
        compiler_params=pltpu.CompilerParams(
            dimension_semantics=("arbitrary",), vmem_limit_bytes=VMEM
        ),
        cost_estimate=cost(tokens * width * 14000),
        name="mixer_forward",
    )(order, split, pre, bias[None], bound[None], gain[None])


def backward_kernel(
    heads,
    chunks,
    order_ref,
    split_ref,
    pre_ref,
    mixed_ref,
    grad_ref,
    states_ref,
    bias_ref,
    bound_ref,
    gain_ref,
    out_ref,
    sums_ref,
    adjoint,
    later,
):
    step = pl.program_id(0)
    steps = pl.num_programs(0)
    width = heads * HEAD
    count = CHUNK // SUB

    @pl.when(step == 0)
    def _():
        adjoint[...] = jnp.zeros_like(adjoint)
        later[...] = jnp.zeros_like(later)
        sums_ref[...] = jnp.zeros_like(sums_ref)

    split = split_ref[0]
    tri = triangle(False)
    tri_up = triangle(True)
    for n in reversed(range(chunks)):
        start = ((steps - 1 - step) * chunks + n) * CHUNK
        allowed, enter, tail, kept = chunk_masks(start, split)
        rows = slice(n * CHUNK, (n + 1) * CHUNK)
        for h in range(heads):
            cols = slice(h * HEAD, (h + 1) * HEAD)

            def part(which):
                return pre_ref[rows, which * width + h * HEAD : which * width + (h + 1) * HEAD]

            def store(which, value):
                out_ref[rows, which * width + h * HEAD : which * width + (h + 1) * HEAD] = value.astype(BF16)

            pre_q = part(0)
            sig_q, sig_nq = sigmoid_pair(pre_q)
            q = pre_q * sig_q
            bound = bound_ref[:, cols]
            plus, minus = sigmoid_pair(part(1) + bias_ref[:, cols])
            k = (1.0 - bound) * minus
            forget = bound + (1.0 - bound) * plus
            _, mids, ends, to_mid, from_mid, to_end, whole, final, to_final, qd, keys = chunk_common(
                q, k, jnp.log(forget), tri
            )
            v = part(2).astype(BF16)

            mixed = mixed_ref[rows, cols]
            grad = grad_ref[rows, cols].astype(F32)
            gain = gain_ref[:, cols]
            scale = lax.rsqrt(jnp.mean(mixed * mixed, axis=-1, keepdims=True) + EPS_GROUP)
            pre_g = part(3)
            sig_g, sig_ng = sigmoid_pair(pre_g)
            gate = pre_g * sig_g
            unit = mixed * scale
            u = grad * gain * gate
            moment = jnp.mean(u * unit, axis=-1, keepdims=True)
            mixed_grad = scale * (u - unit * moment)
            gu = grad * unit
            gain_sum = jnp.sum(gu * gate, axis=0, keepdims=True)
            store(3, gu * gain * (sig_g * (1.0 + pre_g * sig_ng)))

            do = mixed_grad.astype(BF16)
            old = states_ref[n, h]
            lam = adjoint[h]
            old_low = old.astype(BF16)
            lam_low = lam.astype(BF16)
            scores = jnp.where(allowed, scores_of(qd, keys), 0.0).astype(BF16)
            pair = jnp.where(allowed, dot_nt(do, v), 0.0).astype(BF16)
            reach = whole * enter
            remain = to_final * tail
            ending = (k * remain).astype(BF16)
            store(2, dot_tn(scores, do) + dot_nt(ending, lam_low))

            q_rows = []
            k_rows = [None] * count
            for i in range(count):
                pair_i = pair[i * SUB : (i + 1) * SUB]
                q_rows.append(dot_nn(pair_i, keys[i]))
                back = dot_tn(pair_i, qd[i * SUB : (i + 1) * SUB])
                for j in range(i + 1):
                    piece = back[j * SUB : (j + 1) * SUB]
                    if j == i:
                        piece = piece * from_mid[j * SUB : (j + 1) * SUB]
                        k_rows[j] = (k_rows[j], piece)
                    else:
                        piece = piece * jnp.exp(mids[i] - ends[j])
                        first = k_rows[j]
                        k_rows[j] = piece if first is None else first + piece
                diagonal = k_rows[i][1]
                k_rows[i] = None
                if i == 0:
                    diagonals = []
                diagonals.append(diagonal)
            k_intra = []
            for j in range(count):
                piece = diagonals[j]
                if k_rows[j] is not None:
                    piece = piece + k_rows[j] * to_end[j * SUB : (j + 1) * SUB]
                k_intra.append(piece)
            dq = jnp.concatenate(q_rows, axis=0) * to_mid + dot_nn(do, old_low) * reach
            dk = jnp.concatenate(k_intra, axis=0) + dot_nn(v, lam_low) * remain
            anchor = jnp.sum(lam * later[h], axis=0, keepdims=True)
            dlog = tri_dot(tri_up, q * dq - k * dk) + anchor
            adjoint[h] = lam * (jnp.exp(final) * kept) + dot_tn(do, (q * reach).astype(BF16))
            later[h] = old

            store(0, dq * (sig_q * (1.0 + pre_q * sig_nq)))
            drive = minus * (dlog / forget - dk)
            forget_grad = (1.0 - bound) * plus * drive
            store(1, forget_grad)
            sums_ref[0:1, cols] += gain_sum
            sums_ref[1:2, cols] += jnp.sum(forget_grad, axis=0, keepdims=True)
            sums_ref[2:3, cols] += jnp.sum(drive, axis=0, keepdims=True)


def mixer_backward(pre, mixed, grad, states, bias, bound, gain, split, order):
    tokens, wide = pre.shape
    width = wide // 4
    heads = width // HEAD
    steps = order.shape[0]
    block = tokens // steps
    chunks = block // CHUNK
    row = pl.BlockSpec((1, width), lambda i, order: (0, 0))
    placed = lambda i, order: (order[steps - 1 - i], 0)
    grid_spec = pltpu.PrefetchScalarGridSpec(
        num_scalar_prefetch=1,
        grid=(steps,),
        in_specs=[
            pl.BlockSpec(memory_space=pltpu.SMEM),
            pl.BlockSpec((block, wide), placed),
            pl.BlockSpec((block, width), lambda i, order: (steps - 1 - i, 0)),
            pl.BlockSpec((block, width), placed),
            pl.BlockSpec((chunks, heads, HEAD, HEAD), lambda i, order: (steps - 1 - i, 0, 0, 0)),
            row,
            row,
            row,
        ],
        out_specs=[
            pl.BlockSpec((block, wide), placed),
            pl.BlockSpec((8, width), lambda i, order: (0, 0)),
        ],
        scratch_shapes=[pltpu.VMEM((heads, HEAD, HEAD), F32), pltpu.VMEM((heads, HEAD, HEAD), F32)],
    )
    return pl.pallas_call(
        functools.partial(backward_kernel, heads, chunks),
        grid_spec=grid_spec,
        out_shape=[
            jax.ShapeDtypeStruct((tokens, wide), BF16),
            jax.ShapeDtypeStruct((8, width), F32),
        ],
        compiler_params=pltpu.CompilerParams(
            dimension_semantics=("arbitrary",), vmem_limit_bytes=VMEM
        ),
        cost_estimate=cost(tokens * width * 22000),
        name="mixer_backward",
    )(order, split, pre, mixed, grad, states, bias[None], bound[None], gain[None])


def blocks_of(array, count):
    size = array.shape[0] // count
    return [array[m * size : (m + 1) * size] for m in range(count)]


def product_kernel(dims, parts, a_ref, b_ref, *refs):
    dot = lax.dot_general(a_ref[...], b_ref[...], (dims, ((), ())), preferred_element_type=F32)
    for block, out_ref in zip(blocks_of(dot, parts), refs[len(refs) - parts :]):
        out_ref[...] = block.astype(out_ref.dtype)


NN = ((1,), (0,))
NT = ((1,), (1,))
TN = ((0,), (0,))


def product(a, b, dims, kind, rows=None, cols=None, a_half=None, b_half=None, parts=1, wait=()):
    count = a.shape[1 - dims[0][0]] if a_half is None else a.shape[0] // 2
    depth = a.shape[dims[0][0]]
    wide = b.shape[1 - dims[1][0]] // (1 if b_half is None else 2)
    tile_rows = rows or count
    tile_cols = cols or wide
    by_rows = rows is not None
    shift = (a_half or 0) * (count // tile_rows)

    def at_row(i):
        return (i if by_rows else 0) + shift

    def at_col(i):
        return 0 if by_rows else i

    b_shift = (b_half or 0) * (wide // tile_cols)

    if dims[0][0] == 1:
        a_spec = pl.BlockSpec((tile_rows, depth), lambda i: (at_row(i), 0))
    else:
        a_spec = pl.BlockSpec((depth, tile_rows), lambda i: (0, at_row(i)))
    if dims[1][0] == 0:
        b_spec = pl.BlockSpec((depth, tile_cols), lambda i: (0, at_col(i) + b_shift))
    else:
        b_spec = pl.BlockSpec((tile_cols, depth), lambda i: (at_col(i) + b_shift, 0))
    out_spec = pl.BlockSpec((tile_rows // parts, tile_cols), lambda i: (at_row(i) - shift, at_col(i)))
    out = pl.pallas_call(
        functools.partial(product_kernel, dims, parts),
        grid=(count // tile_rows * (wide // tile_cols),),
        in_specs=[a_spec, b_spec] + [UNREAD] * len(wait),
        out_specs=[out_spec] * parts,
        out_shape=[jax.ShapeDtypeStruct((count // parts, wide), kind)] * parts,
        compiler_params=pltpu.CompilerParams(
            dimension_semantics=("arbitrary",), vmem_limit_bytes=VMEM
        ),
        cost_estimate=cost(2 * count * wide * depth),
        name="product",
    )(a, b, *wait)
    return out[0] if parts == 1 else out


def gate_kernel(low_ref, weight_ref, pre_ref, hidden_ref):
    half = hidden_ref.shape[1]
    pre = dot_nn(low_ref[...], weight_ref[...])
    pre_ref[...] = pre
    gate = pre[:, :half]
    hidden_ref[...] = (gate * sigmoid_pair(gate)[0] * pre[:, half:]).astype(BF16)


def gate_product(low, weight, rows=256):
    count, depth = low.shape
    wide = weight.shape[1]
    return pl.pallas_call(
        gate_kernel,
        grid=(count // rows,),
        in_specs=[
            pl.BlockSpec((rows, depth), lambda i: (i, 0)),
            pl.BlockSpec((depth, wide), lambda i: (0, 0)),
        ],
        out_specs=[
            pl.BlockSpec((rows, wide), lambda i: (i, 0)),
            pl.BlockSpec((rows, wide // 2), lambda i: (i, 0)),
        ],
        out_shape=[
            jax.ShapeDtypeStruct((count, wide), F32),
            jax.ShapeDtypeStruct((count, wide // 2), BF16),
        ],
        compiler_params=pltpu.CompilerParams(
            dimension_semantics=("arbitrary",), vmem_limit_bytes=VMEM
        ),
        cost_estimate=cost(2 * count * depth * wide),
        name="gate_product",
    )(low, weight)


def hidden_back_kernel(grad_ref, weight_ref, pre_ref, out_ref):
    half = out_ref.shape[1] // 2
    grad = dot_nt(grad_ref[...], weight_ref[...])
    gate, up = pre_ref[:, :half], pre_ref[:, half:]
    sig, rest = sigmoid_pair(gate)
    out_ref[:, :half] = (grad * up * sig * (1.0 + gate * rest)).astype(BF16)
    out_ref[:, half:] = (grad * (gate * sig)).astype(BF16)


def hidden_back(grad, weight, pre, rows=256, wait=()):
    count, depth = grad.shape
    wide = pre.shape[1]
    return pl.pallas_call(
        lambda *refs: hidden_back_kernel(*refs[:3], refs[-1]),
        grid=(count // rows,),
        in_specs=[
            pl.BlockSpec((rows, depth), lambda i: (i, 0)),
            pl.BlockSpec(weight.shape, lambda i: (0, 0)),
            pl.BlockSpec((rows, wide), lambda i: (i, 0)),
        ]
        + [UNREAD] * len(wait),
        out_specs=pl.BlockSpec((rows, wide), lambda i: (i, 0)),
        out_shape=jax.ShapeDtypeStruct((count, wide), BF16),
        compiler_params=pltpu.CompilerParams(
            dimension_semantics=("arbitrary",), vmem_limit_bytes=VMEM
        ),
        cost_estimate=cost(count * depth * wide),
        name="hidden_back",
    )(grad, weight, pre, *wait)


def weight_sum_kernel(own_ref, other_ref, b_ref, weight_ref, right_ref, *refs):
    out_ref, sum_ref = refs[-2:]
    half = own_ref.shape[0]
    wide = b_ref.shape[1]
    dot = dot_tn(own_ref[...], b_ref[:half]) + dot_tn(other_ref[...], b_ref[half:])
    out_ref[:, :wide] = dot.astype(out_ref.dtype)
    total = jnp.sum(dot * weight_ref[...].astype(F32), axis=1, keepdims=True)
    sum_ref[...] = jnp.broadcast_to(total, sum_ref.shape)
    start = 0
    more = None
    for ref in refs[:-2]:
        size = ref.shape[0]
        if start < right_ref.shape[0]:
            term = dot_tn(ref[...], right_ref[start : start + size])
            more = term if more is None else more + term
            start += size
    out_ref[:, wide:] = more.astype(out_ref.dtype)


def weight_sum_product(own, other, b, weight, blocks, right, rows=256, wait=()):
    half, count = own.shape
    depth, wide = b.shape
    extra = right.shape[1]
    a_spec = pl.BlockSpec((half, rows), lambda i: (0, i))
    out, total = pl.pallas_call(
        weight_sum_kernel,
        grid=(count // rows,),
        in_specs=[
            a_spec,
            a_spec,
            pl.BlockSpec((depth, wide), lambda i: (0, 0)),
            pl.BlockSpec((rows, wide), lambda i: (i, 0)),
            pl.BlockSpec((depth, extra), lambda i: (0, 0)),
        ]
        + [pl.BlockSpec((block.shape[0], rows), lambda i: (0, i)) for block in blocks]
        + [UNREAD] * len(wait),
        out_specs=[
            pl.BlockSpec((rows, wide + extra), lambda i: (i, 0)),
            pl.BlockSpec((rows, HEAD), lambda i: (i, 0)),
        ],
        out_shape=[
            jax.ShapeDtypeStruct((count, wide + extra), BF16),
            jax.ShapeDtypeStruct((count, HEAD), F32),
        ],
        compiler_params=pltpu.CompilerParams(
            dimension_semantics=("arbitrary",), vmem_limit_bytes=VMEM
        ),
        cost_estimate=cost(2 * count * (wide + extra) * depth),
        name="weight_sum_product",
    )(own, other, b, weight, right, *blocks, *wait)
    return out, total[:, 0]


def early_product_kernel(b_ref, *refs):
    out_ref = refs[-1]
    size = refs[0].shape[0]
    for ref, block in zip(refs[:-1], (0, 1, 2, 4, 5, 6)):
        out_ref[block * size : (block + 1) * size] = dot_nt(ref[...], b_ref[...])


def late_product_kernel(b_ref, early_ref, *refs):
    out_ref = refs[-1]
    for step in range(2):

        @pl.when(pl.program_id(0) == step)
        def _(step=step):
            half = refs[0].shape[0]
            out_ref[:half] = dot_nt(refs[2 * step][...], b_ref[...])
            out_ref[half:] = dot_nt(refs[2 * step + 1][...], b_ref[...])


def early_product(blocks, b):
    size = blocks[0].shape[0]
    return pl.pallas_call(
        early_product_kernel,
        out_shape=jax.ShapeDtypeStruct((8 * size, b.shape[0]), F32),
        compiler_params=pltpu.CompilerParams(vmem_limit_bytes=VMEM),
        cost_estimate=cost(2 * 6 * size * b.size),
        name="early_product",
    )(b, *blocks)


def late_product(out, late, b):
    size = 2 * late[0].shape[0]
    width = b.shape[0]
    whole = [pl.BlockSpec(part.shape, lambda i: (0, 0)) for part in late]
    return pl.pallas_call(
        late_product_kernel,
        grid=(2,),
        in_specs=[pl.BlockSpec(b.shape, lambda i: (0, 0)), UNREAD] + whole,
        out_specs=pl.BlockSpec((size, width), lambda i: (4 * i + 3, 0)),
        out_shape=jax.ShapeDtypeStruct(out.shape, F32),
        input_output_aliases={1: 0},
        compiler_params=pltpu.CompilerParams(vmem_limit_bytes=VMEM),
        cost_estimate=cost(2 * 2 * size * b.size),
        name="late_product",
    )(b, out, *late)


def joined_columns_kernel(width, at_ref, own_ref, other_ref, *out_refs):
    def store(ref):
        for which in range(4):
            out_refs[which][...] = ref[:, which * width : (which + 1) * width].astype(F32)
        out_refs[4][...] = ref[:, 4 * width :].astype(F32).T

    mine = pl.program_id(0) == at_ref[0]
    pl.when(mine)(lambda: store(own_ref))
    pl.when(jnp.logical_not(mine))(lambda: store(other_ref))


def joined_columns(own, other, at, width):
    rows = own.shape[0]
    whole = pl.BlockSpec(own.shape, lambda i, at: (0, 0))
    beside = pl.BlockSpec((rows, width), lambda i, at: (0, i))
    return pl.pallas_call(
        functools.partial(joined_columns_kernel, width),
        grid_spec=pltpu.PrefetchScalarGridSpec(
            num_scalar_prefetch=1,
            grid=(2,),
            in_specs=[whole, whole],
            out_specs=[beside] * 4 + [pl.BlockSpec((width, rows), lambda i, at: (i, 0))],
        ),
        out_shape=[jax.ShapeDtypeStruct((rows, 2 * width), F32)] * 4
        + [jax.ShapeDtypeStruct((2 * width, rows), F32)],
        compiler_params=pltpu.CompilerParams(
            dimension_semantics=("arbitrary",), vmem_limit_bytes=VMEM
        ),
        cost_estimate=cost(1 << 20),
        name="joined_columns",
    )(at.astype(jnp.int32).reshape(1), own, other)


def rms_rows(rows_in):
    return lax.rsqrt(jnp.mean(rows_in * rows_in, axis=-1, keepdims=True) + EPS_NORM)


def norm_back(grad, rows_in, gain_vec):
    inv = rms_rows(rows_in)
    u = grad * gain_vec
    moment = jnp.mean(u * rows_in, axis=-1, keepdims=True)
    return inv * u - rows_in * (inv * inv * inv * moment), jnp.sum(grad * rows_in * inv, axis=0)


def gather(part, axes, dim):
    return lax.all_gather(part, axes, axis=dim, tiled=True)


def gather_columns(part, axis):
    count, at = lax.axis_size(axis), lax.axis_index(axis)
    if count > 4:
        return gather(part, axis, 1)
    size = part.shape[1]
    out = jnp.zeros((part.shape[0], count * size), part.dtype)
    for m in range(count):
        block = part if m == 0 else lax.ppermute(part, axis, [(i, i ^ m) for i in range(count)])
        out = lax.dynamic_update_slice_in_dim(out, block, (at ^ m) * size, 1)
    return out


def scatter(whole, axes, dim):
    return lax.psum_scatter(whole, axes, scatter_dimension=dim, tiled=True)


def matmul(left_side, right_side):
    return jnp.dot(left_side, right_side, preferred_element_type=F32)


def after(value, *others):
    return lax.optimization_barrier((value, *others))[0]


def small_sum(part, axis):
    count = lax.axis_size(axis)
    if count <= 4:
        got = [lax.ppermute(part, axis, [(i, i ^ m) for i in range(count)]) for m in range(1, count)]
        return sum(got, part)
    mask = 1
    while mask < count:
        part = part + lax.ppermute(part, axis, [(i, i ^ mask) for i in range(count)])
        mask *= 2
    return part


def together(*values):
    return lax.optimization_barrier(values)


def swap(part):
    return lax.ppermute(part, "ctx", [(0, 1), (1, 0)])


def in_order(own, dim):
    other = swap(own)
    first = lax.axis_index("ctx") == 0
    return jnp.concatenate([jnp.where(first, own, other), jnp.where(first, other, own)], axis=dim)


def partner(part, mask):
    return lax.ppermute(part, "tp", [(i, i ^ mask) for i in range(lax.axis_size("tp"))])


def relative(array, count, at):
    size = array.shape[0] // count
    return jnp.concatenate(
        [lax.dynamic_slice_in_dim(array, (at ^ m) * size, size, 0) for m in range(count)], axis=0
    )


def parts_of(blocks):
    half = blocks[0].shape[0] // 2
    low, high = [block[:half] for block in blocks], [block[half:] for block in blocks]
    near = jnp.concatenate([low[1], low[3]], axis=0)
    far = jnp.concatenate([high[2], high[3]], axis=0)
    return [near, far, blocks[0], low[2], high[1]]


def sum_first(parts):
    return partner(parts[0], 1), partner(parts[1], 2)


def sum_second(parts, near, far):
    half = near.shape[0] // 2
    near, far = together(near, far)
    pass_far = (parts[3].astype(F32) + near[half:].astype(F32)).astype(BF16)
    pass_near = (parts[4].astype(F32) + far[half:].astype(F32)).astype(BF16)
    pass_far, pass_near = together(pass_far, pass_near)
    return together(partner(pass_far, 2), partner(pass_near, 1))


def sum_total(parts, first, second):
    half = second[0].shape[0]
    halves = [
        parts[2][which * half : (which + 1) * half].astype(F32)
        + first[which][:half].astype(F32)
        + second[which].astype(F32)
        for which in (0, 1)
    ]
    return jnp.concatenate(halves, axis=0)


def gather_first(own):
    return partner(own, 1), partner(own, 2)


def gather_second(near, far):
    half = near.shape[0] // 2
    return partner(far[:half], 1), partner(near[half:], 2)


def gathered_parts(own, first, second):
    near, far = first
    half = second[0].shape[0]
    return [near[:half], second[0], far[half:], second[1], own, far[:half], near[half:]]


def placed_kernel(at_ref, own_ref, near_ref, far_ref, top_ref, bottom_ref, *refs):
    out_ref = refs[-1]
    step = pl.program_id(0)
    half = top_ref.shape[0]
    for which, ref in enumerate((own_ref, near_ref, far_ref)):

        @pl.when(step == which)
        def _(ref=ref):
            out_ref[...] = ref[...].astype(out_ref.dtype)

    @pl.when(step == 3)
    def _():
        out_ref[:half] = top_ref[...].astype(out_ref.dtype)
        out_ref[half:] = bottom_ref[...].astype(out_ref.dtype)


def placed_blocks(own, near, far, top, bottom, at, kind, wait=()):
    size, width = own.shape
    inputs = [own, near, far, top, bottom]
    return pl.pallas_call(
        placed_kernel,
        grid_spec=pltpu.PrefetchScalarGridSpec(
            num_scalar_prefetch=1,
            grid=(4,),
            in_specs=[pl.BlockSpec(part.shape, lambda i, at: (0, 0)) for part in inputs] + [UNREAD] * len(wait),
            out_specs=pl.BlockSpec((size, width), lambda i, at: (i ^ at[0], 0)),
        ),
        out_shape=jax.ShapeDtypeStruct((4 * size, width), kind),
        compiler_params=pltpu.CompilerParams(
            dimension_semantics=("arbitrary",), vmem_limit_bytes=VMEM
        ),
        cost_estimate=cost(3 << 30),
        name="placed_blocks",
    )(at.astype(jnp.int32).reshape(1), *inputs, *wait)


def body(
    block_in,
    query_proj,
    forget_proj,
    value_proj,
    outgate_proj,
    out_proj,
    ffn_gate,
    ffn_up,
    ffn_down,
    first_gain,
    second_gain,
    group_gain,
    forget_bias,
    bound_table,
    layer_index,
    second_start,
    cotangent,
):
    ctx_count, ctx_at = lax.axis_size("ctx"), lax.axis_index("ctx")
    tp_count, tp_at = lax.axis_size("tp"), lax.axis_index("tp")
    row_count, model = block_in.shape
    local_width = query_proj.shape[1]
    width = local_width // ctx_count
    hidden_width = ffn_gate.shape[1]
    shard_rows = row_count // tp_count

    def own_half(array, dim):
        size = array.shape[dim] // ctx_count
        return lax.dynamic_slice_in_dim(array, ctx_at * size, size, dim)

    blocks = ctx_count * tp_count
    order = lax.iota(jnp.int32, blocks) ^ (ctx_at * tp_count + tp_at)

    mix_full = gather(
        jnp.concatenate(
            [own_half(w, 1) for w in (query_proj, forget_proj, value_proj, outgate_proj)], axis=1
        ),
        "dp",
        0,
    )
    out_full = gather_columns(own_half(out_proj, 0), "dp")
    ffn_full = gather(own_half(jnp.concatenate([ffn_gate, ffn_up], axis=1), 0), ("dp", "ctx"), 0)
    down_full = gather(own_half(ffn_down, 1), ("dp", "ctx"), 1)

    inputs = relative(block_in, tp_count, tp_at).astype(F32)
    first_low = (inputs * rms_rows(inputs) * first_gain).astype(BF16)
    first_swapped = swap(first_low)
    first_all = jnp.concatenate([first_low, first_swapped], axis=0)
    table = own_half(bound_table, 1)
    weights = jax.nn.softmax(table, axis=0)
    rows = lax.broadcasted_iota(jnp.int32, (table.shape[0], 1), 0)
    counted = jnp.where((rows >= 1) & (rows <= layer_index[0]), 1.0, 0.0)
    bound = jnp.sum(weights * counted, axis=0)
    bias = own_half(forget_bias, 0)
    gain = own_half(group_gain, 0)
    pre = product(first_all, mix_full, NN, F32, rows=512)
    gated, mixed, states = mixer_forward(pre, bias, bound, gain, second_start, order)
    inputs_own = inputs[:shard_rows]
    out_other = [
        swap(block) for block in product(gated, out_full, NN, BF16, cols=512, a_half=1, parts=tp_count)
    ]
    out_own = product(gated, out_full, NN, BF16, cols=512, a_half=0, parts=tp_count)
    out_part = parts_of([(a.astype(F32) + b.astype(F32)).astype(BF16) for a, b in zip(out_own, out_other)])
    first = sum_first(out_part)
    second = sum_second(out_part, *first)
    resid = inputs_own + sum_total(out_part, first, second)

    second_own = (resid * rms_rows(resid) * second_gain).astype(BF16)
    first = gather_first(second_own)
    second_low = jnp.concatenate(
        gathered_parts(second_own, first, gather_second(*first)), axis=0
    )
    cotangent_blocks = blocks_of(relative(cotangent, tp_count, tp_at), tp_count)
    cotangent_rel = jnp.concatenate(parts_of(cotangent_blocks), axis=0)
    gate_up, hidden = gate_product(second_low, ffn_full)

    down_grad = product(hidden, cotangent_rel, TN, BF16, cols=512)
    down_sum = scatter(down_grad, ("dp", "ctx"), 1)
    gate_up_grad = hidden_back(cotangent_rel, down_full, gate_up, wait=[down_grad])
    second_sent = product(gate_up_grad, ffn_full, NT, BF16, cols=512, a_half=0, parts=2)
    first = sum_first(second_sent)
    second_kept = product(gate_up_grad, ffn_full, NT, BF16, cols=512, a_half=1, wait=second_sent)
    half_rows = shard_rows // 2
    second_part = [
        *second_sent,
        second_kept[:shard_rows],
        second_kept[shard_rows : shard_rows + half_rows],
        second_kept[shard_rows + half_rows :],
    ]
    ffn_rows = product(hidden, down_full, NN, BF16, cols=256, parts=tp_count, wait=[second_kept])
    gate_weight_grad = product(second_low, gate_up_grad, TN, BF16, rows=256, b_half=0)
    gate_sum = scatter(after(gate_weight_grad, second_kept, *first), ("dp", "ctx"), 0)
    second = sum_second(second_part, *first)
    second_total = sum_total(second_part, first, second)
    resid_part, second_gain_grad = norm_back(
        after(second_total, down_sum, ffn_rows[0]), resid, second_gain
    )
    resid_grad = cotangent_blocks[0].astype(F32) + resid_part
    resid_own = resid_grad.astype(BF16)
    first = gather_first(resid_own)
    up_weight_grad = product(second_low, gate_up_grad, TN, BF16, rows=256, b_half=1)
    up_sum = scatter(after(up_weight_grad, *first), ("dp", "ctx"), 0)
    resid_second = gather_second(*first)
    resid_early = [resid_own, *first]
    resid_early = resid_early + [swap(block) for block in resid_early]
    early_grad = early_product(resid_early, out_full)
    resid_late = [*resid_second, *[swap(after(block, early_grad)) for block in resid_second]]
    resid_blocks = [*resid_early[:3], *resid_late[:2], *resid_early[3:], *resid_late[2:]]

    ffn_rows = [after(part, *resid_second) for part in ffn_rows]
    ffn_part = [*ffn_rows[:3], ffn_rows[3][:half_rows], ffn_rows[3][half_rows:]]
    ffn_first = sum_first(ffn_part)
    gated_grad = late_product(early_grad, resid_late, out_full)
    proj_grad, sums = mixer_backward(pre, mixed, gated_grad, states, bias, bound, gain, second_start, order)
    first_other = product(proj_grad, mix_full, NT, BF16, cols=256, a_half=1, parts=tp_count, wait=ffn_first)
    ffn_second = sum_second([after(block, proj_grad) for block in ffn_part], *ffn_first)
    block_own = (resid + sum_total(ffn_part, ffn_first, ffn_second)).astype(BF16)
    first_own = product(
        proj_grad, mix_full, NT, BF16, cols=256, a_half=0, parts=tp_count, wait=[first_other[0], block_own]
    )
    block_first = gather_first(block_own)
    first_part = [
        (own.astype(F32) + swap(other).astype(F32)).astype(BF16)
        for own, other in zip(first_own, first_other)
    ]
    first_part = parts_of(first_part)
    first = sum_first(first_part)
    mix_grad, first_sum = weight_sum_product(
        first_low, first_swapped, proj_grad, mix_full, resid_blocks, gated, wait=block_first
    )
    mix_sum = scatter(after(mix_grad, gate_sum, up_sum, *first), "dp", 0)
    final_first = first
    second = sum_second(first_part, *first)
    input_part, _ = norm_back(sum_total(first_part, first, second), inputs_own, first_gain)
    input_own = (resid_grad + input_part).astype(BF16)
    block_second = gather_second(*[after(block, *second) for block in block_first])
    input_own = after(input_own, *block_second)
    first = gather_first(input_own)

    block_out = placed_blocks(block_own, *block_first, *block_second, tp_at, BF16)
    input_second = gather_second(*[after(block, block_out) for block in first])
    input_grad = placed_blocks(input_own, *first, *input_second, tp_at, F32)

    gains = jnp.concatenate([first_sum / first_gain, second_gain_grad]).reshape(-1, HEAD)
    gains = after(gains, *input_second)
    gains = small_sum(gains + swap(gains), "tp")
    small = small_sum(jnp.concatenate([sums[:3].reshape(-1, HEAD), gains]), "dp")
    cut = 3 * width // HEAD
    head_sums = in_order(small[:cut].reshape(3, width), 1)
    gain_sums = small[cut:].reshape(-1)
    all_weights = jax.nn.softmax(bound_table, axis=0)
    all_bound = jnp.sum(all_weights * counted, axis=0)
    table_grad = all_weights * (counted - all_bound) * head_sums[2]

    *mix_shards, out_shard = joined_columns(mix_sum, swap(mix_sum), ctx_at, width)

    return (
        block_out,
        input_grad,
        *mix_shards,
        out_shard,
        in_order(after(gate_sum, *final_first), 0).astype(F32),
        in_order(after(up_sum, *final_first), 0).astype(F32),
        in_order(after(down_sum, *final_first), 1).astype(F32),
        gain_sums[:model],
        gain_sums[model:],
        head_sums[0],
        head_sums[1],
        table_grad,
    )


def solution(mesh):
    return jax.shard_map(
        body,
        mesh=mesh,
        in_specs=(
            P(("dp", "ctx"), None),
            P("dp", "tp"),
            P("dp", "tp"),
            P("dp", "tp"),
            P("dp", "tp"),
            P("tp", "dp"),
            P("dp", "tp"),
            P("dp", "tp"),
            P("tp", "dp"),
            P(),
            P(),
            P("tp"),
            P("tp"),
            P(None, "tp"),
            P(),
            P("dp"),
            P(("dp", "ctx"), None),
        ),
        out_specs=(
            P(("dp", "ctx"), None),
            P(("dp", "ctx"), None),
            P("dp", "tp"),
            P("dp", "tp"),
            P("dp", "tp"),
            P("dp", "tp"),
            P("tp", "dp"),
            P("dp", "tp"),
            P("dp", "tp"),
            P("tp", "dp"),
            P(),
            P(),
            P("tp"),
            P("tp"),
            P(None, "tp"),
        ),
        check_vma=False,
    )
```

```python
import functools

import jax
import jax.numpy as jnp
from jax import lax
from jax.experimental import pallas as pl
from jax.experimental.pallas import tpu as pltpu
from jax.sharding import PartitionSpec as P

HEAD = 128
SUB = 32
CHUNK = 128
EPS_NORM = 1e-06
EPS_GROUP = 1e-05
F32 = jnp.float32
VMEM = 58 << 20
UNREAD = pl.BlockSpec(memory_space=pl.ANY)
BF16 = jnp.bfloat16


def cost(flops):
    return pl.CostEstimate(flops=2 * flops, bytes_accessed=1 << 20, transcendentals=0)


def dot_nn(a, b):
    return lax.dot_general(a, b, (((1,), (0,)), ((), ())), preferred_element_type=F32)


def dot_nt(a, b):
    return lax.dot_general(a, b, (((1,), (1,)), ((), ())), preferred_element_type=F32)


def dot_tn(a, b):
    return lax.dot_general(a, b, (((0,), (0,)), ((), ())), preferred_element_type=F32)


def sigmoid_pair(x):
    small = jnp.exp(-jnp.abs(x))
    inv = 1.0 / (1.0 + small)
    rest = small * inv
    up = x >= 0.0
    return jnp.where(up, inv, rest), jnp.where(up, rest, inv)


def tri_dot(tri, x):
    high = x.astype(BF16)
    low = (x - high.astype(F32)).astype(BF16)
    return dot_nn(tri, high) + dot_nn(tri, low)


def triangle(upper):
    rows = lax.broadcasted_iota(jnp.int32, (CHUNK, CHUNK), 0)
    cols = lax.broadcasted_iota(jnp.int32, (CHUNK, CHUNK), 1)
    keep = rows <= cols if upper else rows >= cols
    return jnp.where(keep, 1.0, 0.0).astype(BF16)


def chunk_masks(start, split):
    rows = lax.broadcasted_iota(jnp.int32, (CHUNK, CHUNK), 0)
    cols = lax.broadcasted_iota(jnp.int32, (CHUNK, CHUNK), 1)
    local = split - start
    causal = rows >= cols
    same = (rows >= local) == (cols >= local)
    token = lax.broadcasted_iota(jnp.int32, (CHUNK, HEAD), 0)
    before = start > split
    enter = jnp.where(jnp.logical_or(token < local, before), 1.0, 0.0)
    last = CHUNK - 1 >= local
    tail = jnp.where((token >= local) == last, 1.0, 0.0)
    kept = jnp.where(jnp.logical_or(jnp.logical_not(last), before), 1.0, 0.0)
    return causal & same, enter, tail, kept


def key_rows(k, b, kd, k_end_sub, mids, ends):
    out = []
    count = CHUNK // SUB
    for i in range(count):
        parts = []
        for j in range(i):
            part = k_end_sub[j * SUB : (j + 1) * SUB]
            parts.append(part * jnp.exp(mids[i] - ends[j]))
        parts.append(kd[i * SUB : (i + 1) * SUB])
        if i < count - 1:
            parts.append(jnp.zeros(((count - 1 - i) * SUB, HEAD), F32))
        out.append(jnp.concatenate(parts, axis=0).astype(BF16))
    return out


def spread(rows_list):
    return jnp.concatenate([jnp.broadcast_to(r, (SUB, HEAD)) for r in rows_list], axis=0)


def chunk_common(q, k, log_forget, tri):
    count = CHUNK // SUB
    b = tri_dot(tri, log_forget)
    mids = [b[i * SUB + SUB // 2 : i * SUB + SUB // 2 + 1] for i in range(count)]
    ends = [b[(i + 1) * SUB - 1 : (i + 1) * SUB] for i in range(count)]
    mid = spread(mids)
    end = spread(ends)
    to_mid = jnp.exp(b - mid)
    from_mid = jnp.exp(mid - b)
    to_end = jnp.exp(end - b)
    whole = jnp.exp(b)
    final = ends[-1]
    to_final = jnp.exp(final - b)
    qd = (q * to_mid).astype(BF16)
    keys = key_rows(k, b, k * from_mid, k * to_end, mids, ends)
    return b, mids, ends, to_mid, from_mid, to_end, whole, final, to_final, qd, keys


def scores_of(qd, keys):
    count = CHUNK // SUB
    return jnp.concatenate(
        [dot_nt(qd[i * SUB : (i + 1) * SUB], keys[i]) for i in range(count)], axis=0
    )


def forward_kernel(
    heads,
    chunks,
    order_ref,
    split_ref,
    pre_ref,
    bias_ref,
    bound_ref,
    gain_ref,
    gated_ref,
    mixed_ref,
    states_ref,
    state,
):
    step = pl.program_id(0)
    width = heads * HEAD

    @pl.when(step == 0)
    def _():
        state[...] = jnp.zeros_like(state)

    split = split_ref[0]
    tri = triangle(False)
    for n in range(chunks):
        start = (step * chunks + n) * CHUNK
        allowed, enter, tail, kept = chunk_masks(start, split)
        rows = slice(n * CHUNK, (n + 1) * CHUNK)
        for h in range(heads):
            cols = slice(h * HEAD, (h + 1) * HEAD)

            def part(which):
                return pre_ref[rows, which * width + h * HEAD : which * width + (h + 1) * HEAD]

            pre_q = part(0)
            q = pre_q * sigmoid_pair(pre_q)[0]
            bound = bound_ref[:, cols]
            plus, minus = sigmoid_pair(part(1) + bias_ref[:, cols])
            k = (1.0 - bound) * minus
            log_forget = jnp.log(bound + (1.0 - bound) * plus)
            _, _, _, _, _, _, whole, final, to_final, qd, keys = chunk_common(q, k, log_forget, tri)
            v = part(2).astype(BF16)
            scores = jnp.where(allowed, scores_of(qd, keys), 0.0).astype(BF16)
            old = state[h]
            states_ref[n, h] = old
            mixed = dot_nn(scores, v) + dot_nt((q * whole * enter).astype(BF16), old.astype(BF16))
            ending = (k * to_final * tail).astype(BF16)
            state[h] = old * (jnp.exp(final) * kept) + dot_tn(v, ending)
            mixed_ref[rows, cols] = mixed
            scale = lax.rsqrt(jnp.mean(mixed * mixed, axis=-1, keepdims=True) + EPS_GROUP)
            pre_g = part(3)
            gate = pre_g * sigmoid_pair(pre_g)[0]
            gated_ref[rows, cols] = (mixed * scale * gain_ref[:, cols] * gate).astype(BF16)


def mixer_forward(pre, bias, bound, gain, split, order):
    tokens, wide = pre.shape
    width = wide // 4
    heads = width // HEAD
    steps = order.shape[0]
    block = tokens // steps
    chunks = block // CHUNK
    row = pl.BlockSpec((1, width), lambda i, order: (0, 0))
    grid_spec = pltpu.PrefetchScalarGridSpec(
        num_scalar_prefetch=1,
        grid=(steps,),
        in_specs=[
            pl.BlockSpec(memory_space=pltpu.SMEM),
            pl.BlockSpec((block, wide), lambda i, order: (order[i], 0)),
            row,
            row,
            row,
        ],
        out_specs=[
            pl.BlockSpec((block, width), lambda i, order: (order[i], 0)),
            pl.BlockSpec((block, width), lambda i, order: (i, 0)),
            pl.BlockSpec((chunks, heads, HEAD, HEAD), lambda i, order: (i, 0, 0, 0)),
        ],
        scratch_shapes=[pltpu.VMEM((heads, HEAD, HEAD), F32)],
    )
    return pl.pallas_call(
        functools.partial(forward_kernel, heads, chunks),
        grid_spec=grid_spec,
        out_shape=[
            jax.ShapeDtypeStruct((tokens, width), BF16),
            jax.ShapeDtypeStruct((tokens, width), F32),
            jax.ShapeDtypeStruct((tokens // CHUNK, heads, HEAD, HEAD), F32),
        ],
        compiler_params=pltpu.CompilerParams(
            dimension_semantics=("arbitrary",), vmem_limit_bytes=VMEM
        ),
        cost_estimate=cost(tokens * width * 14000),
        name="mixer_forward",
    )(order, split, pre, bias[None], bound[None], gain[None])


def backward_kernel(
    heads,
    chunks,
    order_ref,
    split_ref,
    pre_ref,
    mixed_ref,
    grad_ref,
    states_ref,
    bias_ref,
    bound_ref,
    gain_ref,
    out_ref,
    sums_ref,
    adjoint,
    later,
):
    step = pl.program_id(0)
    steps = pl.num_programs(0)
    width = heads * HEAD
    count = CHUNK // SUB

    @pl.when(step == 0)
    def _():
        adjoint[...] = jnp.zeros_like(adjoint)
        later[...] = jnp.zeros_like(later)
        sums_ref[...] = jnp.zeros_like(sums_ref)

    split = split_ref[0]
    tri = triangle(False)
    tri_up = triangle(True)
    for n in reversed(range(chunks)):
        start = ((steps - 1 - step) * chunks + n) * CHUNK
        allowed, enter, tail, kept = chunk_masks(start, split)
        rows = slice(n * CHUNK, (n + 1) * CHUNK)
        for h in range(heads):
            cols = slice(h * HEAD, (h + 1) * HEAD)

            def part(which):
                return pre_ref[rows, which * width + h * HEAD : which * width + (h + 1) * HEAD]

            def store(which, value):
                out_ref[rows, which * width + h * HEAD : which * width + (h + 1) * HEAD] = value.astype(BF16)

            pre_q = part(0)
            sig_q, sig_nq = sigmoid_pair(pre_q)
            q = pre_q * sig_q
            bound = bound_ref[:, cols]
            plus, minus = sigmoid_pair(part(1) + bias_ref[:, cols])
            k = (1.0 - bound) * minus
            forget = bound + (1.0 - bound) * plus
            _, mids, ends, to_mid, from_mid, to_end, whole, final, to_final, qd, keys = chunk_common(
                q, k, jnp.log(forget), tri
            )
            v = part(2).astype(BF16)

            mixed = mixed_ref[rows, cols]
            grad = grad_ref[rows, cols].astype(F32)
            gain = gain_ref[:, cols]
            scale = lax.rsqrt(jnp.mean(mixed * mixed, axis=-1, keepdims=True) + EPS_GROUP)
            pre_g = part(3)
            sig_g, sig_ng = sigmoid_pair(pre_g)
            gate = pre_g * sig_g
            unit = mixed * scale
            u = grad * gain * gate
            moment = jnp.mean(u * unit, axis=-1, keepdims=True)
            mixed_grad = scale * (u - unit * moment)
            gu = grad * unit
            gain_sum = jnp.sum(gu * gate, axis=0, keepdims=True)
            store(3, gu * gain * (sig_g * (1.0 + pre_g * sig_ng)))

            do = mixed_grad.astype(BF16)
            old = states_ref[n, h]
            lam = adjoint[h]
            old_low = old.astype(BF16)
            lam_low = lam.astype(BF16)
            scores = jnp.where(allowed, scores_of(qd, keys), 0.0).astype(BF16)
            pair = jnp.where(allowed, dot_nt(do, v), 0.0).astype(BF16)
            reach = whole * enter
            remain = to_final * tail
            ending = (k * remain).astype(BF16)
            store(2, dot_tn(scores, do) + dot_nt(ending, lam_low))

            q_rows = []
            k_rows = [None] * count
            for i in range(count):
                pair_i = pair[i * SUB : (i + 1) * SUB]
                q_rows.append(dot_nn(pair_i, keys[i]))
                back = dot_tn(pair_i, qd[i * SUB : (i + 1) * SUB])
                for j in range(i + 1):
                    piece = back[j * SUB : (j + 1) * SUB]
                    if j == i:
                        piece = piece * from_mid[j * SUB : (j + 1) * SUB]
                        k_rows[j] = (k_rows[j], piece)
                    else:
                        piece = piece * jnp.exp(mids[i] - ends[j])
                        first = k_rows[j]
                        k_rows[j] = piece if first is None else first + piece
                diagonal = k_rows[i][1]
                k_rows[i] = None
                if i == 0:
                    diagonals = []
                diagonals.append(diagonal)
            k_intra = []
            for j in range(count):
                piece = diagonals[j]
                if k_rows[j] is not None:
                    piece = piece + k_rows[j] * to_end[j * SUB : (j + 1) * SUB]
                k_intra.append(piece)
            dq = jnp.concatenate(q_rows, axis=0) * to_mid + dot_nn(do, old_low) * reach
            dk = jnp.concatenate(k_intra, axis=0) + dot_nn(v, lam_low) * remain
            anchor = jnp.sum(lam * later[h], axis=0, keepdims=True)
            dlog = tri_dot(tri_up, q * dq - k * dk) + anchor
            adjoint[h] = lam * (jnp.exp(final) * kept) + dot_tn(do, (q * reach).astype(BF16))
            later[h] = old

            store(0, dq * (sig_q * (1.0 + pre_q * sig_nq)))
            drive = minus * (dlog / forget - dk)
            forget_grad = (1.0 - bound) * plus * drive
            store(1, forget_grad)
            sums_ref[0:1, cols] += gain_sum
            sums_ref[1:2, cols] += jnp.sum(forget_grad, axis=0, keepdims=True)
            sums_ref[2:3, cols] += jnp.sum(drive, axis=0, keepdims=True)


def mixer_backward(pre, mixed, grad, states, bias, bound, gain, split, order):
    tokens, wide = pre.shape
    width = wide // 4
    heads = width // HEAD
    steps = order.shape[0]
    block = tokens // steps
    chunks = block // CHUNK
    row = pl.BlockSpec((1, width), lambda i, order: (0, 0))
    placed = lambda i, order: (order[steps - 1 - i], 0)
    grid_spec = pltpu.PrefetchScalarGridSpec(
        num_scalar_prefetch=1,
        grid=(steps,),
        in_specs=[
            pl.BlockSpec(memory_space=pltpu.SMEM),
            pl.BlockSpec((block, wide), placed),
            pl.BlockSpec((block, width), lambda i, order: (steps - 1 - i, 0)),
            pl.BlockSpec((block, width), placed),
            pl.BlockSpec((chunks, heads, HEAD, HEAD), lambda i, order: (steps - 1 - i, 0, 0, 0)),
            row,
            row,
            row,
        ],
        out_specs=[
            pl.BlockSpec((block, wide), placed),
            pl.BlockSpec((8, width), lambda i, order: (0, 0)),
        ],
        scratch_shapes=[pltpu.VMEM((heads, HEAD, HEAD), F32), pltpu.VMEM((heads, HEAD, HEAD), F32)],
    )
    return pl.pallas_call(
        functools.partial(backward_kernel, heads, chunks),
        grid_spec=grid_spec,
        out_shape=[
            jax.ShapeDtypeStruct((tokens, wide), BF16),
            jax.ShapeDtypeStruct((8, width), F32),
        ],
        compiler_params=pltpu.CompilerParams(
            dimension_semantics=("arbitrary",), vmem_limit_bytes=VMEM
        ),
        cost_estimate=cost(tokens * width * 22000),
        name="mixer_backward",
    )(order, split, pre, mixed, grad, states, bias[None], bound[None], gain[None])


def blocks_of(array, count):
    size = array.shape[0] // count
    return [array[m * size : (m + 1) * size] for m in range(count)]


def product_kernel(dims, parts, a_ref, b_ref, *refs):
    dot = lax.dot_general(a_ref[...], b_ref[...], (dims, ((), ())), preferred_element_type=F32)
    for block, out_ref in zip(blocks_of(dot, parts), refs[len(refs) - parts :]):
        out_ref[...] = block.astype(out_ref.dtype)


NN = ((1,), (0,))
NT = ((1,), (1,))
TN = ((0,), (0,))


def product(a, b, dims, kind, rows=None, cols=None, a_half=None, b_half=None, parts=1, wait=()):
    count = a.shape[1 - dims[0][0]] if a_half is None else a.shape[0] // 2
    depth = a.shape[dims[0][0]]
    wide = b.shape[1 - dims[1][0]] // (1 if b_half is None else 2)
    tile_rows = rows or count
    tile_cols = cols or wide
    by_rows = rows is not None
    shift = (a_half or 0) * (count // tile_rows)

    def at_row(i):
        return (i if by_rows else 0) + shift

    def at_col(i):
        return 0 if by_rows else i

    b_shift = (b_half or 0) * (wide // tile_cols)

    if dims[0][0] == 1:
        a_spec = pl.BlockSpec((tile_rows, depth), lambda i: (at_row(i), 0))
    else:
        a_spec = pl.BlockSpec((depth, tile_rows), lambda i: (0, at_row(i)))
    if dims[1][0] == 0:
        b_spec = pl.BlockSpec((depth, tile_cols), lambda i: (0, at_col(i) + b_shift))
    else:
        b_spec = pl.BlockSpec((tile_cols, depth), lambda i: (at_col(i) + b_shift, 0))
    out_spec = pl.BlockSpec((tile_rows // parts, tile_cols), lambda i: (at_row(i) - shift, at_col(i)))
    out = pl.pallas_call(
        functools.partial(product_kernel, dims, parts),
        grid=(count // tile_rows * (wide // tile_cols),),
        in_specs=[a_spec, b_spec] + [UNREAD] * len(wait),
        out_specs=[out_spec] * parts,
        out_shape=[jax.ShapeDtypeStruct((count // parts, wide), kind)] * parts,
        compiler_params=pltpu.CompilerParams(
            dimension_semantics=("arbitrary",), vmem_limit_bytes=VMEM
        ),
        cost_estimate=cost(2 * count * wide * depth),
        name="product",
    )(a, b, *wait)
    return out[0] if parts == 1 else out


def gate_kernel(low_ref, weight_ref, pre_ref, hidden_ref):
    half = hidden_ref.shape[1]
    pre = dot_nn(low_ref[...], weight_ref[...])
    pre_ref[...] = pre
    gate = pre[:, :half]
    hidden_ref[...] = (gate * sigmoid_pair(gate)[0] * pre[:, half:]).astype(BF16)


def gate_product(low, weight, rows=256):
    count, depth = low.shape
    wide = weight.shape[1]
    return pl.pallas_call(
        gate_kernel,
        grid=(count // rows,),
        in_specs=[
            pl.BlockSpec((rows, depth), lambda i: (i, 0)),
            pl.BlockSpec((depth, wide), lambda i: (0, 0)),
        ],
        out_specs=[
            pl.BlockSpec((rows, wide), lambda i: (i, 0)),
            pl.BlockSpec((rows, wide // 2), lambda i: (i, 0)),
        ],
        out_shape=[
            jax.ShapeDtypeStruct((count, wide), F32),
            jax.ShapeDtypeStruct((count, wide // 2), BF16),
        ],
        compiler_params=pltpu.CompilerParams(
            dimension_semantics=("arbitrary",), vmem_limit_bytes=VMEM
        ),
        cost_estimate=cost(2 * count * depth * wide),
        name="gate_product",
    )(low, weight)


def hidden_back_kernel(grad_ref, weight_ref, pre_ref, out_ref):
    half = out_ref.shape[1] // 2
    grad = dot_nt(grad_ref[...], weight_ref[...])
    gate, up = pre_ref[:, :half], pre_ref[:, half:]
    sig, rest = sigmoid_pair(gate)
    out_ref[:, :half] = (grad * up * sig * (1.0 + gate * rest)).astype(BF16)
    out_ref[:, half:] = (grad * (gate * sig)).astype(BF16)


def hidden_back(grad, weight, pre, rows=256, wait=()):
    count, depth = grad.shape
    wide = pre.shape[1]
    return pl.pallas_call(
        lambda *refs: hidden_back_kernel(*refs[:3], refs[-1]),
        grid=(count // rows,),
        in_specs=[
            pl.BlockSpec((rows, depth), lambda i: (i, 0)),
            pl.BlockSpec(weight.shape, lambda i: (0, 0)),
            pl.BlockSpec((rows, wide), lambda i: (i, 0)),
        ]
        + [UNREAD] * len(wait),
        out_specs=pl.BlockSpec((rows, wide), lambda i: (i, 0)),
        out_shape=jax.ShapeDtypeStruct((count, wide), BF16),
        compiler_params=pltpu.CompilerParams(
            dimension_semantics=("arbitrary",), vmem_limit_bytes=VMEM
        ),
        cost_estimate=cost(count * depth * wide),
        name="hidden_back",
    )(grad, weight, pre, *wait)


def weight_sum_kernel(own_ref, other_ref, b_ref, weight_ref, right_ref, *refs):
    out_ref, sum_ref = refs[-2:]
    half = own_ref.shape[0]
    wide = b_ref.shape[1]
    dot = dot_tn(own_ref[...], b_ref[:half]) + dot_tn(other_ref[...], b_ref[half:])
    out_ref[:, :wide] = dot.astype(out_ref.dtype)
    total = jnp.sum(dot * weight_ref[...].astype(F32), axis=1, keepdims=True)
    sum_ref[...] = jnp.broadcast_to(total, sum_ref.shape)
    start = 0
    more = None
    for ref in refs[:-2]:
        size = ref.shape[0]
        if start < right_ref.shape[0]:
            term = dot_tn(ref[...], right_ref[start : start + size])
            more = term if more is None else more + term
            start += size
    out_ref[:, wide:] = more.astype(out_ref.dtype)


def weight_sum_product(own, other, b, weight, blocks, right, rows=256, wait=()):
    half, count = own.shape
    depth, wide = b.shape
    extra = right.shape[1]
    a_spec = pl.BlockSpec((half, rows), lambda i: (0, i))
    out, total = pl.pallas_call(
        weight_sum_kernel,
        grid=(count // rows,),
        in_specs=[
            a_spec,
            a_spec,
            pl.BlockSpec((depth, wide), lambda i: (0, 0)),
            pl.BlockSpec((rows, wide), lambda i: (i, 0)),
            pl.BlockSpec((depth, extra), lambda i: (0, 0)),
        ]
        + [pl.BlockSpec((block.shape[0], rows), lambda i: (0, i)) for block in blocks]
        + [UNREAD] * len(wait),
        out_specs=[
            pl.BlockSpec((rows, wide + extra), lambda i: (i, 0)),
            pl.BlockSpec((rows, HEAD), lambda i: (i, 0)),
        ],
        out_shape=[
            jax.ShapeDtypeStruct((count, wide + extra), BF16),
            jax.ShapeDtypeStruct((count, HEAD), F32),
        ],
        compiler_params=pltpu.CompilerParams(
            dimension_semantics=("arbitrary",), vmem_limit_bytes=VMEM
        ),
        cost_estimate=cost(2 * count * (wide + extra) * depth),
        name="weight_sum_product",
    )(own, other, b, weight, right, *blocks, *wait)
    return out, total[:, 0]


def early_product_kernel(b_ref, *refs):
    out_ref = refs[-1]
    size = refs[0].shape[0]
    for ref, block in zip(refs[:-1], (0, 1, 2, 4, 5, 6)):
        out_ref[block * size : (block + 1) * size] = dot_nt(ref[...], b_ref[...])


def late_product_kernel(b_ref, early_ref, *refs):
    out_ref = refs[-1]
    for step in range(2):

        @pl.when(pl.program_id(0) == step)
        def _(step=step):
            half = refs[0].shape[0]
            out_ref[:half] = dot_nt(refs[2 * step][...], b_ref[...])
            out_ref[half:] = dot_nt(refs[2 * step + 1][...], b_ref[...])


def early_product(blocks, b):
    size = blocks[0].shape[0]
    return pl.pallas_call(
        early_product_kernel,
        out_shape=jax.ShapeDtypeStruct((8 * size, b.shape[0]), F32),
        compiler_params=pltpu.CompilerParams(vmem_limit_bytes=VMEM),
        cost_estimate=cost(2 * 6 * size * b.size),
        name="early_product",
    )(b, *blocks)


def late_product(out, late, b):
    size = 2 * late[0].shape[0]
    width = b.shape[0]
    whole = [pl.BlockSpec(part.shape, lambda i: (0, 0)) for part in late]
    return pl.pallas_call(
        late_product_kernel,
        grid=(2,),
        in_specs=[pl.BlockSpec(b.shape, lambda i: (0, 0)), UNREAD] + whole,
        out_specs=pl.BlockSpec((size, width), lambda i: (4 * i + 3, 0)),
        out_shape=jax.ShapeDtypeStruct(out.shape, F32),
        input_output_aliases={1: 0},
        compiler_params=pltpu.CompilerParams(vmem_limit_bytes=VMEM),
        cost_estimate=cost(2 * 2 * size * b.size),
        name="late_product",
    )(b, out, *late)


def joined_columns_kernel(width, at_ref, own_ref, other_ref, *out_refs):
    def store(ref):
        for which in range(4):
            out_refs[which][...] = ref[:, which * width : (which + 1) * width].astype(F32)
        out_refs[4][...] = ref[:, 4 * width :].astype(F32).T

    mine = pl.program_id(0) == at_ref[0]
    pl.when(mine)(lambda: store(own_ref))
    pl.when(jnp.logical_not(mine))(lambda: store(other_ref))


def joined_columns(own, other, at, width):
    rows = own.shape[0]
    whole = pl.BlockSpec(own.shape, lambda i, at: (0, 0))
    beside = pl.BlockSpec((rows, width), lambda i, at: (0, i))
    return pl.pallas_call(
        functools.partial(joined_columns_kernel, width),
        grid_spec=pltpu.PrefetchScalarGridSpec(
            num_scalar_prefetch=1,
            grid=(2,),
            in_specs=[whole, whole],
            out_specs=[beside] * 4 + [pl.BlockSpec((width, rows), lambda i, at: (i, 0))],
        ),
        out_shape=[jax.ShapeDtypeStruct((rows, 2 * width), F32)] * 4
        + [jax.ShapeDtypeStruct((2 * width, rows), F32)],
        compiler_params=pltpu.CompilerParams(
            dimension_semantics=("arbitrary",), vmem_limit_bytes=VMEM
        ),
        cost_estimate=cost(1 << 20),
        name="joined_columns",
    )(at.astype(jnp.int32).reshape(1), own, other)


def rms_rows(rows_in):
    return lax.rsqrt(jnp.mean(rows_in * rows_in, axis=-1, keepdims=True) + EPS_NORM)


def norm_back(grad, rows_in, gain_vec):
    inv = rms_rows(rows_in)
    u = grad * gain_vec
    moment = jnp.mean(u * rows_in, axis=-1, keepdims=True)
    return inv * u - rows_in * (inv * inv * inv * moment), jnp.sum(grad * rows_in * inv, axis=0)


def gather(part, axes, dim):
    return lax.all_gather(part, axes, axis=dim, tiled=True)


def gather_columns(part, axis):
    count, at = lax.axis_size(axis), lax.axis_index(axis)
    if count > 4:
        return gather(part, axis, 1)
    size = part.shape[1]
    out = jnp.zeros((part.shape[0], count * size), part.dtype)
    for m in range(count):
        block = part if m == 0 else lax.ppermute(part, axis, [(i, i ^ m) for i in range(count)])
        out = lax.dynamic_update_slice_in_dim(out, block, (at ^ m) * size, 1)
    return out


def scatter(whole, axes, dim):
    return lax.psum_scatter(whole, axes, scatter_dimension=dim, tiled=True)


def matmul(left_side, right_side):
    return jnp.dot(left_side, right_side, preferred_element_type=F32)


def after(value, *others):
    return lax.optimization_barrier((value, *others))[0]


def small_sum(part, axis):
    count = lax.axis_size(axis)
    if count <= 4:
        got = [lax.ppermute(part, axis, [(i, i ^ m) for i in range(count)]) for m in range(1, count)]
        return sum(got, part)
    mask = 1
    while mask < count:
        part = part + lax.ppermute(part, axis, [(i, i ^ mask) for i in range(count)])
        mask *= 2
    return part


def together(*values):
    return lax.optimization_barrier(values)


def swap(part):
    return lax.ppermute(part, "ctx", [(0, 1), (1, 0)])


def in_order(own, dim):
    other = swap(own)
    first = lax.axis_index("ctx") == 0
    return jnp.concatenate([jnp.where(first, own, other), jnp.where(first, other, own)], axis=dim)


def partner(part, mask):
    return lax.ppermute(part, "tp", [(i, i ^ mask) for i in range(lax.axis_size("tp"))])


def relative(array, count, at):
    size = array.shape[0] // count
    return jnp.concatenate(
        [lax.dynamic_slice_in_dim(array, (at ^ m) * size, size, 0) for m in range(count)], axis=0
    )


def parts_of(blocks):
    half = blocks[0].shape[0] // 2
    low, high = [block[:half] for block in blocks], [block[half:] for block in blocks]
    near = jnp.concatenate([low[1], low[3]], axis=0)
    far = jnp.concatenate([high[2], high[3]], axis=0)
    return [near, far, blocks[0], low[2], high[1]]


def sum_first(parts):
    return partner(parts[0], 1), partner(parts[1], 2)


def sum_second(parts, near, far):
    half = near.shape[0] // 2
    near, far = together(near, far)
    pass_far = (parts[3].astype(F32) + near[half:].astype(F32)).astype(BF16)
    pass_near = (parts[4].astype(F32) + far[half:].astype(F32)).astype(BF16)
    pass_far, pass_near = together(pass_far, pass_near)
    return together(partner(pass_far, 2), partner(pass_near, 1))


def sum_total(parts, first, second):
    half = second[0].shape[0]
    halves = [
        parts[2][which * half : (which + 1) * half].astype(F32)
        + first[which][:half].astype(F32)
        + second[which].astype(F32)
        for which in (0, 1)
    ]
    return jnp.concatenate(halves, axis=0)


def gather_first(own):
    return partner(own, 1), partner(own, 2)


def gather_second(near, far):
    half = near.shape[0] // 2
    return partner(far[:half], 1), partner(near[half:], 2)


def gathered_parts(own, first, second):
    near, far = first
    half = second[0].shape[0]
    return [near[:half], second[0], far[half:], second[1], own, far[:half], near[half:]]


def placed_kernel(at_ref, own_ref, near_ref, far_ref, top_ref, bottom_ref, *refs):
    out_ref = refs[-1]
    step = pl.program_id(0)
    half = top_ref.shape[0]
    for which, ref in enumerate((own_ref, near_ref, far_ref)):

        @pl.when(step == which)
        def _(ref=ref):
            out_ref[...] = ref[...].astype(out_ref.dtype)

    @pl.when(step == 3)
    def _():
        out_ref[:half] = top_ref[...].astype(out_ref.dtype)
        out_ref[half:] = bottom_ref[...].astype(out_ref.dtype)


def placed_blocks(own, near, far, top, bottom, at, kind, wait=()):
    size, width = own.shape
    inputs = [own, near, far, top, bottom]
    return pl.pallas_call(
        placed_kernel,
        grid_spec=pltpu.PrefetchScalarGridSpec(
            num_scalar_prefetch=1,
            grid=(4,),
            in_specs=[pl.BlockSpec(part.shape, lambda i, at: (0, 0)) for part in inputs] + [UNREAD] * len(wait),
            out_specs=pl.BlockSpec((size, width), lambda i, at: (i ^ at[0], 0)),
        ),
        out_shape=jax.ShapeDtypeStruct((4 * size, width), kind),
        compiler_params=pltpu.CompilerParams(
            dimension_semantics=("arbitrary",), vmem_limit_bytes=VMEM
        ),
        cost_estimate=cost(3 << 30),
        name="placed_blocks",
    )(at.astype(jnp.int32).reshape(1), *inputs, *wait)


def resid_back_kernel(
    own_ref, near_ref, far_ref, top_ref, bottom_ref, resid_ref, cot_ref, gain_ref, *refs
):
    grad_ref, low_ref, sum_ref = refs[-3:]
    half = top_ref.shape[0]
    gain = gain_ref[...]
    total = jnp.zeros_like(gain)
    for which, (first_ref, second_ref) in enumerate(((near_ref, top_ref), (far_ref, bottom_ref))):
        rows = slice(which * half, (which + 1) * half)
        grad = own_ref[rows].astype(F32) + first_ref[...].astype(F32) + second_ref[...].astype(F32)
        resid = resid_ref[rows]
        inv = rms_rows(resid)
        u = grad * gain
        moment = jnp.mean(u * resid, axis=-1, keepdims=True)
        out = cot_ref[rows].astype(F32) + inv * u - resid * (inv * inv * inv * moment)
        grad_ref[rows] = out
        low_ref[rows] = out.astype(BF16)
        total = total + jnp.sum(grad * resid * inv, axis=0, keepdims=True)
    sum_ref[...] = total


def resid_back(kept, first, second, resid, cot, gain, wait=()):
    size, width = resid.shape
    whole = pl.BlockSpec((size, width), lambda i: (0, 0))
    half = pl.BlockSpec((size // 2, width), lambda i: (0, 0))
    row = pl.BlockSpec((1, width), lambda i: (0, 0))
    grad, low, total = pl.pallas_call(
        resid_back_kernel,
        grid=(1,),
        in_specs=[whole] + [half] * 4 + [whole, whole, row] + [UNREAD] * len(wait),
        out_specs=[whole, whole, row],
        out_shape=[
            jax.ShapeDtypeStruct((size, width), F32),
            jax.ShapeDtypeStruct((size, width), BF16),
            jax.ShapeDtypeStruct((1, width), F32),
        ],
        compiler_params=pltpu.CompilerParams(
            dimension_semantics=("arbitrary",), vmem_limit_bytes=VMEM
        ),
        cost_estimate=cost(2 << 30),
        name="resid_back",
    )(kept, *first, *second, resid, cot, gain[None], *wait)
    return grad, low, total[0]


def body(
    block_in,
    query_proj,
    forget_proj,
    value_proj,
    outgate_proj,
    out_proj,
    ffn_gate,
    ffn_up,
    ffn_down,
    first_gain,
    second_gain,
    group_gain,
    forget_bias,
    bound_table,
    layer_index,
    second_start,
    cotangent,
):
    ctx_count, ctx_at = lax.axis_size("ctx"), lax.axis_index("ctx")
    tp_count, tp_at = lax.axis_size("tp"), lax.axis_index("tp")
    row_count, model = block_in.shape
    local_width = query_proj.shape[1]
    width = local_width // ctx_count
    hidden_width = ffn_gate.shape[1]
    shard_rows = row_count // tp_count

    def own_half(array, dim):
        size = array.shape[dim] // ctx_count
        return lax.dynamic_slice_in_dim(array, ctx_at * size, size, dim)

    blocks = ctx_count * tp_count
    order = lax.iota(jnp.int32, blocks) ^ (ctx_at * tp_count + tp_at)

    mix_full = gather(
        jnp.concatenate(
            [own_half(w, 1) for w in (query_proj, forget_proj, value_proj, outgate_proj)], axis=1
        ),
        "dp",
        0,
    )
    out_full = gather_columns(own_half(out_proj, 0), "dp")
    ffn_full = gather(own_half(jnp.concatenate([ffn_gate, ffn_up], axis=1), 0), ("dp", "ctx"), 0)
    down_full = gather(own_half(ffn_down, 1), ("dp", "ctx"), 1)

    inputs = relative(block_in, tp_count, tp_at).astype(F32)
    first_low = (inputs * rms_rows(inputs) * first_gain).astype(BF16)
    first_swapped = swap(first_low)
    first_all = jnp.concatenate([first_low, first_swapped], axis=0)
    table = own_half(bound_table, 1)
    weights = jax.nn.softmax(table, axis=0)
    rows = lax.broadcasted_iota(jnp.int32, (table.shape[0], 1), 0)
    counted = jnp.where((rows >= 1) & (rows <= layer_index[0]), 1.0, 0.0)
    bound = jnp.sum(weights * counted, axis=0)
    bias = own_half(forget_bias, 0)
    gain = own_half(group_gain, 0)
    pre = product(first_all, mix_full, NN, F32, rows=512)
    gated, mixed, states = mixer_forward(pre, bias, bound, gain, second_start, order)
    inputs_own = inputs[:shard_rows]
    out_other = [
        swap(block) for block in product(gated, out_full, NN, BF16, cols=512, a_half=1, parts=tp_count)
    ]
    out_own = product(gated, out_full, NN, BF16, cols=512, a_half=0, parts=tp_count)
    out_part = parts_of([(a.astype(F32) + b.astype(F32)).astype(BF16) for a, b in zip(out_own, out_other)])
    first = sum_first(out_part)
    second = sum_second(out_part, *first)
    resid = inputs_own + sum_total(out_part, first, second)

    second_own = (resid * rms_rows(resid) * second_gain).astype(BF16)
    first = gather_first(second_own)
    second_low = jnp.concatenate(
        gathered_parts(second_own, first, gather_second(*first)), axis=0
    )
    cotangent_blocks = blocks_of(relative(cotangent, tp_count, tp_at), tp_count)
    cotangent_rel = jnp.concatenate(parts_of(cotangent_blocks), axis=0)
    gate_up, hidden = gate_product(second_low, ffn_full)

    down_grad = product(hidden, cotangent_rel, TN, BF16, cols=512)
    down_sum = scatter(down_grad, ("dp", "ctx"), 1)
    gate_up_grad = hidden_back(cotangent_rel, down_full, gate_up, wait=[down_grad])
    second_sent = product(gate_up_grad, ffn_full, NT, BF16, cols=512, a_half=0, parts=2)
    first = sum_first(second_sent)
    second_kept = product(gate_up_grad, ffn_full, NT, BF16, cols=512, a_half=1, wait=second_sent)
    half_rows = shard_rows // 2
    second_part = [
        *second_sent,
        second_kept[:shard_rows],
        second_kept[shard_rows : shard_rows + half_rows],
        second_kept[shard_rows + half_rows :],
    ]
    ffn_rows = product(hidden, down_full, NN, BF16, cols=256, parts=tp_count, wait=[second_kept])
    gate_weight_grad = product(second_low, gate_up_grad, TN, BF16, rows=256, b_half=0)
    gate_sum = scatter(after(gate_weight_grad, second_kept, *first), ("dp", "ctx"), 0)
    second = sum_second(second_part, *first)
    resid_grad, resid_own, second_gain_grad = resid_back(
        second_kept, first, second, resid, cotangent_blocks[0], second_gain, wait=[down_sum, ffn_rows[0]]
    )
    first = gather_first(resid_own)
    up_weight_grad = product(second_low, gate_up_grad, TN, BF16, rows=256, b_half=1)
    up_sum = scatter(after(up_weight_grad, *first), ("dp", "ctx"), 0)
    resid_second = gather_second(*first)
    resid_early = [resid_own, *first]
    resid_early = resid_early + [swap(block) for block in resid_early]
    early_grad = early_product(resid_early, out_full)
    resid_late = [*resid_second, *[swap(after(block, early_grad)) for block in resid_second]]
    resid_blocks = [*resid_early[:3], *resid_late[:2], *resid_early[3:], *resid_late[2:]]

    ffn_rows = [after(part, *resid_second) for part in ffn_rows]
    ffn_part = [*ffn_rows[:3], ffn_rows[3][:half_rows], ffn_rows[3][half_rows:]]
    ffn_first = sum_first(ffn_part)
    gated_grad = late_product(early_grad, resid_late, out_full)
    proj_grad, sums = mixer_backward(pre, mixed, gated_grad, states, bias, bound, gain, second_start, order)
    first_other = product(proj_grad, mix_full, NT, BF16, cols=256, a_half=1, parts=tp_count, wait=ffn_first)
    ffn_second = sum_second([after(block, proj_grad) for block in ffn_part], *ffn_first)
    block_own = (resid + sum_total(ffn_part, ffn_first, ffn_second)).astype(BF16)
    first_own = product(
        proj_grad, mix_full, NT, BF16, cols=256, a_half=0, parts=tp_count, wait=[first_other[0], block_own]
    )
    block_first = gather_first(block_own)
    first_part = [
        (own.astype(F32) + swap(other).astype(F32)).astype(BF16)
        for own, other in zip(first_own, first_other)
    ]
    first_part = parts_of(first_part)
    first = sum_first(first_part)
    mix_grad, first_sum = weight_sum_product(
        first_low, first_swapped, proj_grad, mix_full, resid_blocks, gated, wait=block_first
    )
    mix_sum = scatter(after(mix_grad, gate_sum, up_sum, *first), "dp", 0)
    final_first = first
    second = sum_second(first_part, *first)
    input_part, _ = norm_back(sum_total(first_part, first, second), inputs_own, first_gain)
    input_own = (resid_grad + input_part).astype(BF16)
    block_second = gather_second(*[after(block, *second) for block in block_first])
    input_own = after(input_own, *block_second)
    first = gather_first(input_own)

    block_out = placed_blocks(block_own, *block_first, *block_second, tp_at, BF16)
    input_second = gather_second(*[after(block, block_out) for block in first])
    input_grad = placed_blocks(input_own, *first, *input_second, tp_at, F32)

    gains = jnp.concatenate([first_sum / first_gain, second_gain_grad]).reshape(-1, HEAD)
    gains = after(gains, *input_second)
    gains = small_sum(gains + swap(gains), "tp")
    small = small_sum(jnp.concatenate([sums[:3].reshape(-1, HEAD), gains]), "dp")
    cut = 3 * width // HEAD
    head_sums = in_order(small[:cut].reshape(3, width), 1)
    gain_sums = small[cut:].reshape(-1)
    all_weights = jax.nn.softmax(bound_table, axis=0)
    all_bound = jnp.sum(all_weights * counted, axis=0)
    table_grad = all_weights * (counted - all_bound) * head_sums[2]

    *mix_shards, out_shard = joined_columns(mix_sum, swap(mix_sum), ctx_at, width)

    return (
        block_out,
        input_grad,
        *mix_shards,
        out_shard,
        in_order(after(gate_sum, *final_first), 0).astype(F32),
        in_order(after(up_sum, *final_first), 0).astype(F32),
        in_order(after(down_sum, *final_first), 1).astype(F32),
        gain_sums[:model],
        gain_sums[model:],
        head_sums[0],
        head_sums[1],
        table_grad,
    )


def solution(mesh):
    return jax.shard_map(
        body,
        mesh=mesh,
        in_specs=(
            P(("dp", "ctx"), None),
            P("dp", "tp"),
            P("dp", "tp"),
            P("dp", "tp"),
            P("dp", "tp"),
            P("tp", "dp"),
            P("dp", "tp"),
            P("dp", "tp"),
            P("tp", "dp"),
            P(),
            P(),
            P("tp"),
            P("tp"),
            P(None, "tp"),
            P(),
            P("dp"),
            P(("dp", "ctx"), None),
        ),
        out_specs=(
            P(("dp", "ctx"), None),
            P(("dp", "ctx"), None),
            P("dp", "tp"),
            P("dp", "tp"),
            P("dp", "tp"),
            P("dp", "tp"),
            P("tp", "dp"),
            P("dp", "tp"),
            P("dp", "tp"),
            P("tp", "dp"),
            P(),
            P(),
            P("tp"),
            P("tp"),
            P(None, "tp"),
        ),
        check_vma=False,
    )
```
